256 devices in a mesh: leaf: 2 (over core), row: 4 (over x), col: 32 (over z, y).
Axes of the slice: x: 4, y: 4, z: 8, core: 2. Of those that a mesh axis runs over, the one named last changes fastest.
Arguments:
- child_rhs: float32 [512, 256, 256], P(('leaf', 'row', 'col')), may hold values from -6 to 6
- child_diag: float32 [512, 256, 256], P(('leaf', 'row', 'col')), may hold values from -0.375 to 0.375
- child_off: float32 [512, 256, 256], P(('leaf', 'row', 'col')), may hold values from -0.046875 to 0.046875
- live: int32 [512], P(('leaf', 'row', 'col')), may hold values from 1 to 256, 81920 in all
- targets: int32 [512, 256], P(('leaf', 'row', 'col')), may hold values from 0 to 2047
- top_rhs: float32 [2048, 256], P('row'), may hold values from -6 to 6
- top_factor: float32 [2048, 2048], P('row', 'col'), may hold values from -0.125 to 0.125
- top_diag: float32 [2048, 512], P('row'), may hold values from -0.25 to 0.25
Outputs:
- child_sol: float32 [512, 256, 256], P(('leaf', 'row', 'col'))
- top_sol: float32 [2048, 256], P('row')
The draws below stay inside these ranges and needn't reach their ends.
All inputs are finite; a program needn't handle non-finite values. No bound on the sum of `live` on one device may be relied on, other than what follows from the above.
Results may differ from the reference program's by a relative error of at most 0.0003.
Values sent between devices are 32-bit elements; how exact they have to be, the bound alone decides.
A program may use at most 64 MiB of HBM per device.

```python
import math
import jax
import jax.numpy as jnp
import numpy as np
from jax import lax

W = 256
NRHS = 256
TILE = 256
TB = 512
CH_DEV = 2
NTOP = 2048
CHILD = 512
FAN = 16384


def set_ends(values, own_key, smallest, top_value):
    longest = values.shape.index(max(values.shape))
    spots = []
    for shift in (0, 1):
        where = [jax.random.randint(jax.random.fold_in(own_key, axis), (), 0, length) for axis, length in enumerate(values.shape)]
        where[longest] = (where[longest] + shift) % values.shape[longest]
        spots.append(tuple(where))
    return values.at[spots[0]].set(smallest).at[spots[1]].set(top_value)


def levels(key, dims, split, smallest, top_value):
    level = 1.0
    for axis_at, shards_of in split:
        steps = jax.random.uniform(jax.random.fold_in(jax.random.fold_in(key, 6), axis_at), (shards_of,), jnp.float32, smallest / len(split), top_value / len(split))
        level = level * jnp.repeat(jnp.exp(steps), dims[axis_at] // shards_of).reshape((-1,) + (1,) * (len(dims) - 1 - axis_at))
    return level


def rank_table(number_of, skew):
    portions = [(1 << 20) // math.isqrt(standing ** skew) + 1 for standing in range(1, number_of + 1)]
    width = 1 + sum(portions) // (1 << 30)
    return np.cumsum(np.array([max(1, weight // width) for weight in portions]))


def ranked_ids(stream_key, shape, amount, skew):
    table = rank_table(amount, skew)
    ticket = jax.random.randint(jax.random.fold_in(stream_key, 1), shape, 0, int(table[amount - 1]))
    standing = jnp.searchsorted(jnp.asarray(table, jnp.int32), ticket, side="right")
    return jax.random.permutation(jax.random.fold_in(stream_key, 2), amount)[standing].astype(jnp.int32)


def profile(number_of, total, reach, skew):
    loads = [(1 << 20) // math.isqrt(grade ** skew) + 1 for grade in range(2, number_of + 1)]
    surplus, holding = total - reach - (number_of - 1), [1] * (number_of - 1)
    while surplus > 0:
        movable = [i for i in range(number_of - 1) if holding[i] < reach]
        mass, budget = sum([loads[i] for i in movable]), surplus
        for i in movable:
            more = min(reach - holding[i], max(1, budget * loads[i] // mass), surplus)
            holding[i] = holding[i] + more
            surplus = surplus - more
    return np.array([reach] + holding)


def uneven(stream_key, count, total, limit, skew):
    if count == 2:
        one = jax.random.randint(stream_key, (), max(1, total - limit), min(limit, total - 1) + 1)
        return jnp.stack([one, total - one])
    tallies = jnp.asarray(profile(count, total, limit, skew), jnp.int32)
    pairs = (count - 1) // 2
    donor, sink = tallies[1:1 + 2 * pairs:2], tallies[2:2 + 2 * pairs:2]
    margin = jnp.minimum(donor - 1, limit - sink)
    passed = jax.random.randint(jax.random.fold_in(stream_key, 1), (pairs,), 0, 1 << 20) % (margin + 1)
    tallies = tallies.at[1:1 + 2 * pairs:2].set(donor - passed).at[2:2 + 2 * pairs:2].set(sink + passed)
    return tallies[jax.random.permutation(jax.random.fold_in(stream_key, 2), count)]


def gaussian(stream_key, extent, spread, most, split=(), held_as=jnp.bfloat16):
    result = jax.random.normal(stream_key, extent, jnp.float32) * spread
    if len(split) > 0:
        result = levels(stream_key, extent, split, -0.22, 0.18) * result
    return jnp.clip(result, min=-most, max=most).astype(held_as)


def setup_inputs(seed: int = 0) -> dict:
    arg_keys = jax.random.split(jax.random.key(seed), 9)
    child_rhs = gaussian(arg_keys[0], (CHILD, W, NRHS), 1.0, 6.0, ((0, 256),), jnp.float32)
    child_diag = gaussian(arg_keys[1], (CHILD, W, W), W ** -0.5, 0.375, ((0, 256),), jnp.float32)
    child_off = gaussian(arg_keys[2], (CHILD, TILE, W), FAN ** -0.5, 0.046875, ((0, 256),), jnp.float32)
    live = uneven(arg_keys[3], CHILD, CHILD * TILE * 5 // 8, TILE, 0).astype(jnp.int32)
    targets = set_ends(ranked_ids(arg_keys[4], (CHILD, TILE), NTOP, 2), jax.random.fold_in(arg_keys[4], 3), 0, NTOP - 1).astype(jnp.int32)
    top_rhs = gaussian(arg_keys[5], (NTOP, NRHS), 1.0, 6.0, ((0, 4),), jnp.float32)
    top_factor = gaussian(arg_keys[6], (NTOP, NTOP), NTOP ** -0.5, 0.125, ((0, 4), (1, 32)), jnp.float32)
    top_diag = gaussian(arg_keys[7], (NTOP, TB), TB ** -0.5, 0.25, ((0, 4),), jnp.float32)
    return {"child_rhs": child_rhs, "child_diag": child_diag, "child_off": child_off, "live": live, "targets": targets, "top_rhs": top_rhs, "top_factor": top_factor, "top_diag": top_diag}


def unit_lower(matrix):
    return jnp.tril(matrix) + jnp.eye(matrix.shape[-1], dtype=matrix.dtype)


def reference(child_rhs, child_diag, child_off, live, targets, top_rhs, top_factor, top_diag):
    blocks = CHILD // CH_DEV
    highest = lax.Precision.HIGHEST
    slot_index = jnp.arange(TILE, dtype=jnp.int32)

    def child_step(contrib, pieces):
        rhs_part, diag_part, off_part, live_part, target_part = pieces
        solved = jnp.einsum("bij,bjr->bir", unit_lower(diag_part), rhs_part, precision=highest)
        tiles = jnp.einsum("btj,bjr->btr", off_part, solved, precision=highest)
        keep = slot_index[None, :] < live_part[:, None]
        tiles = jnp.where(keep[:, :, None], tiles, jnp.zeros_like(tiles))
        contrib = contrib.at[target_part.reshape(-1)].add(tiles.reshape(-1, NRHS))
        return contrib, solved

    pieces = (child_rhs.reshape(blocks, CH_DEV, W, NRHS), child_diag.reshape(blocks, CH_DEV, W, W),
              child_off.reshape(blocks, CH_DEV, TILE, W), live.reshape(blocks, CH_DEV),
              targets.reshape(blocks, CH_DEV, TILE))
    updates, solved_all = lax.scan(child_step, jnp.zeros((NTOP, NRHS), jnp.float32), pieces)
    child_sol = solved_all.reshape(CHILD, W, NRHS)
    reduced = top_rhs - updates
    block_of = jnp.arange(NTOP, dtype=jnp.int32) // TB

    def top_step(block, solution):
        start = (block * TB).astype(jnp.int32)
        factor_rows = lax.dynamic_slice_in_dim(top_factor, start, TB, 0)
        factor_rows = jnp.where((block_of < block)[None, :], factor_rows, jnp.zeros_like(factor_rows))
        before = jnp.dot(factor_rows, solution, precision=highest, preferred_element_type=jnp.float32)
        inverse = unit_lower(lax.dynamic_slice_in_dim(top_diag, start, TB, 0))
        rhs_block = lax.dynamic_slice_in_dim(reduced, start, TB, 0)
        solved = jnp.dot(inverse, rhs_block - before, precision=highest, preferred_element_type=jnp.float32)
        return lax.dynamic_update_slice_in_dim(solution, solved, start, 0)

    top_sol = lax.fori_loop(0, NTOP // TB, top_step, jnp.zeros((NTOP, NRHS), jnp.float32))
    return child_sol, top_sol
```

```python
import jax
import jax.numpy as jnp
from jax import lax
from jax.experimental import pallas as pl
from jax.experimental.pallas import tpu as pltpu
from jax.sharding import PartitionSpec as P

MESH = pl.DeviceIdType.MESH
F32 = jnp.float32
BF16 = jnp.bfloat16
NX, NY, NZ = 4, 4, 8


def split(value):
    high = value.astype(BF16)
    return high, (value - high.astype(F32)).astype(BF16)


def dot(a, b):
    return jnp.dot(a, b, preferred_element_type=F32)


def dot3(a, b):
    ah, al = split(a)
    bh, bl = split(b)
    return dot(ah, bh) + (dot(ah, bl) + dot(al, bh))


def tril(value, row0, col0):
    rows = lax.broadcasted_iota(jnp.int32, value.shape, 0) + row0
    cols = lax.broadcasted_iota(jnp.int32, value.shape, 1) + col0
    return jnp.where(rows >= cols, value, 0.0), rows == cols


def kernel(
    live_ref, targ_ref, rhs_hbm, diag_hbm, off_hbm, trhs_hbm, fac_hbm, td_hbm,
    csol_hbm, top_hbm,
    rhs_v, diag_v, off_v, csol_v, tile_v, trhs_v, fac_v, td_v,
    tg, trecv, tcol, tt, cbuf, s1recv, s2src, s2recv, s3src, s3recv,
    rhst, tinv, gsrc, grecv, fsrc, xrecv, f1recv, pbuf, outv,
    load_sem, out_sem, tgs, tgr, cs, cr, gs, gr, s1s, s1r, s2s, s2r, s3s, s3r, xs, xr, f1s, f1r, f2s, f2r,
):
    leaf, x, col = lax.axis_index("leaf"), lax.axis_index("row"), lax.axis_index("col")
    y, z = col % NY, col // NY
    sibling = 1 - leaf

    def local(src, dst, sem):
        return pltpu.make_async_copy(src, dst, sem)

    def remote(src, dst, send, recv, l2, x2, y2, z2):
        return pltpu.make_async_remote_copy(
            src_ref=src, dst_ref=dst, send_sem=send, recv_sem=recv,
            device_id=(l2, x2, z2 * NY + y2), device_id_type=MESH,
        )

    def arrived(ref, sem):
        pltpu.make_async_copy(ref, ref, sem).wait()

    loads = [
        local(diag_hbm, diag_v, load_sem.at[0]),
        local(rhs_hbm, rhs_v, load_sem.at[1]),
        local(off_hbm, off_v, load_sem.at[2]),
        local(td_hbm, td_v, load_sem.at[3]),
        local(fac_hbm, fac_v, load_sem.at[4]),
        local(trhs_hbm, trhs_v, load_sem.at[5]),
    ]
    for copy in loads:
        copy.start()

    barrier = pltpu.get_barrier_semaphore()
    mine = leaf * (NX * NY) + x * NY + y

    def greet_z(i, _):
        other = (mine + i) % (2 * NX * NY)
        l2, x2, y2 = other // (NX * NY), (other // NY) % NX, other % NY
        pl.semaphore_signal(barrier, inc=1, device_id=(l2, x2, z * NY + y2), device_id_type=MESH)
        return 0

    lax.fori_loop(1, 2 * NX * NY, greet_z, 0)

    def greet_x(i, _):
        z2 = (z + 1 + i // (2 * NY)) % NZ
        l2, y2 = (i // NY) % 2, i % NY
        pl.semaphore_signal(barrier, inc=1, device_id=(l2, x, z2 * NY + y2), device_id_type=MESH)
        return 0

    lax.fori_loop(0, (NZ - 1) * 2 * NY, greet_x, 0)

    lane = lax.broadcasted_iota(jnp.int32, (1, 256), 1)
    for s in range(2):
        row = jnp.where(lane < live_ref[s], targ_ref[s : s + 1, :], -1).astype(F32)
        tg[0, s, :, :] = jnp.broadcast_to(row, (8, 256))

    pl.semaphore_wait(barrier, 2 * NX * NY - 1 + (NZ - 1) * 2 * NY)

    tg_copy = remote(tg.at[0], tg.at[1], tgs, tgr, sibling, x, y, z)
    tg_copy.start()

    loads[0].wait()
    loads[1].wait()
    loads[2].wait()
    core_copies = []
    for s in range(2):
        low, _ = tril(diag_v[s], 0, 0)
        sol = rhs_v[s] + dot3(low, rhs_v[s])
        csol_v[s] = sol
        tile_v[s] = dot3(off_v[s], sol)
        copy = remote(
            tile_v.at[s, :, pl.ds(pl.multiple_of(sibling * 128, 128), 128)], trecv.at[s],
            cs.at[s], cr.at[s], sibling, x, y, z,
        )
        copy.start()
        core_copies.append(copy)
    csol_copy = local(csol_v, csol_hbm, out_sem.at[0])
    csol_copy.start()

    loads[3].wait()
    loads[4].wait()
    low, _ = tril(td_v[...], 0, 0)
    fac = fac_v[...]
    gt = (fac + dot3(low, fac)).T
    for y2 in range(NY):
        gsrc[y2] = gt[:, 128 * y2 : 128 * y2 + 128]

    def g_copy(i):
        y2 = (y + i % NY) % NY
        z2 = 2 * (i // NY) + leaf
        own = (y2 == y) & (z2 == z) & (z % 2 == leaf)
        return own, remote(
            gsrc.at[y2], grecv.at[z // 2, y], gs.at[i], gr.at[z // 2], z % 2, x, y2, z2
        ), local(gsrc.at[y2], grecv.at[z // 2, y], gr.at[z // 2])

    def g_start(i, _):
        own, there, here = g_copy(i)

        @pl.when(own)
        def _():
            here.start()

        @pl.when(jnp.logical_not(own))
        def _():
            there.start()

        return 0

    @pl.when(z // 2 < x)
    def _():
        lax.fori_loop(0, 16, g_start, 0)

    row0, col0 = pl.multiple_of(y * 128, 128), pl.multiple_of(leaf * 256, 256)
    low, eye = tril(td_v[pl.ds(row0, 128), pl.ds(col0, 256)], row0, col0)
    tinv[...] = (low + jnp.where(eye, 1.0, 0.0)).T
    loads[5].wait()
    rhst[...] = trhs_v[pl.ds(col0, 256), :].T

    half = pl.ds(pl.multiple_of(leaf * 128, 128), 128)
    for s in range(2):
        tcol[256 * s : 256 * s + 256, :] = jnp.broadcast_to(tg[0, s, 0:1, :], (128, 256)).T
        high, rest = split(tile_v[s, :, half].T)
        tt[0:128, 256 * s : 256 * s + 256] = high
        tt[128:256, 256 * s : 256 * s + 256] = rest
    tg_copy.wait_recv()
    for s in range(2):
        tcol[512 + 256 * s : 768 + 256 * s, :] = jnp.broadcast_to(tg[1, s, 0:1, :], (128, 256)).T
        core_copies[s].wait_recv()
        high, rest = split(trecv[s].T)
        tt[0:128, 512 + 256 * s : 768 + 256 * s] = high
        tt[128:256, 512 + 256 * s : 768 + 256 * s] = rest

    lane = lax.broadcasted_iota(jnp.int32, (1024, 128), 1)

    def contrib(q, d):
        block = (x + d) % NX
        rel = tcol[...] - (block * 512 + q * 256).astype(F32)
        lanes = lane.astype(F32)
        hot = jnp.concatenate(
            [jnp.where(rel == lanes, 1.0, 0.0), jnp.where(rel == lanes + 128.0, 1.0, 0.0)], axis=1
        ).astype(BF16)
        both = dot(tt[...], hot)
        cbuf[q, d] = both[0:128] + both[128:256]

    def s1_copy(q, d):
        return remote(
            cbuf.at[q, d], s1recv.at[q, d - 1], s1s.at[q, d], s1r.at[q], leaf, (x + d) % NX, y, z
        )

    for q in range(2):

        def s1_step(d, _, q=q):
            contrib(q, d)
            s1_copy(q, d).start()
            return 0

        lax.fori_loop(1, NX, s1_step, 0)
        contrib(q, 0)

    def s2_copy(q, e):
        z2 = (z + e) % NZ
        return remote(
            s2src.at[q, z2], s2recv.at[q, e - 1], s2s.at[q, e], s2r.at[q], leaf, x, y, z2
        )

    for q in range(2):
        arrived(s1recv.at[q], s1r.at[q])
        s2src[q] = (cbuf[q, 0] + s1recv[q, 0] + s1recv[q, 1] + s1recv[q, 2]).reshape(NZ, 16, 256)

        def s2_step(e, _, q=q):
            s2_copy(q, e).start()
            return 0

        lax.fori_loop(1, NZ, s2_step, 0)

    def s3_copy(q, dy):
        y2 = (y + dy) % NY
        return remote(s3src.at[q], s3recv.at[leaf, dy], s3s.at[q, dy], s3r, q, x, y2, z)

    for q in range(2):
        arrived(s2recv.at[q], s2r.at[q])
        total = s2src[q, z]
        for e in range(NZ - 1):
            total = total + s2recv[q, e]
        s3src[q] = total
        for dy in range(1, NY):
            s3_copy(q, dy).start()

        @pl.when(leaf == q)
        def _(q=q):
            local(s3src.at[q], s3recv.at[leaf, 0], s3r).start()

        @pl.when(leaf != q)
        def _(q=q):
            s3_copy(q, 0).start()

    arrived(s3recv, s3r)
    reds = []
    for h in range(2):
        upd = s3recv[h, 0] + s3recv[h, 1] + s3recv[h, 2] + s3recv[h, 3]
        reds.append(rhst[pl.ds(pl.multiple_of(h * 128 + z * 16, 16), 16), :] - upd)
    acc = dot3(jnp.concatenate(reds, axis=0), tinv[...])
    fsrc[...] = acc.reshape(2, 16, 128)

    def x_copy(k, x2, y2):
        return remote(
            fsrc, xrecv.at[k, leaf, y % 2], xs.at[x2, y2], xr.at[k], y // 2, x2, y2, z
        )

    for k in range(NX - 1):

        @pl.when(x == k)
        def _(k=k):
            for x2 in range(k + 1, NX):
                for y2 in range(NY):
                    x_copy(k, x2, y2).start()

        @pl.when(x > k)
        def _(k=k):
            arrived(grecv.at[k], gr.at[k])
            arrived(xrecv.at[k], xr.at[k])
            parts = (xrecv[k, 0] + xrecv[k, 1]).reshape(2, 32, 128)
            solved = jnp.concatenate([parts[0], parts[1]], axis=1)
            step = dot3(solved, grecv[k].reshape(256, 128))
            fsrc[...] = fsrc[...] - step.reshape(2, 16, 128)

    def f1_copy(h, e):
        z2 = (z + e) % NZ
        return remote(fsrc.at[h], f1recv.at[leaf, z], f1s.at[h, e], f1r, h, x, y, z2)

    for h in range(2):

        def f1_step(e, _, h=h):
            f1_copy(h, e).start()
            return 0

        lax.fori_loop(1, NZ, f1_step, 0)

        @pl.when(leaf == h)
        def _(h=h):
            local(fsrc.at[h], f1recv.at[leaf, z], f1r).start()

        @pl.when(leaf != h)
        def _(h=h):
            f1_copy(h, 0).start()

    arrived(f1recv, f1r)
    piece = (f1recv[0] + f1recv[1]).reshape(128, 128).T
    pbuf[...] = piece
    place = (pl.ds(row0, 128), half)

    def f2_copy(i):
        l2, y2 = (leaf + i // NY) % 2, (y + i % NY) % NY
        return remote(pbuf, outv.at[place[0], place[1]], f2s.at[i], f2r, l2, x, y2, z)

    def f2_step(i, _):
        f2_copy(i).start()
        return 0

    local(pbuf, outv.at[place[0], place[1]], f2r).start()
    lax.fori_loop(1, 2 * NY, f2_step, 0)
    arrived(outv, f2r)
    top_copy = local(outv, top_hbm, out_sem.at[1])
    top_copy.start()

    tg_copy.wait_send()
    for s in range(2):
        core_copies[s].wait_send()

    def g_wait(i, _):
        own, there, here = g_copy(i)

        @pl.when(jnp.logical_not(own))
        def _():
            there.wait_send()

        return 0

    @pl.when(z // 2 < x)
    def _():
        lax.fori_loop(0, 16, g_wait, 0)

    for q in range(2):
        for d in range(1, NX):
            s1_copy(q, d).wait_send()
        for e in range(1, NZ):
            s2_copy(q, e).wait_send()
        for dy in range(1, NY):
            s3_copy(q, dy).wait_send()

        @pl.when(leaf != q)
        def _(q=q):
            s3_copy(q, 0).wait_send()
            f1_copy(q, 0).wait_send()

        for e in range(1, NZ):
            f1_copy(q, e).wait_send()
    for k in range(NX - 1):

        @pl.when(x == k)
        def _(k=k):
            for x2 in range(k + 1, NX):
                for y2 in range(NY):
                    x_copy(k, x2, y2).wait_send()

    for i in range(1, 2 * NY):
        f2_copy(i).wait_send()
    csol_copy.wait()
    top_copy.wait()


def shards(child_rhs, child_diag, child_off, live, targets, top_rhs, top_factor, top_diag):
    any_ = pl.BlockSpec(memory_space=pl.ANY)
    vm = pltpu.VMEM
    dma = pltpu.SemaphoreType.DMA
    return pl.pallas_call(
        kernel,
        out_shape=(
            jax.ShapeDtypeStruct(child_rhs.shape, F32),
            jax.ShapeDtypeStruct(top_rhs.shape, F32),
        ),
        in_specs=[
            pl.BlockSpec(memory_space=pltpu.SMEM),
            pl.BlockSpec(memory_space=pltpu.VMEM),
        ] + [any_] * 6,
        out_specs=(any_, any_),
        scratch_shapes=[
            vm((2, 256, 256), F32), vm((2, 256, 256), F32), vm((2, 256, 256), F32),
            vm((2, 256, 256), F32), vm((2, 256, 256), F32),
            vm((512, 256), F32), vm((512, 64), F32), vm((512, 512), F32),
            vm((2, 2, 8, 256), F32), vm((2, 256, 128), F32), vm((1024, 128), F32), vm((256, 1024), BF16),
            vm((2, 4, 128, 256), F32), vm((2, 3, 128, 256), F32),
            vm((2, 8, 16, 256), F32), vm((2, 7, 16, 256), F32),
            vm((2, 16, 256), F32), vm((2, 4, 16, 256), F32),
            vm((256, 256), F32), vm((256, 128), F32),
            vm((4, 64, 128), F32), vm((3, 4, 64, 128), F32),
            vm((2, 16, 128), F32), vm((3, 2, 2, 2, 16, 128), F32),
            vm((2, 8, 16, 128), F32), vm((128, 128), F32), vm((512, 256), F32),
            dma((6,)), dma((2,)), dma, dma, dma((2,)), dma((2,)), dma((16,)), dma((4,)),
            dma((2, 4)), dma((2,)), dma((2, 8)), dma((2,)), dma((2, 4)), dma,
            dma((4, 4)), dma((3,)), dma((2, 8)), dma, dma((8,)), dma,
        ],
        compiler_params=pltpu.CompilerParams(collective_id=0, has_side_effects=True),
    )(live, targets, child_rhs, child_diag, child_off, top_rhs, top_factor, top_diag)


def solution(mesh):
    parts = ("leaf", "row", "col")
    in_specs = (
        P(parts, None, None),
        P(parts, None, None),
        P(parts, None, None),
        P(parts),
        P(parts, None),
        P("row", None),
        P("row", "col"),
        P("row", None),
    )
    out_specs = (P(parts, None, None), P("row", None))
    return jax.shard_map(shards, mesh=mesh, in_specs=in_specs, out_specs=out_specs, check_vma=False)
```

```python
import jax
import jax.numpy as jnp
from jax import lax
from jax.experimental import pallas as pl
from jax.experimental.pallas import tpu as pltpu
from jax.sharding import PartitionSpec as P

MESH = pl.DeviceIdType.MESH
F32 = jnp.float32
BF16 = jnp.bfloat16
NX, NY, NZ = 4, 4, 8


def split(value):
    high = value.astype(BF16)
    return high, (value - high.astype(F32)).astype(BF16)


def dot(a, b):
    return jnp.dot(a, b, preferred_element_type=F32)


def dot3(a, b):
    ah, al = split(a)
    bh, bl = split(b)
    return dot(ah, bh) + (dot(ah, bl) + dot(al, bh))


def dott(a, b):
    return lax.dot_general(a, b, (((1,), (1,)), ((), ())), preferred_element_type=F32)


def dot3t(a, b):
    ah, al = split(a)
    bh, bl = split(b)
    return dott(ah, bh) + (dott(ah, bl) + dott(al, bh))


def tril(value, row0, col0):
    rows = lax.broadcasted_iota(jnp.int32, value.shape, 0) + row0
    cols = lax.broadcasted_iota(jnp.int32, value.shape, 1) + col0
    return jnp.where(rows >= cols, value, 0.0), rows == cols


def kernel(
    live_ref, targ_ref, rhs_hbm, diag_hbm, off_hbm, trhs_hbm, fac_hbm, td_hbm,
    csol_v, outv,
    rhs_v, diag_v, off_v, tile_v, trhs_v, fac_v, td_v,
    tg, trecv, tcol, tt, cbuf, s1recv, s2src, s2recv, s3src, s3recv,
    rhst, tinv, gsrc, grecv, fsrc, xrecv, f1recv,
    load_sem, tgs, tgr, cs, cr, gas, gar, gs, gr, s1s, s1r, s2s, s2r, s3s, s3r, xs, xr, f1s, f1r, f2s, f2r, f3s, f3r,
):
    leaf, x, col = lax.axis_index("leaf"), lax.axis_index("row"), lax.axis_index("col")
    y, z = col % NY, col // NY
    sibling = 1 - leaf

    def local(src, dst, sem):
        return pltpu.make_async_copy(src, dst, sem)

    def remote(src, dst, send, recv, l2, x2, y2, z2):
        return pltpu.make_async_remote_copy(
            src_ref=src, dst_ref=dst, send_sem=send, recv_sem=recv,
            device_id=(l2, x2, z2 * NY + y2), device_id_type=MESH,
        )

    def arrived(ref, sem):
        pltpu.make_async_copy(ref, ref, sem).wait()

    drain = []

    def finish():
        for wait in drain:
            wait()

    loads = [
        local(ref.at[s], buf.at[s], load_sem.at[i, s])
        for s in range(2)
        for i, (ref, buf) in enumerate(((diag_hbm, diag_v), (rhs_hbm, rhs_v), (off_hbm, off_v)))
    ] + [
        local(td_hbm, td_v, load_sem.at[3, 0]),
        local(fac_hbm, fac_v, load_sem.at[4, 0]),
        local(trhs_hbm, trhs_v, load_sem.at[5, 0]),
    ]
    for copy in loads:
        copy.start()

    barrier = pltpu.get_barrier_semaphore()

    def greet(l2, x2, y2, z2):
        pl.semaphore_signal(barrier, inc=1, device_id=(l2, x2, z2 * NY + y2), device_id_type=MESH)

    greet(sibling, x, y, z)
    for d in range(1, NX):
        greet(leaf, (x + d) % NX, y, z)
    for d in range(1, NY):
        greet(leaf, x, (y + d) % NY, z)
    for d in range(1, NZ):
        greet(leaf, x, y, (z + d) % NZ)

    lane = lax.broadcasted_iota(jnp.int32, (1, 256), 1)
    for s in range(2):
        row = jnp.where(lane < live_ref[s], targ_ref[s : s + 1, :], -1).astype(F32)
        tg[0, s, :, :] = jnp.broadcast_to(row, (8, 256))

    for s in range(2):
        loads[3 * s].wait()
        loads[3 * s + 1].wait()
        low, _ = tril(diag_v[s], 0, 0)
        sol = rhs_v[s] + dot3(low, rhs_v[s])
        csol_v[s] = sol
        loads[3 * s + 2].wait()
        tile_v[s] = dot3(off_v[s], sol)

    pl.semaphore_wait(barrier, 1 + NX - 1 + NY - 1 + NZ - 1)
    tg_copy = remote(tg.at[0], tg.at[1], tgs, tgr, sibling, x, y, z)
    tg_copy.start()
    drain.append(tg_copy.wait_send)
    core_copies = []
    for s in range(2):
        copy = remote(
            tile_v.at[s, :, pl.ds(pl.multiple_of(sibling * 128, 128), 128)], trecv.at[s],
            cs.at[s], cr.at[s], sibling, x, y, z,
        )
        copy.start()
        core_copies.append(copy)
        drain.append(copy.wait_send)

    giver = (leaf == z % 2) & (z // 2 < x)
    for load in loads[6:]:
        load.wait()

    def ga_copy(d):
        y2 = (y + d) % NY
        return remote(gsrc.at[y2], grecv.at[z // 2, y], gas.at[d], gar, leaf, x, y2, z)

    @pl.when(giver)
    def _():
        low, _ = tril(td_v[...], 0, 0)
        fac = fac_v[...]
        gt = fac + dot3t(fac, low)
        for y2 in range(NY):
            gsrc[y2] = gt[:, 128 * y2 : 128 * y2 + 128]
        for d in range(1, NY):
            ga_copy(d).start()
        local(gsrc.at[y], grecv.at[z // 2, y], gar).start()

    def gb_copy(d):
        return remote(
            grecv.at[z // 2], grecv.at[z // 2], gs.at[d], gr.at[z // 2], leaf, x, y, (z + d) % NZ
        )

    def g_forward():
        @pl.when(giver)
        def _():
            arrived(grecv.at[z // 2], gar)
            for d in range(1, NZ):
                gb_copy(d).start()

    def g_drain():
        @pl.when(giver)
        def _():
            for d in range(1, NY):
                ga_copy(d).wait_send()
            for d in range(1, NZ):
                gb_copy(d).wait_send()

    drain.append(g_drain)

    row0, col0 = pl.multiple_of(y * 128, 128), pl.multiple_of(leaf * 256, 256)
    low, eye = tril(td_v[pl.ds(row0, 128), pl.ds(col0, 256)], row0, col0)
    tinv[...] = (low + jnp.where(eye, 1.0, 0.0)).T
    rhst[...] = trhs_v[pl.ds(col0, 256), :].T

    half = pl.ds(pl.multiple_of(leaf * 128, 128), 128)
    for s in range(2):
        tcol[256 * s : 256 * s + 256, :] = jnp.broadcast_to(tg[0, s, 0:1, :], (128, 256)).T
        high, rest = split(tile_v[s, :, half].T)
        tt[0:128, 256 * s : 256 * s + 256] = high
        tt[128:256, 256 * s : 256 * s + 256] = rest
    tg_copy.wait_recv()
    for s in range(2):
        tcol[512 + 256 * s : 768 + 256 * s, :] = jnp.broadcast_to(tg[1, s, 0:1, :], (128, 256)).T
        core_copies[s].wait_recv()
        high, rest = split(trecv[s].T)
        tt[0:128, 512 + 256 * s : 768 + 256 * s] = high
        tt[128:256, 512 + 256 * s : 768 + 256 * s] = rest
    lane = lax.broadcasted_iota(jnp.int32, (1024, 128), 1)

    def contrib(q, d):
        block = (x + d) % NX
        rel = tcol[...] - (block * 512 + q * 256).astype(F32)
        lanes = lane.astype(F32)
        hot = jnp.concatenate(
            [jnp.where(rel == lanes, 1.0, 0.0), jnp.where(rel == lanes + 128.0, 1.0, 0.0)], axis=1
        ).astype(BF16)
        both = dot(tt[...], hot)
        cbuf[q, d] = both[0:128] + both[128:256]

    def s1_copy(q, d):
        return remote(
            cbuf.at[q, d], s1recv.at[q, d - 1], s1s.at[q, d], s1r.at[q], leaf, (x + d) % NX, y, z
        )

    for q in range(2):

        def s1_step(d, _, q=q):
            contrib(q, d)
            s1_copy(q, d).start()
            return 0

        lax.fori_loop(1, NX, s1_step, 0)
        drain += [s1_copy(q, d).wait_send for d in range(1, NX)]
        contrib(q, 0)
        if q == 0:
            g_forward()

    def s2_copy(q, e):
        z2 = (z + e) % NZ
        return remote(
            s2src.at[q, z2], s2recv.at[q, e - 1], s2s.at[q, e], s2r.at[q], leaf, x, y, z2
        )

    for q in range(2):
        arrived(s1recv.at[q], s1r.at[q])
        s2src[q] = (cbuf[q, 0] + s1recv[q, 0] + s1recv[q, 1] + s1recv[q, 2]).reshape(NZ, 16, 256)

        def s2_step(e, _, q=q):
            s2_copy(q, e).start()
            return 0

        lax.fori_loop(1, NZ, s2_step, 0)
        drain += [s2_copy(q, e).wait_send for e in range(1, NZ)]

    def s3_copy(q, dy):
        y2 = (y + dy) % NY
        return remote(s3src.at[q], s3recv.at[leaf, dy], s3s.at[q, dy], s3r, q, x, y2, z)

    for q in range(2):
        arrived(s2recv.at[q], s2r.at[q])
        total = s2src[q, z]
        for e in range(NZ - 1):
            total = total + s2recv[q, e]
        s3src[q] = total
        for dy in range(1, NY):
            s3_copy(q, dy).start()

        @pl.when(leaf == q)
        def _(q=q):
            local(s3src.at[q], s3recv.at[leaf, 0], s3r).start()

        @pl.when(leaf != q)
        def _(q=q):
            s3_copy(q, 0).start()

        def s3_drain(q=q):
            for dy in range(1, NY):
                s3_copy(q, dy).wait_send()

            @pl.when(leaf != q)
            def _():
                s3_copy(q, 0).wait_send()

        drain.append(s3_drain)

    arrived(s3recv, s3r)
    reds = []
    for h in range(2):
        upd = s3recv[h, 0] + s3recv[h, 1] + s3recv[h, 2] + s3recv[h, 3]
        reds.append(rhst[pl.ds(pl.multiple_of(h * 128 + z * 16, 16), 16), :] - upd)
    acc = dot3(jnp.concatenate(reds, axis=0), tinv[...])
    fsrc[...] = acc.reshape(2, 16, 128)

    def x_copy(k, x2, y2):
        return remote(
            fsrc, xrecv.at[k, leaf, y % 2], xs.at[x2, y2], xr.at[k], y // 2, x2, y2, z
        )

    for k in range(NX - 1):

        @pl.when(x == k)
        def _(k=k):
            for x2 in range(k + 1, NX):
                for y2 in range(NY):
                    x_copy(k, x2, y2).start()

        @pl.when(x > k)
        def _(k=k):
            @pl.when(z != 2 * k + leaf)
            def _():
                arrived(grecv.at[k], gr.at[k])

            arrived(xrecv.at[k], xr.at[k])
            parts = (xrecv[k, 0] + xrecv[k, 1]).reshape(2, 32, 128)
            solved = jnp.concatenate([parts[0], parts[1]], axis=1)
            step = dot3(solved, grecv[k].reshape(256, 128))
            fsrc[...] = fsrc[...] - step.reshape(2, 16, 128)

        def x_drain(k=k):
            @pl.when(x == k)
            def _():
                for x2 in range(k + 1, NX):
                    for y2 in range(NY):
                        x_copy(k, x2, y2).wait_send()

        drain.append(x_drain)

    def f1_copy(h, e):
        z2 = (z + e) % NZ
        return remote(fsrc.at[h], f1recv.at[leaf, z], f1s.at[h, e], f1r, h, x, y, z2)

    for h in range(2):

        def f1_step(e, _, h=h):
            f1_copy(h, e).start()
            return 0

        lax.fori_loop(1, NZ, f1_step, 0)

        @pl.when(leaf == h)
        def _(h=h):
            local(fsrc.at[h], f1recv.at[leaf, z], f1r).start()

        @pl.when(leaf != h)
        def _(h=h):
            f1_copy(h, 0).start()

        def f1_drain(h=h):
            for e in range(1, NZ):
                f1_copy(h, e).wait_send()

            @pl.when(leaf != h)
            def _():
                f1_copy(h, 0).wait_send()

        drain.append(f1_drain)

    arrived(f1recv, f1r)
    piece = (f1recv[0] + f1recv[1]).reshape(128, 128).T
    def f2_part(d):
        return outv.at[pl.ds(pl.multiple_of((y + d) % NY * 128, 128), 128), half]

    def f2_copy(d):
        return remote(f2_part(0), f2_part(0), f2s.at[d], f2r.at[d], leaf, x, (y + d) % NY, z)

    def f3_copy(d):
        part = f2_part((NY - d) % NY)
        return remote(part, part, f3s.at[d], f3r, sibling, x, y, z)

    outv[pl.ds(row0, 128), half] = piece
    for d in range(1, NY):
        f2_copy(d).start()
    f3_copy(0).start()
    for d in range(1, NY):
        arrived(f2_part(NY - d), f2r.at[d])
        f3_copy(d).start()
    drain += [f2_copy(d).wait_send for d in range(1, NY)]
    drain += [f3_copy(d).wait_send for d in range(NY)]
    arrived(outv.at[:, pl.ds(pl.multiple_of(sibling * 128, 128), 128)], f3r)
    finish()


def shards(child_rhs, child_diag, child_off, live, targets, top_rhs, top_factor, top_diag):
    any_ = pl.BlockSpec(memory_space=pl.ANY)
    vm = pltpu.VMEM
    dma = pltpu.SemaphoreType.DMA
    return pl.pallas_call(
        kernel,
        out_shape=(
            pltpu.VMEM(child_rhs.shape, F32),
            pltpu.VMEM(top_rhs.shape, F32),
        ),
        in_specs=[
            pl.BlockSpec(memory_space=pltpu.SMEM),
            pl.BlockSpec(memory_space=pltpu.VMEM),
        ] + [any_] * 6,
        out_specs=(pl.BlockSpec(memory_space=pltpu.VMEM),) * 2,
        scratch_shapes=[
            vm((2, 256, 256), F32), vm((2, 256, 256), F32), vm((2, 256, 256), F32),
            vm((2, 256, 256), F32),
            vm((512, 256), F32), vm((64, 512), F32), vm((512, 512), F32),
            vm((2, 2, 8, 256), F32), vm((2, 256, 128), F32), vm((1024, 128), F32), vm((256, 1024), BF16),
            vm((2, 4, 128, 256), F32), vm((2, 3, 128, 256), F32),
            vm((2, 8, 16, 256), F32), vm((2, 7, 16, 256), F32),
            vm((2, 16, 256), F32), vm((2, 4, 16, 256), F32),
            vm((256, 256), F32), vm((256, 128), F32),
            vm((4, 64, 128), F32), vm((3, 4, 64, 128), F32),
            vm((2, 16, 128), F32), vm((3, 2, 2, 2, 16, 128), F32),
            vm((2, 8, 16, 128), F32),
            dma((6, 2)), dma, dma, dma((2,)), dma((2,)), dma((4,)), dma, dma((8,)), dma((4,)),
            dma((2, 4)), dma((2,)), dma((2, 8)), dma((2,)), dma((2, 4)), dma,
            dma((4, 4)), dma((3,)), dma((2, 8)), dma, dma((4,)), dma((4,)), dma((4,)), dma,
        ],
        compiler_params=pltpu.CompilerParams(collective_id=0, has_side_effects=True),
    )(live, targets, child_rhs, child_diag, child_off, top_rhs, top_factor.T, top_diag)


def solution(mesh):
    parts = ("leaf", "row", "col")
    in_specs = (
        P(parts, None, None),
        P(parts, None, None),
        P(parts, None, None),
        P(parts),
        P(parts, None),
        P("row", None),
        P("row", "col"),
        P("row", None),
    )
    out_specs = (P(parts, None, None), P("row", None))
    return jax.shard_map(shards, mesh=mesh, in_specs=in_specs, out_specs=out_specs, check_vma=False)
```

```python
import jax
import jax.numpy as jnp
from jax import lax
from jax.experimental import pallas as pl
from jax.experimental.pallas import tpu as pltpu
from jax.sharding import PartitionSpec as P

MESH = pl.DeviceIdType.MESH
F32 = jnp.float32
BF16 = jnp.bfloat16
NX, NY, NZ = 4, 4, 8


def split(value):
    high = value.astype(BF16)
    return high, (value - high.astype(F32)).astype(BF16)


def dot(a, b):
    return jnp.dot(a, b, preferred_element_type=F32)


def dot3(a, b):
    ah, al = split(a)
    bh, bl = split(b)
    return dot(ah, bh) + (dot(ah, bl) + dot(al, bh))


def dot3p(a, bh, bl):
    n = a.shape[0]
    ah, al = split(a)
    both = dot(jnp.concatenate([ah, al], axis=0), bh)
    return both[:n] + (dot(ah, bl) + both[n:])


def dott(a, b):
    return lax.dot_general(a, b, (((1,), (1,)), ((), ())), preferred_element_type=F32)


def dot3t(a, b):
    ah, al = split(a)
    bh, bl = split(b)
    return dott(ah, bh) + (dott(ah, bl) + dott(al, bh))


def tril(value, row0, col0):
    rows = lax.broadcasted_iota(jnp.int32, value.shape, 0) + row0
    cols = lax.broadcasted_iota(jnp.int32, value.shape, 1) + col0
    return jnp.where(rows >= cols, value, 0.0), rows == cols


def kernel(
    live_ref, targ_ref, rhs_hbm, diag_hbm, off_hbm, trhs_hbm, fac_hbm, td_hbm,
    csol_v, outv,
    rhs_v, diag_v, off_v, tile_v, trhs_v, fac_v, td_v,
    tg, trecv, tcol, tt, cbuf, s1recv, s2src, s2recv, s3src, s3recv,
    rhst, tinv, gsrc, grecv, gparts, fsrc, xrecv, frecv, fown, fall,
    load_sem, tgs, tgr, cs, cr, gas, gar, gs, gr, s1s, s1r, s2s, s2r, s3s, s3r, xs, xr, fps, fpr, f1s, f1r, f3s, f3r,
):
    leaf, x, col = lax.axis_index("leaf"), lax.axis_index("row"), lax.axis_index("col")
    y, z = col % NY, col // NY
    sibling = 1 - leaf

    def local(src, dst, sem):
        return pltpu.make_async_copy(src, dst, sem)

    def remote(src, dst, send, recv, l2, x2, y2, z2):
        return pltpu.make_async_remote_copy(
            src_ref=src, dst_ref=dst, send_sem=send, recv_sem=recv,
            device_id=(l2, x2, z2 * NY + y2), device_id_type=MESH,
        )

    def arrived(ref, sem):
        pltpu.make_async_copy(ref, ref, sem).wait()

    drain = []

    def finish():
        for wait in drain:
            wait()

    loads = [
        local(ref.at[s], buf.at[s], load_sem.at[i, s])
        for s in range(2)
        for i, (ref, buf) in enumerate(((diag_hbm, diag_v), (rhs_hbm, rhs_v), (off_hbm, off_v)))
    ] + [
        local(td_hbm, td_v, load_sem.at[3, 0]),
        local(fac_hbm, fac_v, load_sem.at[4, 0]),
        local(trhs_hbm, trhs_v, load_sem.at[5, 0]),
    ]
    for copy in loads:
        copy.start()

    barrier = pltpu.get_barrier_semaphore()

    def greet(l2, x2, y2, z2):
        pl.semaphore_signal(barrier, inc=1, device_id=(l2, x2, z2 * NY + y2), device_id_type=MESH)

    greet(sibling, x, y, z)
    for d in range(1, NX):
        greet(leaf, (x + d) % NX, y, z)
    for d in range(1, NY):
        greet(leaf, x, (y + d) % NY, z)
    for d in range(1, NZ):
        greet(leaf, x, y, (z + d) % NZ)

    lane = lax.broadcasted_iota(jnp.int32, (1, 256), 1)
    for s in range(2):
        row = jnp.where(lane < live_ref[s], targ_ref[s : s + 1, :], -1).astype(F32)
        tg[0, s, :, :] = jnp.broadcast_to(row, (8, 256))

    for s in range(2):
        loads[3 * s].wait()
        loads[3 * s + 1].wait()
        low, _ = tril(diag_v[s], 0, 0)
        sol = rhs_v[s] + dot3(low, rhs_v[s])
        csol_v[s] = sol
        loads[3 * s + 2].wait()
        tile_v[s] = dot3(off_v[s], sol)

    pl.semaphore_wait(barrier, 1 + NX - 1 + NY - 1 + NZ - 1)
    tg_copy = remote(tg.at[0], tg.at[1], tgs, tgr, sibling, x, y, z)
    tg_copy.start()
    drain.append(tg_copy.wait_send)
    core_copies = []
    for s in range(2):
        copy = remote(
            tile_v.at[s, :, pl.ds(pl.multiple_of(sibling * 128, 128), 128)], trecv.at[s],
            cs.at[s], cr.at[s], sibling, x, y, z,
        )
        copy.start()
        core_copies.append(copy)
        drain.append(copy.wait_send)

    giver = (leaf == z % 2) & (z // 2 < x)
    for load in loads[6:]:
        load.wait()

    def ga_copy(d):
        y2 = (y + d) % NY
        return remote(gsrc.at[y2], grecv.at[z // 2, y], gas.at[d], gar, leaf, x, y2, z)

    @pl.when(giver)
    def _():
        low, _ = tril(td_v[...], 0, 0)
        fac = fac_v[...]
        gt = fac + dot3t(fac, low)
        for y2 in range(NY):
            gsrc[y2] = gt[:, 128 * y2 : 128 * y2 + 128]
        for d in range(1, NY):
            ga_copy(d).start()
        local(gsrc.at[y], grecv.at[z // 2, y], gar).start()

    def gb_copy(d):
        return remote(
            grecv.at[z // 2], grecv.at[z // 2], gs.at[d], gr.at[z // 2], leaf, x, y, (z + d) % NZ
        )

    def g_forward():
        @pl.when(giver)
        def _():
            arrived(grecv.at[z // 2], gar)
            for d in range(1, NZ):
                gb_copy(d).start()

    def g_drain():
        @pl.when(giver)
        def _():
            for d in range(1, NY):
                ga_copy(d).wait_send()
            for d in range(1, NZ):
                gb_copy(d).wait_send()

    drain.append(g_drain)

    row0, col0 = pl.multiple_of(y * 128, 128), pl.multiple_of(leaf * 256, 256)
    low, eye = tril(td_v[pl.ds(row0, 128), pl.ds(col0, 256)], row0, col0)
    tinv[0], tinv[1] = split((low + jnp.where(eye, 1.0, 0.0)).T)
    rhst[...] = trhs_v[pl.ds(col0, 256), :].T

    half = pl.ds(pl.multiple_of(leaf * 128, 128), 128)
    for s in range(2):
        tcol[256 * s : 256 * s + 256, :] = jnp.broadcast_to(tg[0, s, 0:1, :], (128, 256)).T
        high, rest = split(tile_v[s, :, half].T)
        tt[0:128, 256 * s : 256 * s + 256] = high
        tt[128:256, 256 * s : 256 * s + 256] = rest
    tg_copy.wait_recv()
    for s in range(2):
        tcol[512 + 256 * s : 768 + 256 * s, :] = jnp.broadcast_to(tg[1, s, 0:1, :], (128, 256)).T
        core_copies[s].wait_recv()
        high, rest = split(trecv[s].T)
        tt[0:128, 512 + 256 * s : 768 + 256 * s] = high
        tt[128:256, 512 + 256 * s : 768 + 256 * s] = rest
    lane = lax.broadcasted_iota(jnp.int32, (1024, 128), 1)

    def contrib(q, d):
        block = (x + d) % NX
        rel = tcol[...] - (block * 512 + q * 256).astype(F32)
        lanes = lane.astype(F32)
        hot = jnp.concatenate(
            [jnp.where(rel == lanes, 1.0, 0.0), jnp.where(rel == lanes + 128.0, 1.0, 0.0)], axis=1
        ).astype(BF16)
        both = dot(tt[...], hot)
        cbuf[q, d] = both[0:128] + both[128:256]

    def s1_copy(q, d):
        return remote(
            cbuf.at[q, d], s1recv.at[q, d - 1], s1s.at[q, d], s1r.at[q], leaf, (x + d) % NX, y, z
        )

    for q in range(2):

        def s1_step(d, _, q=q):
            contrib(q, d)
            s1_copy(q, d).start()
            return 0

        lax.fori_loop(1, NX, s1_step, 0)
        drain += [s1_copy(q, d).wait_send for d in range(1, NX)]
        contrib(q, 0)
        if q == 0:
            g_forward()

    def s2_copy(q, e):
        z2 = (z + e) % NZ
        return remote(
            s2src.at[q, z2], s2recv.at[q, e - 1], s2s.at[q, e], s2r.at[q], leaf, x, y, z2
        )

    for q in range(2):
        arrived(s1recv.at[q], s1r.at[q])
        s2src[q] = (cbuf[q, 0] + s1recv[q, 0] + s1recv[q, 1] + s1recv[q, 2]).reshape(NZ, 16, 256)

        def s2_step(e, _, q=q):
            s2_copy(q, e).start()
            return 0

        lax.fori_loop(1, NZ, s2_step, 0)
        drain += [s2_copy(q, e).wait_send for e in range(1, NZ)]

    def s3_copy(q, dy):
        y2 = (y + dy) % NY
        return remote(s3src.at[q], s3recv.at[leaf, dy], s3s.at[q, dy], s3r, q, x, y2, z)

    for q in range(2):
        arrived(s2recv.at[q], s2r.at[q])
        total = s2src[q, z]
        for e in range(NZ - 1):
            total = total + s2recv[q, e]
        s3src[q] = total
        for dy in range(1, NY):
            s3_copy(q, dy).start()

        @pl.when(leaf == q)
        def _(q=q):
            local(s3src.at[q], s3recv.at[leaf, 0], s3r).start()

        @pl.when(leaf != q)
        def _(q=q):
            s3_copy(q, 0).start()

        def s3_drain(q=q):
            for dy in range(1, NY):
                s3_copy(q, dy).wait_send()

            @pl.when(leaf != q)
            def _():
                s3_copy(q, 0).wait_send()

        drain.append(s3_drain)

    for k in range(NX - 1):

        @pl.when(x > k)
        def _(k=k):
            @pl.when(z != 2 * k + leaf)
            def _():
                arrived(grecv.at[k], gr.at[k])

            high, rest = split(grecv[k].reshape(256, 128))
            gparts[k, 0] = high
            gparts[k, 1] = rest

    arrived(s3recv, s3r)
    reds = []
    for h in range(2):
        upd = s3recv[h, 0] + s3recv[h, 1] + s3recv[h, 2] + s3recv[h, 3]
        reds.append(rhst[pl.ds(pl.multiple_of(h * 128 + z * 16, 16), 16), :] - upd)
    acc = dot3p(jnp.concatenate(reds, axis=0), tinv[0], tinv[1])
    fsrc[...] = acc.reshape(2, 16, 128)

    def x_copy(k, x2, y2):
        return remote(
            fsrc, xrecv.at[k, leaf, y % 2], xs.at[x2, y2], xr.at[k], y // 2, x2, y2, z
        )

    for k in range(NX - 1):

        @pl.when(x == k)
        def _(k=k):
            for x2 in range(k + 1, NX):
                for y2 in range(NY):
                    x_copy(k, x2, y2).start()

        @pl.when(x > k)
        def _(k=k):
            arrived(xrecv.at[k], xr.at[k])
            parts = (xrecv[k, 0] + xrecv[k, 1]).reshape(2, 32, 128)
            solved = jnp.concatenate([parts[0], parts[1]], axis=1)
            step = dot3p(solved, gparts[k, 0], gparts[k, 1])
            fsrc[...] = fsrc[...] - step.reshape(2, 16, 128)

        def x_drain(k=k):
            @pl.when(x == k)
            def _():
                for x2 in range(k + 1, NX):
                    for y2 in range(NY):
                        x_copy(k, x2, y2).wait_send()

        drain.append(x_drain)

    pair = remote(fsrc.at[sibling], frecv, fps, fpr, sibling, x, y, z)
    pair.start()
    drain.append(pair.wait_send)
    pair.wait_recv()
    fown[...] = fsrc[leaf] + frecv[...]

    def f1_copy(dy, dz):
        return remote(
            fown, fall.at[y, z], f1s.at[dy, dz], f1r.at[y], leaf, x, (y + dy) % NY, (z + dz) % NZ
        )

    for dz in (4, 3, 5, 2, 6, 1, 7, 0):
        for dy in (2, 1, 3, 0):
            if dy or dz:
                f1_copy(dy, dz).start()
                drain.append(f1_copy(dy, dz).wait_send)
    local(fown, fall.at[y, z], f1r.at[y]).start()

    def f3_copy(y2):
        part = outv.at[pl.ds(pl.multiple_of(y2 * 128, 128), 128), half]
        return remote(part, part, f3s.at[y2], f3r, sibling, x, y, z)

    for d in (0, 1, 3, 2):
        y2 = (y + d) % NY
        arrived(fall.at[y2], f1r.at[y2])
        outv[pl.ds(pl.multiple_of(y2 * 128, 128), 128), half] = fall[y2].reshape(128, 128).T
        f3_copy(y2).start()
    drain += [f3_copy(y2).wait_send for y2 in range(NY)]
    arrived(outv.at[:, pl.ds(pl.multiple_of(sibling * 128, 128), 128)], f3r)
    finish()


def shards(child_rhs, child_diag, child_off, live, targets, top_rhs, top_factor, top_diag):
    any_ = pl.BlockSpec(memory_space=pl.ANY)
    vm = pltpu.VMEM
    dma = pltpu.SemaphoreType.DMA
    return pl.pallas_call(
        kernel,
        out_shape=(
            pltpu.VMEM(child_rhs.shape, F32),
            pltpu.VMEM(top_rhs.shape, F32),
        ),
        in_specs=[
            pl.BlockSpec(memory_space=pltpu.SMEM),
            pl.BlockSpec(memory_space=pltpu.VMEM),
        ] + [any_] * 6,
        out_specs=(pl.BlockSpec(memory_space=pltpu.VMEM),) * 2,
        scratch_shapes=[
            vm((2, 256, 256), F32), vm((2, 256, 256), F32), vm((2, 256, 256), F32),
            vm((2, 256, 256), F32),
            vm((512, 256), F32), vm((64, 512), F32), vm((512, 512), F32),
            vm((2, 2, 8, 256), F32), vm((2, 256, 128), F32), vm((1024, 128), F32), vm((256, 1024), BF16),
            vm((2, 4, 128, 256), F32), vm((2, 3, 128, 256), F32),
            vm((2, 8, 16, 256), F32), vm((2, 7, 16, 256), F32),
            vm((2, 16, 256), F32), vm((2, 4, 16, 256), F32),
            vm((256, 256), F32), vm((2, 256, 128), BF16),
            vm((4, 64, 128), F32), vm((3, 4, 64, 128), F32), vm((3, 2, 256, 128), BF16),
            vm((2, 16, 128), F32), vm((3, 2, 2, 2, 16, 128), F32),
            vm((16, 128), F32), vm((16, 128), F32), vm((4, 8, 16, 128), F32),
            dma((6, 2)), dma, dma, dma((2,)), dma((2,)), dma((4,)), dma, dma((8,)), dma((4,)),
            dma((2, 4)), dma((2,)), dma((2, 8)), dma((2,)), dma((2, 4)), dma,
            dma((4, 4)), dma((3,)), dma, dma, dma((4, 8)), dma((4,)), dma((4,)), dma,
        ],
        compiler_params=pltpu.CompilerParams(collective_id=0, has_side_effects=True),
    )(live, targets, child_rhs, child_diag, child_off, top_rhs, top_factor.T, top_diag)


def solution(mesh):
    parts = ("leaf", "row", "col")
    in_specs = (
        P(parts, None, None),
        P(parts, None, None),
        P(parts, None, None),
        P(parts),
        P(parts, None),
        P("row", None),
        P("row", "col"),
        P("row", None),
    )
    out_specs = (P(parts, None, None), P("row", None))
    return jax.shard_map(shards, mesh=mesh, in_specs=in_specs, out_specs=out_specs, check_vma=False)
```

```python
import jax
import jax.numpy as jnp
from jax import lax
from jax.experimental import pallas as pl
from jax.experimental.pallas import tpu as pltpu
from jax.sharding import PartitionSpec as P

MESH = pl.DeviceIdType.MESH
F32 = jnp.float32
BF16 = jnp.bfloat16
NX, NY, NZ = 4, 4, 8


def split(value):
    high = value.astype(BF16)
    return high, (value - high.astype(F32)).astype(BF16)


def dot(a, b):
    return jnp.dot(a, b, preferred_element_type=F32)


def dot3(a, b):
    ah, al = split(a)
    bh, bl = split(b)
    return dot(ah, bh) + (dot(ah, bl) + dot(al, bh))


def dot3p(a, bh, bl):
    n = a.shape[0]
    ah, al = split(a)
    both = dot(jnp.concatenate([ah, al], axis=0), bh)
    return both[:n] + (dot(ah, bl) + both[n:])


def dott(a, b):
    return lax.dot_general(a, b, (((1,), (1,)), ((), ())), preferred_element_type=F32)


def dot3t(a, b):
    ah, al = split(a)
    bh, bl = split(b)
    return dott(ah, bh) + (dott(ah, bl) + dott(al, bh))


def tril(value, row0, col0):
    rows = lax.broadcasted_iota(jnp.int32, value.shape, 0) + row0
    cols = lax.broadcasted_iota(jnp.int32, value.shape, 1) + col0
    return jnp.where(rows >= cols, value, 0.0), rows == cols


def kernel(
    live_ref, targ_ref, rhs_hbm, diag_hbm, off_hbm, trhs_hbm, fac_hbm, td_hbm,
    csol_v, outv,
    rhs_v, diag_v, off_v, tile_v, trhs_v, fac_v, td_v,
    tg, trecv, tcol, tt, cbuf, s1recv, s2src, s2recv, s3src, s3recv,
    rhst, tinv, gsrc, grecv, gparts, fsrc, xrecv, frecv, fown, fall,
    load_sem, tgs, tgr, cs, cr, gas, gar, gs, gr, s1s, s1r, s2s, s2r, s3s, s3r, xs, xr, fps, fpr, f1s, f1r, f2s, f2r, f3s, f3r,
):
    leaf, x, col = lax.axis_index("leaf"), lax.axis_index("row"), lax.axis_index("col")
    y, z = col % NY, col // NY
    sibling = 1 - leaf

    def local(src, dst, sem):
        return pltpu.make_async_copy(src, dst, sem)

    def remote(src, dst, send, recv, l2, x2, y2, z2):
        return pltpu.make_async_remote_copy(
            src_ref=src, dst_ref=dst, send_sem=send, recv_sem=recv,
            device_id=(l2, x2, z2 * NY + y2), device_id_type=MESH,
        )

    def arrived(ref, sem):
        pltpu.make_async_copy(ref, ref, sem).wait()

    drain = []

    def finish():
        for wait in drain:
            wait()

    loads = [
        local(ref.at[s], buf.at[s], load_sem.at[i, s])
        for s in range(2)
        for i, (ref, buf) in enumerate(((diag_hbm, diag_v), (rhs_hbm, rhs_v), (off_hbm, off_v)))
    ] + [
        local(td_hbm, td_v, load_sem.at[3, 0]),
        local(fac_hbm, fac_v, load_sem.at[4, 0]),
        local(trhs_hbm, trhs_v, load_sem.at[5, 0]),
    ]
    for copy in loads:
        copy.start()

    barrier = pltpu.get_barrier_semaphore()

    def greet(l2, x2, y2, z2):
        pl.semaphore_signal(barrier, inc=1, device_id=(l2, x2, z2 * NY + y2), device_id_type=MESH)

    greet(sibling, x, y, z)
    for d in range(1, NX):
        greet(leaf, (x + d) % NX, y, z)
    for d in range(1, NY):
        greet(leaf, x, (y + d) % NY, z)
    for d in range(1, NZ):
        greet(leaf, x, y, (z + d) % NZ)

    lane = lax.broadcasted_iota(jnp.int32, (1, 256), 1)
    for s in range(2):
        row = jnp.where(lane < live_ref[s], targ_ref[s : s + 1, :], -1).astype(F32)
        tg[0, s, :, :] = jnp.broadcast_to(row, (8, 256))

    for s in range(2):
        loads[3 * s].wait()
        loads[3 * s + 1].wait()
        low, _ = tril(diag_v[s], 0, 0)
        sol = rhs_v[s] + dot3(low, rhs_v[s])
        csol_v[s] = sol
        loads[3 * s + 2].wait()
        tile_v[s] = dot3(off_v[s], sol)

    pl.semaphore_wait(barrier, 1 + NX - 1 + NY - 1 + NZ - 1)
    tg_copy = remote(tg.at[0], tg.at[1], tgs, tgr, sibling, x, y, z)
    tg_copy.start()
    drain.append(tg_copy.wait_send)
    core_copies = []
    for s in range(2):
        copy = remote(
            tile_v.at[s, :, pl.ds(pl.multiple_of(sibling * 128, 128), 128)], trecv.at[s],
            cs.at[s], cr.at[s], sibling, x, y, z,
        )
        copy.start()
        core_copies.append(copy)
        drain.append(copy.wait_send)

    half = pl.ds(pl.multiple_of(leaf * 128, 128), 128)
    for s in range(2):
        tcol[256 * s : 256 * s + 256, :] = jnp.broadcast_to(tg[0, s, 0:1, :], (128, 256)).T
        high, rest = split(tile_v[s, :, half].T)
        tt[0:128, 256 * s : 256 * s + 256] = high
        tt[128:256, 256 * s : 256 * s + 256] = rest
    tg_copy.wait_recv()
    for s in range(2):
        tcol[512 + 256 * s : 768 + 256 * s, :] = jnp.broadcast_to(tg[1, s, 0:1, :], (128, 256)).T
        core_copies[s].wait_recv()
        high, rest = split(trecv[s].T)
        tt[0:128, 512 + 256 * s : 768 + 256 * s] = high
        tt[128:256, 512 + 256 * s : 768 + 256 * s] = rest
    lane = lax.broadcasted_iota(jnp.int32, (1024, 128), 1)

    def contrib(q, d):
        block = (x + d) % NX
        rel = tcol[...] - (block * 512 + q * 256).astype(F32)
        lanes = lane.astype(F32)
        hot = jnp.concatenate(
            [jnp.where(rel == lanes, 1.0, 0.0), jnp.where(rel == lanes + 128.0, 1.0, 0.0)], axis=1
        ).astype(BF16)
        both = dot(tt[...], hot)
        cbuf[q, d] = both[0:128] + both[128:256]

    def s1_copy(q, d):
        return remote(
            cbuf.at[q, d], s1recv.at[q, d - 1], s1s.at[q, d], s1r.at[q], leaf, (x + d) % NX, y, z
        )

    for q in range(2):

        def s1_step(d, _, q=q):
            contrib(q, d)
            s1_copy(q, d).start()
            return 0

        lax.fori_loop(1, NX, s1_step, 0)
        drain += [s1_copy(q, d).wait_send for d in range(1, NX)]

    giver = (leaf == z % 2) & (z // 2 < x)
    for load in loads[6:]:
        load.wait()

    def ga_copy(d):
        y2 = (y + d) % NY
        return remote(gsrc.at[y2], grecv.at[z // 2, y], gas.at[d], gar, leaf, x, y2, z)

    @pl.when(giver)
    def _():
        low, _ = tril(td_v[...], 0, 0)
        fac = fac_v[...]
        gt = fac + dot3t(fac, low)
        for y2 in range(NY):
            gsrc[y2] = gt[:, 128 * y2 : 128 * y2 + 128]
        for d in range(1, NY):
            ga_copy(d).start()
        local(gsrc.at[y], grecv.at[z // 2, y], gar).start()

    def gb_copy(d):
        return remote(
            grecv.at[z // 2], grecv.at[z // 2], gs.at[d], gr.at[z // 2], leaf, x, y, (z + d) % NZ
        )

    def g_forward():
        @pl.when(giver)
        def _():
            arrived(grecv.at[z // 2], gar)
            for d in range(1, NZ):
                gb_copy(d).start()

    def g_drain():
        @pl.when(giver)
        def _():
            for d in range(1, NY):
                ga_copy(d).wait_send()
            for d in range(1, NZ):
                gb_copy(d).wait_send()

    drain.append(g_drain)

    row0, col0 = pl.multiple_of(y * 128, 128), pl.multiple_of(leaf * 256, 256)
    low, eye = tril(td_v[pl.ds(row0, 128), pl.ds(col0, 256)], row0, col0)
    tinv[0], tinv[1] = split((low + jnp.where(eye, 1.0, 0.0)).T)
    rhst[...] = trhs_v[pl.ds(col0, 256), :].T

    for q in range(2):
        contrib(q, 0)

    def s2_copy(q, e):
        z2 = (z + e) % NZ
        return remote(
            s2src.at[q, z2], s2recv.at[q, e - 1], s2s.at[q, e], s2r.at[q], leaf, x, y, z2
        )

    for q in range(2):
        arrived(s1recv.at[q], s1r.at[q])
        s2src[q] = (cbuf[q, 0] + s1recv[q, 0] + s1recv[q, 1] + s1recv[q, 2]).reshape(NZ, 16, 256)

        def s2_step(e, _, q=q):
            s2_copy(q, e).start()
            return 0

        lax.fori_loop(1, NZ, s2_step, 0)
        drain += [s2_copy(q, e).wait_send for e in range(1, NZ)]
    g_forward()

    def s3_copy(q, dy):
        y2 = (y + dy) % NY
        return remote(s3src.at[q], s3recv.at[leaf, dy], s3s.at[q, dy], s3r, q, x, y2, z)

    for q in range(2):
        arrived(s2recv.at[q], s2r.at[q])
        total = s2src[q, z]
        for e in range(NZ - 1):
            total = total + s2recv[q, e]
        s3src[q] = total
        for dy in range(1, NY):
            s3_copy(q, dy).start()

        @pl.when(leaf == q)
        def _(q=q):
            local(s3src.at[q], s3recv.at[leaf, 0], s3r).start()

        @pl.when(leaf != q)
        def _(q=q):
            s3_copy(q, 0).start()

        def s3_drain(q=q):
            for dy in range(1, NY):
                s3_copy(q, dy).wait_send()

            @pl.when(leaf != q)
            def _():
                s3_copy(q, 0).wait_send()

        drain.append(s3_drain)

    arrived(s3recv, s3r)
    reds = []
    for h in range(2):
        upd = s3recv[h, 0] + s3recv[h, 1] + s3recv[h, 2] + s3recv[h, 3]
        reds.append(rhst[pl.ds(pl.multiple_of(h * 128 + z * 16, 16), 16), :] - upd)
    acc = dot3p(jnp.concatenate(reds, axis=0), tinv[0], tinv[1])
    fsrc[...] = acc.reshape(2, 16, 128)

    def x_copy(k, x2, y2):
        return remote(
            fsrc, xrecv.at[k, leaf, y % 2], xs.at[x2, y2], xr.at[k], y // 2, x2, y2, z
        )

    for k in range(NX - 1):

        @pl.when(x == k)
        def _(k=k):
            for x2 in range(k + 1, NX):
                for y2 in range(NY):
                    x_copy(k, x2, y2).start()

        @pl.when(x > k)
        def _(k=k):
            @pl.when(z != 2 * k + leaf)
            def _():
                arrived(grecv.at[k], gr.at[k])

            high, rest = split(grecv[k].reshape(256, 128))
            gparts[k, 0] = high
            gparts[k, 1] = rest
            arrived(xrecv.at[k], xr.at[k])
            parts = (xrecv[k, 0] + xrecv[k, 1]).reshape(2, 32, 128)
            solved = jnp.concatenate([parts[0], parts[1]], axis=1)
            step = dot3p(solved, gparts[k, 0], gparts[k, 1])
            fsrc[...] = fsrc[...] - step.reshape(2, 16, 128)

        def x_drain(k=k):
            @pl.when(x == k)
            def _():
                for x2 in range(k + 1, NX):
                    for y2 in range(NY):
                        x_copy(k, x2, y2).wait_send()

        drain.append(x_drain)

    pair = remote(fsrc.at[sibling], frecv, fps, fpr, sibling, x, y, z)
    pair.start()
    drain.append(pair.wait_send)
    pair.wait_recv()
    fown[...] = fsrc[leaf] + frecv[...]

    def f1_copy(d):
        return remote(fown, fall.at[y, z], f1s.at[d], f1r.at[d], leaf, x, y, (z + d) % NZ)

    def f2_copy(d, dy):
        part = fall.at[y, (z + NZ - d) % NZ]
        return remote(part, part, f2s.at[d, dy], f2r.at[y], leaf, x, (y + dy) % NY, z)

    for d in (4, 3, 5, 2, 6, 1, 7):
        f1_copy(d).start()
        drain.append(f1_copy(d).wait_send)
    fall[y, z] = fown[...]
    for d in (0, 1, 7, 2, 6, 3, 5, 4):
        if d:
            arrived(fall.at[y, (z + NZ - d) % NZ], f1r.at[d])
        for dy in (2, 1, 3):
            f2_copy(d, dy).start()
            drain.append(f2_copy(d, dy).wait_send)

    def f3_copy(y2):
        part = outv.at[pl.ds(pl.multiple_of(y2 * 128, 128), 128), half]
        return remote(part, part, f3s.at[y2], f3r, sibling, x, y, z)

    for d in (0, 1, 3, 2):
        y2 = (y + d) % NY
        if d:
            arrived(fall.at[y2], f2r.at[y2])
        outv[pl.ds(pl.multiple_of(y2 * 128, 128), 128), half] = fall[y2].reshape(128, 128).T
        f3_copy(y2).start()
    drain += [f3_copy(y2).wait_send for y2 in range(NY)]
    arrived(outv.at[:, pl.ds(pl.multiple_of(sibling * 128, 128), 128)], f3r)
    finish()


def shards(child_rhs, child_diag, child_off, live, targets, top_rhs, top_factor, top_diag):
    any_ = pl.BlockSpec(memory_space=pl.ANY)
    vm = pltpu.VMEM
    dma = pltpu.SemaphoreType.DMA
    return pl.pallas_call(
        kernel,
        out_shape=(
            pltpu.VMEM(child_rhs.shape, F32),
            pltpu.VMEM(top_rhs.shape, F32),
        ),
        in_specs=[
            pl.BlockSpec(memory_space=pltpu.SMEM),
            pl.BlockSpec(memory_space=pltpu.VMEM),
        ] + [any_] * 6,
        out_specs=(pl.BlockSpec(memory_space=pltpu.VMEM),) * 2,
        scratch_shapes=[
            vm((2, 256, 256), F32), vm((2, 256, 256), F32), vm((2, 256, 256), F32),
            vm((2, 256, 256), F32),
            vm((512, 256), F32), vm((64, 512), F32), vm((512, 512), F32),
            vm((2, 2, 8, 256), F32), vm((2, 256, 128), F32), vm((1024, 128), F32), vm((256, 1024), BF16),
            vm((2, 4, 128, 256), F32), vm((2, 3, 128, 256), F32),
            vm((2, 8, 16, 256), F32), vm((2, 7, 16, 256), F32),
            vm((2, 16, 256), F32), vm((2, 4, 16, 256), F32),
            vm((256, 256), F32), vm((2, 256, 128), BF16),
            vm((4, 64, 128), F32), vm((3, 4, 64, 128), F32), vm((3, 2, 256, 128), BF16),
            vm((2, 16, 128), F32), vm((3, 2, 2, 2, 16, 128), F32),
            vm((16, 128), F32), vm((16, 128), F32), vm((4, 8, 16, 128), F32),
            dma((6, 2)), dma, dma, dma((2,)), dma((2,)), dma((4,)), dma, dma((8,)), dma((4,)),
            dma((2, 4)), dma((2,)), dma((2, 8)), dma((2,)), dma((2, 4)), dma,
            dma((4, 4)), dma((3,)), dma, dma, dma((8,)), dma((8,)), dma((8, 4)), dma((4,)), dma((4,)), dma,
        ],
        compiler_params=pltpu.CompilerParams(collective_id=0, has_side_effects=True),
    )(live, targets, child_rhs, child_diag, child_off, top_rhs, top_factor.T, top_diag)


def solution(mesh):
    parts = ("leaf", "row", "col")
    in_specs = (
        P(parts, None, None),
        P(parts, None, None),
        P(parts, None, None),
        P(parts),
        P(parts, None),
        P("row", None),
        P("row", "col"),
        P("row", None),
    )
    out_specs = (P(parts, None, None), P("row", None))
    return jax.shard_map(shards, mesh=mesh, in_specs=in_specs, out_specs=out_specs, check_vma=False)
```

```python
import jax
import jax.numpy as jnp
from jax import lax
from jax.experimental import pallas as pl
from jax.experimental.pallas import tpu as pltpu
from jax.sharding import PartitionSpec as P

MESH = pl.DeviceIdType.MESH
F32 = jnp.float32
BF16 = jnp.bfloat16
NX, NY, NZ = 4, 4, 8


def split(value):
    high = value.astype(BF16)
    return high, (value - high.astype(F32)).astype(BF16)


def dot(a, b):
    return jnp.dot(a, b, preferred_element_type=F32)


def dot3(a, b):
    ah, al = split(a)
    bh, bl = split(b)
    return dot(ah, bh) + (dot(ah, bl) + dot(al, bh))


def dot3p(a, bh, bl):
    n = a.shape[0]
    ah, al = split(a)
    both = dot(jnp.concatenate([ah, al], axis=0), bh)
    return both[:n] + (dot(ah, bl) + both[n:])


def dott(a, b):
    return lax.dot_general(a, b, (((1,), (1,)), ((), ())), preferred_element_type=F32)


def dot3t(a, b):
    ah, al = split(a)
    bh, bl = split(b)
    return dott(ah, bh) + (dott(ah, bl) + dott(al, bh))


def tril(value, row0, col0):
    rows = lax.broadcasted_iota(jnp.int32, value.shape, 0) + row0
    cols = lax.broadcasted_iota(jnp.int32, value.shape, 1) + col0
    return jnp.where(rows >= cols, value, 0.0), rows == cols


def kernel(
    live_ref, targ_ref, rhs_hbm, diag_hbm, off_hbm, trhs_hbm, fac_hbm, td_hbm,
    csol_v, outv,
    rhs_v, diag_v, off_v, tile_v, trhs_v, fac_v, td_v,
    tg, trecv, tcol, tt, cbuf, axrecv, ybuf, byrecv, ysum, bxrecv, azsrc, azrecv, bzsrc, bzrecv,
    aysrc, ayrecv, cysrc, cyrecv, upd,
    rhst, tinv, gsrc, grecv, gparts, fsrc, xrecv, frecv, fown, fall,
    load_sem, tgs, tgr, cs, cr, gas, gar, gs, gr, axs, axr, bys, byr, bxs, bxr, azs, azr,
    bzs, bzr, ays, ayr, cys, cyr, xs, xr, fps, fpr, f1s, f1r, f2s, f2r, f3s, f3r,
):
    leaf, x, col = lax.axis_index("leaf"), lax.axis_index("row"), lax.axis_index("col")
    y, z = col % NY, col // NY
    sibling = 1 - leaf

    def local(src, dst, sem):
        return pltpu.make_async_copy(src, dst, sem)

    def remote(src, dst, send, recv, l2, x2, y2, z2):
        return pltpu.make_async_remote_copy(
            src_ref=src, dst_ref=dst, send_sem=send, recv_sem=recv,
            device_id=(l2, x2, z2 * NY + y2), device_id_type=MESH,
        )

    def arrived(ref, sem):
        pltpu.make_async_copy(ref, ref, sem).wait()

    drain = []

    def finish():
        for wait in drain:
            wait()

    loads = [
        local(ref.at[s], buf.at[s], load_sem.at[i, s])
        for s in range(2)
        for i, (ref, buf) in enumerate(((diag_hbm, diag_v), (rhs_hbm, rhs_v), (off_hbm, off_v)))
    ] + [
        local(td_hbm, td_v, load_sem.at[3, 0]),
        local(fac_hbm, fac_v, load_sem.at[4, 0]),
        local(trhs_hbm, trhs_v, load_sem.at[5, 0]),
    ]
    for copy in loads:
        copy.start()

    barrier = pltpu.get_barrier_semaphore()

    def greet(l2, x2, y2, z2):
        pl.semaphore_signal(barrier, inc=1, device_id=(l2, x2, z2 * NY + y2), device_id_type=MESH)

    greet(sibling, x, y, z)
    for d in range(1, NX):
        greet(leaf, (x + d) % NX, y, z)
    for d in range(1, NY):
        greet(leaf, x, (y + d) % NY, z)
    for d in range(1, NZ):
        greet(leaf, x, y, (z + d) % NZ)

    lane = lax.broadcasted_iota(jnp.int32, (1, 256), 1)
    for s in range(2):
        row = jnp.where(lane < live_ref[s], targ_ref[s : s + 1, :], -1).astype(F32)
        tg[0, s, :, :] = jnp.broadcast_to(row, (8, 256))

    for s in range(2):
        loads[3 * s].wait()
        loads[3 * s + 1].wait()
        low, _ = tril(diag_v[s], 0, 0)
        sol = rhs_v[s] + dot3(low, rhs_v[s])
        csol_v[s] = sol
        loads[3 * s + 2].wait()
        tile_v[s] = dot3(off_v[s], sol)

    pl.semaphore_wait(barrier, 1 + NX - 1 + NY - 1 + NZ - 1)
    tg_copy = remote(tg.at[0], tg.at[1], tgs, tgr, sibling, x, y, z)
    tg_copy.start()
    drain.append(tg_copy.wait_send)
    core_copies = []
    for s in range(2):
        copy = remote(
            tile_v.at[s, :, pl.ds(pl.multiple_of(sibling * 128, 128), 128)], trecv.at[s],
            cs.at[s], cr.at[s], sibling, x, y, z,
        )
        copy.start()
        core_copies.append(copy)
        drain.append(copy.wait_send)

    half = pl.ds(pl.multiple_of(leaf * 128, 128), 128)
    for s in range(2):
        tcol[256 * s : 256 * s + 256, :] = jnp.broadcast_to(tg[0, s, 0:1, :], (128, 256)).T
        high, rest = split(tile_v[s, :, half].T)
        tt[0:128, 256 * s : 256 * s + 256] = high
        tt[128:256, 256 * s : 256 * s + 256] = rest
    tg_copy.wait_recv()
    for s in range(2):
        tcol[512 + 256 * s : 768 + 256 * s, :] = jnp.broadcast_to(tg[1, s, 0:1, :], (128, 256)).T
        core_copies[s].wait_recv()
        high, rest = split(trecv[s].T)
        tt[0:128, 512 + 256 * s : 768 + 256 * s] = high
        tt[128:256, 512 + 256 * s : 768 + 256 * s] = rest
    lane = lax.broadcasted_iota(jnp.int32, (1024, 128), 1)

    def contrib(start):
        rel = tcol[...] - start.astype(F32)
        lanes = lane.astype(F32)
        hot = jnp.concatenate(
            [jnp.where(rel == lanes, 1.0, 0.0), jnp.where(rel == lanes + 128.0, 1.0, 0.0)], axis=1
        ).astype(BF16)
        both = dot(tt[...], hot)
        return both[0:128] + both[128:256]

    def ax_copy(d):
        return remote(cbuf.at[d], axrecv.at[d - 1], axs.at[d], axr, leaf, (x + d) % NX, y, z)

    def by_copy(d, b):
        y2 = (y + d) % NY
        return remote(ybuf.at[y2, b], byrecv.at[d - 1, b], bys.at[d, b], byr, leaf, x, y2, z)

    def lower(d):
        cbuf[d] = contrib((x + d) % NX * 512)

    def upper(b, _):
        value = contrib(b * 512 + 256)
        for part in range(NY):
            ybuf[part, b] = value[
                part % 2 * 64 : part % 2 * 64 + 64, part // 2 * 128 : part // 2 * 128 + 128
            ]
        for d in (2, 1, 3):
            by_copy(d, b).start()
        return 0

    def lower_upper(i, _):
        d = (i * 2 + 1) % NX + i // 2
        lower(d)
        ax_copy(d).start()
        upper(i, 0)
        return 0

    lax.fori_loop(0, 3, lower_upper, 0)
    upper(jnp.int32(3), 0)
    drain += [ax_copy(d).wait_send for d in range(1, NX)]
    drain += [by_copy(d, b).wait_send for d in range(1, NY) for b in range(NX)]

    giver = (leaf == z % 2) & (z // 2 < x)
    for load in loads[6:]:
        load.wait()

    def ga_copy(d):
        y2 = (y + d) % NY
        return remote(gsrc.at[y2], grecv.at[z // 2, y], gas.at[d], gar, leaf, x, y2, z)

    @pl.when(giver)
    def _():
        low, _ = tril(td_v[...], 0, 0)
        fac = fac_v[...]
        gt = fac + dot3t(fac, low)
        for y2 in range(NY):
            gsrc[y2] = gt[:, 128 * y2 : 128 * y2 + 128]
        for d in range(1, NY):
            ga_copy(d).start()
        local(gsrc.at[y], grecv.at[z // 2, y], gar).start()

    def gb_copy(d):
        return remote(
            grecv.at[z // 2], grecv.at[z // 2], gs.at[d], gr.at[z // 2], leaf, x, y, (z + d) % NZ
        )

    def g_forward():
        @pl.when(giver)
        def _():
            arrived(grecv.at[z // 2], gar)
            for d in range(1, NZ):
                gb_copy(d).start()

    def g_drain():
        @pl.when(giver)
        def _():
            for d in range(1, NY):
                ga_copy(d).wait_send()
            for d in range(1, NZ):
                gb_copy(d).wait_send()

    drain.append(g_drain)

    row0, col0 = pl.multiple_of(y * 128, 128), pl.multiple_of(leaf * 256, 256)
    low, eye = tril(td_v[pl.ds(row0, 128), pl.ds(col0, 256)], row0, col0)
    tinv[0], tinv[1] = split((low + jnp.where(eye, 1.0, 0.0)).T)
    rhst[...] = trhs_v[pl.ds(col0, 256), :].T

    lower(0)

    arrived(byrecv, byr)

    def bx_copy(d):
        block = (x + d) % NX
        return remote(ysum.at[block], bxrecv.at[d - 1], bxs.at[d], bxr, leaf, block, y, z)

    def add_y(d):
        b = (x + d) % NX
        ysum[b] = ybuf[y, b] + byrecv[0, b] + byrecv[1, b] + byrecv[2, b]

    for d in (2, 1, 3):
        add_y(d)
        bx_copy(d).start()
        drain.append(bx_copy(d).wait_send)
    add_y(0)

    def az_copy(e):
        z2 = (z + e) % NZ
        return remote(azsrc.at[z2], azrecv.at[e - 1], azs.at[e], azr, leaf, x, y, z2)

    arrived(axrecv, axr)
    azsrc[...] = (cbuf[0] + axrecv[0] + axrecv[1] + axrecv[2]).reshape(NZ, 16, 256)
    for e in (4, 3, 5, 2, 6, 1, 7):
        az_copy(e).start()
        drain.append(az_copy(e).wait_send)

    keeper = z // 4 == y % 2

    def bz_copy(i):
        z2 = y % 2 * 4 + i
        return z2 != z, remote(bzsrc.at[i], bzrecv.at[z], bzs.at[i], bzr, leaf, x, y, z2)

    arrived(bxrecv, bxr)
    bzsrc[...] = (ysum[x] + bxrecv[0] + bxrecv[1] + bxrecv[2]).reshape(4, 16, 128)
    for i in range(4):
        away, copy = bz_copy(i)
        pl.when(away)(copy.start)

    def bz_drain():
        for i in range(4):
            away, copy = bz_copy(i)
            pl.when(away)(copy.wait_send)

    drain.append(bz_drain)
    pl.when(keeper)(local(bzsrc.at[z % 4], bzrecv.at[z], bzr).start)
    g_forward()

    def ay_copy(dy):
        return remote(aysrc, ayrecv.at[leaf, dy], ays.at[dy], ayr, 0, x, (y + dy) % NY, z)

    arrived(azrecv, azr)
    total = azsrc[z]
    for e in range(NZ - 1):
        total = total + azrecv[e]
    aysrc[...] = total
    for dy in (2, 1, 3):
        ay_copy(dy).start()
        drain.append(ay_copy(dy).wait_send)
    pl.when(leaf == 0)(local(aysrc, ayrecv.at[leaf, 0], ayr).start)
    pl.when(leaf == 1)(ay_copy(0).start)
    drain.append(lambda: pl.when(leaf == 1)(ay_copy(0).wait_send))

    def cy_copy(dy):
        return remote(cysrc, cyrecv.at[leaf, y // 2], cys.at[dy], cyr, 1, x, (y + dy) % NY, z)

    @pl.when(keeper)
    def _():
        arrived(bzrecv, bzr)
        total = bzrecv[0]
        for e in range(1, NZ):
            total = total + bzrecv[e]
        cysrc[...] = total
        for dy in (2, 1, 3):
            cy_copy(dy).start()
        pl.when(leaf == 1)(local(cysrc, cyrecv.at[leaf, y // 2], cyr).start)
        pl.when(leaf == 0)(cy_copy(0).start)

    def cy_drain():
        @pl.when(keeper)
        def _():
            for dy in range(1, NY):
                cy_copy(dy).wait_send()
            pl.when(leaf == 0)(cy_copy(0).wait_send)

    drain.append(cy_drain)

    @pl.when(leaf == 0)
    def _():
        arrived(ayrecv, ayr)
        for h in range(2):
            upd[h] = ayrecv[h, 0] + ayrecv[h, 1] + ayrecv[h, 2] + ayrecv[h, 3]

    @pl.when(leaf == 1)
    def _():
        arrived(cyrecv, cyr)
        for h in range(2):
            upd[h] = jnp.concatenate([cyrecv[h, 0], cyrecv[h, 1]], axis=1)

    reds = []
    for h in range(2):
        reds.append(rhst[pl.ds(pl.multiple_of(h * 128 + z * 16, 16), 16), :] - upd[h])
    acc = dot3p(jnp.concatenate(reds, axis=0), tinv[0], tinv[1])
    fsrc[...] = acc.reshape(2, 16, 128)

    def x_copy(k, x2, y2):
        return remote(
            fsrc, xrecv.at[k, leaf, y % 2], xs.at[x2, y2], xr.at[k], y // 2, x2, y2, z
        )

    for k in range(NX - 1):

        @pl.when(x == k)
        def _(k=k):
            for x2 in range(k + 1, NX):
                for y2 in range(NY):
                    x_copy(k, x2, y2).start()

        @pl.when(x > k)
        def _(k=k):
            @pl.when(z != 2 * k + leaf)
            def _():
                arrived(grecv.at[k], gr.at[k])

            high, rest = split(grecv[k].reshape(256, 128))
            gparts[k, 0] = high
            gparts[k, 1] = rest
            arrived(xrecv.at[k], xr.at[k])
            parts = (xrecv[k, 0] + xrecv[k, 1]).reshape(2, 32, 128)
            solved = jnp.concatenate([parts[0], parts[1]], axis=1)
            step = dot3p(solved, gparts[k, 0], gparts[k, 1])
            fsrc[...] = fsrc[...] - step.reshape(2, 16, 128)

        def x_drain(k=k):
            @pl.when(x == k)
            def _():
                for x2 in range(k + 1, NX):
                    for y2 in range(NY):
                        x_copy(k, x2, y2).wait_send()

        drain.append(x_drain)

    pair = remote(fsrc.at[sibling], frecv, fps, fpr, sibling, x, y, z)
    pair.start()
    drain.append(pair.wait_send)
    pair.wait_recv()
    fown[...] = fsrc[leaf] + frecv[...]

    def f1_copy(d):
        return remote(fown, fall.at[y, z], f1s.at[d], f1r.at[d], leaf, x, y, (z + d) % NZ)

    def f2_copy(d, dy):
        part = fall.at[y, (z + NZ - d) % NZ]
        return remote(part, part, f2s.at[d, dy], f2r.at[y], leaf, x, (y + dy) % NY, z)

    for d in (4, 3, 5, 2, 6, 1, 7):
        f1_copy(d).start()
        drain.append(f1_copy(d).wait_send)
    fall[y, z] = fown[...]
    for d in (0, 1, 7, 2, 6, 3, 5, 4):
        if d:
            arrived(fall.at[y, (z + NZ - d) % NZ], f1r.at[d])
        for dy in (2, 1, 3):
            f2_copy(d, dy).start()
            drain.append(f2_copy(d, dy).wait_send)

    def f3_copy(y2):
        part = outv.at[pl.ds(pl.multiple_of(y2 * 128, 128), 128), half]
        return remote(part, part, f3s.at[y2], f3r, sibling, x, y, z)

    for d in (0, 1, 3, 2):
        y2 = (y + d) % NY
        if d:
            arrived(fall.at[y2], f2r.at[y2])
        outv[pl.ds(pl.multiple_of(y2 * 128, 128), 128), half] = fall[y2].reshape(128, 128).T
        f3_copy(y2).start()
    drain += [f3_copy(y2).wait_send for y2 in range(NY)]
    arrived(outv.at[:, pl.ds(pl.multiple_of(sibling * 128, 128), 128)], f3r)
    finish()


def shards(child_rhs, child_diag, child_off, live, targets, top_rhs, top_factor, top_diag):
    any_ = pl.BlockSpec(memory_space=pl.ANY)
    vm = pltpu.VMEM
    dma = pltpu.SemaphoreType.DMA
    return pl.pallas_call(
        kernel,
        out_shape=(
            pltpu.VMEM(child_rhs.shape, F32),
            pltpu.VMEM(top_rhs.shape, F32),
        ),
        in_specs=[
            pl.BlockSpec(memory_space=pltpu.SMEM),
            pl.BlockSpec(memory_space=pltpu.VMEM),
        ] + [any_] * 6,
        out_specs=(pl.BlockSpec(memory_space=pltpu.VMEM),) * 2,
        scratch_shapes=[
            vm((2, 256, 256), F32), vm((2, 256, 256), F32), vm((2, 256, 256), F32),
            vm((2, 256, 256), F32),
            vm((512, 256), F32), vm((64, 512), F32), vm((512, 512), F32),
            vm((2, 2, 8, 256), F32), vm((2, 256, 128), F32), vm((1024, 128), F32), vm((256, 1024), BF16),
            vm((4, 128, 256), F32), vm((3, 128, 256), F32),
            vm((4, 4, 64, 128), F32), vm((3, 4, 64, 128), F32), vm((4, 64, 128), F32), vm((3, 64, 128), F32),
            vm((8, 16, 256), F32), vm((7, 16, 256), F32), vm((4, 16, 128), F32), vm((8, 16, 128), F32),
            vm((16, 256), F32), vm((2, 4, 16, 256), F32), vm((16, 128), F32), vm((2, 2, 16, 128), F32),
            vm((2, 16, 256), F32),
            vm((256, 256), F32), vm((2, 256, 128), BF16),
            vm((4, 64, 128), F32), vm((3, 4, 64, 128), F32), vm((3, 2, 256, 128), BF16),
            vm((2, 16, 128), F32), vm((3, 2, 2, 2, 16, 128), F32),
            vm((16, 128), F32), vm((16, 128), F32), vm((4, 8, 16, 128), F32),
            dma((6, 2)), dma, dma, dma((2,)), dma((2,)), dma((4,)), dma, dma((8,)), dma((4,)),
            dma((4,)), dma, dma((4, 4)), dma, dma((4,)), dma, dma((8,)), dma,
            dma((4,)), dma, dma((4,)), dma, dma((4,)), dma,
            dma((4, 4)), dma((3,)), dma, dma, dma((8,)), dma((8,)), dma((8, 4)), dma((4,)), dma((4,)), dma,
        ],
        compiler_params=pltpu.CompilerParams(collective_id=0, has_side_effects=True),
    )(live, targets, child_rhs, child_diag, child_off, top_rhs, top_factor.T, top_diag)


def solution(mesh):
    parts = ("leaf", "row", "col")
    in_specs = (
        P(parts, None, None),
        P(parts, None, None),
        P(parts, None, None),
        P(parts),
        P(parts, None),
        P("row", None),
        P("row", "col"),
        P("row", None),
    )
    out_specs = (P(parts, None, None), P("row", None))
    return jax.shard_map(shards, mesh=mesh, in_specs=in_specs, out_specs=out_specs, check_vma=False)
```

```python
import jax
import jax.numpy as jnp
from jax import lax
from jax.experimental import pallas as pl
from jax.experimental.pallas import tpu as pltpu
from jax.sharding import PartitionSpec as P

MESH = pl.DeviceIdType.MESH
F32 = jnp.float32
BF16 = jnp.bfloat16
NX, NY, NZ = 4, 4, 8


def split(value):
    high = value.astype(BF16)
    return high, (value - high.astype(F32)).astype(BF16)


def dot(a, b):
    return jnp.dot(a, b, preferred_element_type=F32)


def dot3(a, b):
    ah, al = split(a)
    bh, bl = split(b)
    return dot(ah, bh) + (dot(ah, bl) + dot(al, bh))


def dot3p(a, bh, bl):
    n = a.shape[0]
    ah, al = split(a)
    both = dot(jnp.concatenate([ah, al], axis=0), bh)
    return both[:n] + (dot(ah, bl) + both[n:])


def dott(a, b):
    return lax.dot_general(a, b, (((1,), (1,)), ((), ())), preferred_element_type=F32)


def dot3t(a, b):
    ah, al = split(a)
    bh, bl = split(b)
    return dott(ah, bh) + (dott(ah, bl) + dott(al, bh))


def tril(value, row0, col0):
    rows = lax.broadcasted_iota(jnp.int32, value.shape, 0) + row0
    cols = lax.broadcasted_iota(jnp.int32, value.shape, 1) + col0
    return jnp.where(rows >= cols, value, 0.0), rows == cols


def kernel(
    live_ref, targ_ref, rhs_hbm, diag_hbm, off_hbm, trhs_hbm, fac_hbm, td_hbm,
    csol_v, outv,
    rhs_v, diag_v, off_v, tile_v, trhs_v, fac_v, td_v,
    tg, trecv, tcol, tt, cbuf, axrecv, ybuf, byrecv, ysum, bxrecv, azsrc, azrecv, bzsrc, bzrecv,
    aysrc, ayrecv, cysrc, cyrecv, upd,
    rhst, tinv, gsrc, grecv, gparts, fsrc, xrecv, frecv, fown, fall,
    load_sem, tgs, tgr, cs, cr, gas, gar, gs, gr, axs, axr, bys, byr, bxs, bxr, azs, azr,
    bzs, bzr, ays, ayr, cys, cyr, xs, xr, fps, fpr, f1s, f1r, f2s, f2r, f3s, f3r,
):
    leaf, x, col = lax.axis_index("leaf"), lax.axis_index("row"), lax.axis_index("col")
    y, z = col % NY, col // NY
    sibling = 1 - leaf

    def local(src, dst, sem):
        return pltpu.make_async_copy(src, dst, sem)

    def remote(src, dst, send, recv, l2, x2, y2, z2):
        return pltpu.make_async_remote_copy(
            src_ref=src, dst_ref=dst, send_sem=send, recv_sem=recv,
            device_id=(l2, x2, z2 * NY + y2), device_id_type=MESH,
        )

    def arrived(ref, sem):
        pltpu.make_async_copy(ref, ref, sem).wait()

    drain = []

    def finish():
        for wait in drain:
            wait()

    loads = [
        local(ref.at[s], buf.at[s], load_sem.at[i, s])
        for s in range(2)
        for i, (ref, buf) in enumerate(((diag_hbm, diag_v), (rhs_hbm, rhs_v), (off_hbm, off_v)))
    ] + [
        local(td_hbm, td_v, load_sem.at[3, 0]),
        local(fac_hbm, fac_v, load_sem.at[4, 0]),
        local(trhs_hbm, trhs_v, load_sem.at[5, 0]),
    ]
    for copy in loads:
        copy.start()

    barrier = pltpu.get_barrier_semaphore()

    def greet(l2, x2, y2, z2):
        pl.semaphore_signal(barrier, inc=1, device_id=(l2, x2, z2 * NY + y2), device_id_type=MESH)

    greet(sibling, x, y, z)
    for d in range(1, NX):
        greet(leaf, (x + d) % NX, y, z)
    for d in range(1, NY):
        greet(leaf, x, (y + d) % NY, z)
    for d in range(1, NZ):
        greet(leaf, x, y, (z + d) % NZ)

    lane = lax.broadcasted_iota(jnp.int32, (1, 256), 1)
    for s in range(2):
        row = jnp.where(lane < live_ref[s], targ_ref[s : s + 1, :], -1).astype(F32)
        tg[0, s, :, :] = jnp.broadcast_to(row, (8, 256))

    for s in range(2):
        loads[3 * s].wait()
        loads[3 * s + 1].wait()
        low, _ = tril(diag_v[s], 0, 0)
        sol = rhs_v[s] + dot3(low, rhs_v[s])
        csol_v[s] = sol
        loads[3 * s + 2].wait()
        tile_v[s] = dot3(off_v[s], sol)

    pl.semaphore_wait(barrier, 1 + NX - 1 + NY - 1 + NZ - 1)
    tg_copy = remote(tg.at[0], tg.at[1], tgs, tgr, sibling, x, y, z)
    tg_copy.start()
    drain.append(tg_copy.wait_send)
    core_copies = []
    for s in range(2):
        copy = remote(
            tile_v.at[s, :, pl.ds(pl.multiple_of(sibling * 128, 128), 128)], trecv.at[s],
            cs.at[s], cr.at[s], sibling, x, y, z,
        )
        copy.start()
        core_copies.append(copy)
        drain.append(copy.wait_send)

    half = pl.ds(pl.multiple_of(leaf * 128, 128), 128)
    for s in range(2):
        tcol[256 * s : 256 * s + 256, :] = jnp.broadcast_to(tg[0, s, 0:1, :], (128, 256)).T
        high, rest = split(tile_v[s, :, half].T)
        tt[0:128, 256 * s : 256 * s + 256] = high
        tt[128:256, 256 * s : 256 * s + 256] = rest
    tg_copy.wait_recv()
    for s in range(2):
        tcol[512 + 256 * s : 768 + 256 * s, :] = jnp.broadcast_to(tg[1, s, 0:1, :], (128, 256)).T
        core_copies[s].wait_recv()
        high, rest = split(trecv[s].T)
        tt[0:128, 512 + 256 * s : 768 + 256 * s] = high
        tt[128:256, 512 + 256 * s : 768 + 256 * s] = rest
    lane = lax.broadcasted_iota(jnp.int32, (1024, 128), 1)

    def contrib(start):
        rel = tcol[...] - start.astype(F32)
        lanes = lane.astype(F32)
        hot = jnp.concatenate(
            [jnp.where(rel == lanes, 1.0, 0.0), jnp.where(rel == lanes + 128.0, 1.0, 0.0)], axis=1
        ).astype(BF16)
        both = dot(tt[...], hot)
        return both[0:128] + both[128:256]

    def ax_copy(d):
        return remote(cbuf.at[d], axrecv.at[d - 1], axs.at[d], axr, leaf, (x + d) % NX, y, z)

    def by_copy(d, b):
        y2 = (y + d) % NY
        return remote(ybuf.at[y2, b], byrecv.at[d - 1, b], bys.at[d, b], byr, leaf, x, y2, z)

    def lower(d):
        cbuf[d] = contrib((x + d) % NX * 512)

    def upper(b, _):
        value = contrib(b * 512 + 256)
        for part in range(NY):
            ybuf[part, b] = value[
                part % 2 * 64 : part % 2 * 64 + 64, part // 2 * 128 : part // 2 * 128 + 128
            ]
        for d in (2, 1, 3):
            by_copy(d, b).start()
        return 0

    def lower_upper(i, _):
        d = (i * 2 + 1) % NX + i // 2
        lower(d)
        ax_copy(d).start()
        upper(i, 0)
        return 0

    lax.fori_loop(0, 3, lower_upper, 0)
    upper(jnp.int32(3), 0)
    drain += [ax_copy(d).wait_send for d in range(1, NX)]
    drain += [by_copy(d, b).wait_send for d in range(1, NY) for b in range(NX)]

    giver = (leaf == z % 2) & (z // 2 < x)
    for load in loads[6:]:
        load.wait()

    def ga_copy(d):
        y2 = (y + d) % NY
        return remote(gsrc.at[y2], grecv.at[z // 2, y], gas.at[d], gar, leaf, x, y2, z)

    @pl.when(giver)
    def _():
        low, _ = tril(td_v[...], 0, 0)
        fac = fac_v[...]
        gt = fac + dot3t(fac, low)
        for y2 in range(NY):
            gsrc[y2] = gt[:, 128 * y2 : 128 * y2 + 128]
        for d in range(1, NY):
            ga_copy(d).start()
        local(gsrc.at[y], grecv.at[z // 2, y], gar).start()

    def gb_copy(d):
        return remote(
            grecv.at[z // 2], grecv.at[z // 2], gs.at[d], gr.at[z // 2], leaf, x, y, (z + d) % NZ
        )

    def g_forward():
        @pl.when(giver)
        def _():
            arrived(grecv.at[z // 2], gar)
            for d in range(1, NZ):
                gb_copy(d).start()

    def g_drain():
        @pl.when(giver)
        def _():
            for d in range(1, NY):
                ga_copy(d).wait_send()
            for d in range(1, NZ):
                gb_copy(d).wait_send()

    drain.append(g_drain)

    row0, col0 = pl.multiple_of(y * 128, 128), pl.multiple_of(leaf * 256, 256)
    low, eye = tril(td_v[pl.ds(row0, 128), pl.ds(col0, 256)], row0, col0)
    tinv[0], tinv[1] = split((low + jnp.where(eye, 1.0, 0.0)).T)
    rhst[...] = trhs_v[pl.ds(col0, 256), :].T

    lower(0)

    arrived(byrecv, byr)

    def bx_copy(d):
        block = (x + d) % NX
        return remote(ysum.at[block], bxrecv.at[d - 1], bxs.at[d], bxr, leaf, block, y, z)

    def add_y(d):
        b = (x + d) % NX
        ysum[b] = ybuf[y, b] + byrecv[0, b] + byrecv[1, b] + byrecv[2, b]

    for d in (2, 1, 3):
        add_y(d)
        bx_copy(d).start()
        drain.append(bx_copy(d).wait_send)
    add_y(0)

    def az_copy(e):
        z2 = (z + e) % NZ
        return remote(azsrc.at[z2], azrecv.at[e - 1], azs.at[e], azr, leaf, x, y, z2)

    arrived(axrecv, axr)
    azsrc[...] = (cbuf[0] + axrecv[0] + axrecv[1] + axrecv[2]).reshape(NZ, 16, 256)
    for e in (4, 3, 5, 2, 6, 1, 7):
        az_copy(e).start()
        drain.append(az_copy(e).wait_send)

    keeper = z // 4 == y % 2

    def bz_copy(i):
        z2 = y % 2 * 4 + i
        return z2 != z, remote(bzsrc.at[i], bzrecv.at[z], bzs.at[i], bzr, leaf, x, y, z2)

    arrived(bxrecv, bxr)
    bzsrc[...] = (ysum[x] + bxrecv[0] + bxrecv[1] + bxrecv[2]).reshape(4, 16, 128)
    for i in range(4):
        away, copy = bz_copy(i)
        pl.when(away)(copy.start)

    def bz_drain():
        for i in range(4):
            away, copy = bz_copy(i)
            pl.when(away)(copy.wait_send)

    drain.append(bz_drain)
    pl.when(keeper)(local(bzsrc.at[z % 4], bzrecv.at[z], bzr).start)
    g_forward()

    def ay_copy(dy):
        return remote(aysrc, ayrecv.at[leaf, dy], ays.at[dy], ayr, 0, x, (y + dy) % NY, z)

    arrived(azrecv, azr)
    total = azsrc[z]
    for e in range(NZ - 1):
        total = total + azrecv[e]
    aysrc[...] = total
    for dy in (2, 1, 3):
        ay_copy(dy).start()
        drain.append(ay_copy(dy).wait_send)
    pl.when(leaf == 0)(local(aysrc, ayrecv.at[leaf, 0], ayr).start)
    pl.when(leaf == 1)(ay_copy(0).start)
    drain.append(lambda: pl.when(leaf == 1)(ay_copy(0).wait_send))

    def cy_copy(dy):
        return remote(cysrc, cyrecv.at[leaf, y // 2], cys.at[dy], cyr, 1, x, (y + dy) % NY, z)

    @pl.when(keeper)
    def _():
        arrived(bzrecv, bzr)
        total = bzrecv[0]
        for e in range(1, NZ):
            total = total + bzrecv[e]
        cysrc[...] = total
        for dy in (2, 1, 3):
            cy_copy(dy).start()
        pl.when(leaf == 1)(local(cysrc, cyrecv.at[leaf, y // 2], cyr).start)
        pl.when(leaf == 0)(cy_copy(0).start)

    def cy_drain():
        @pl.when(keeper)
        def _():
            for dy in range(1, NY):
                cy_copy(dy).wait_send()
            pl.when(leaf == 0)(cy_copy(0).wait_send)

    drain.append(cy_drain)

    @pl.when(leaf == 0)
    def _():
        arrived(ayrecv, ayr)
        for h in range(2):
            upd[h] = ayrecv[h, 0] + ayrecv[h, 1] + ayrecv[h, 2] + ayrecv[h, 3]

    @pl.when(leaf == 1)
    def _():
        arrived(cyrecv, cyr)
        for h in range(2):
            upd[h] = jnp.concatenate([cyrecv[h, 0], cyrecv[h, 1]], axis=1)

    reds = []
    for h in range(2):
        reds.append(rhst[pl.ds(pl.multiple_of(h * 128 + z * 16, 16), 16), :] - upd[h])
    acc = dot3p(jnp.concatenate(reds, axis=0), tinv[0], tinv[1])
    fsrc[...] = acc.reshape(2, 16, 128)

    def x_copy(k, x2, y2):
        return remote(
            fsrc, xrecv.at[k, leaf, y % 2], xs.at[x2, y2], xr.at[k], y // 2, x2, y2, z
        )

    for k in range(NX - 1):

        @pl.when(x == k)
        def _(k=k):
            for x2 in range(k + 1, NX):
                for y2 in range(NY):
                    x_copy(k, x2, y2).start()

        @pl.when(x > k)
        def _(k=k):
            @pl.when(z != 2 * k + leaf)
            def _():
                arrived(grecv.at[k], gr.at[k])

            high, rest = split(grecv[k].reshape(256, 128))
            gparts[k, 0] = high
            gparts[k, 1] = rest
            arrived(xrecv.at[k], xr.at[k])
            parts = (xrecv[k, 0] + xrecv[k, 1]).reshape(2, 32, 128)
            solved = jnp.concatenate([parts[0], parts[1]], axis=1)
            step = dot3p(solved, gparts[k, 0], gparts[k, 1])
            fsrc[...] = fsrc[...] - step.reshape(2, 16, 128)

        def x_drain(k=k):
            @pl.when(x == k)
            def _():
                for x2 in range(k + 1, NX):
                    for y2 in range(NY):
                        x_copy(k, x2, y2).wait_send()

        drain.append(x_drain)

    pair = remote(fsrc.at[sibling], frecv, fps, fpr, sibling, x, y, z)
    pair.start()
    drain.append(pair.wait_send)
    pair.wait_recv()
    fown[...] = fsrc[leaf] + frecv[...]

    def f1_copy(d):
        return remote(fown, fall.at[y, z], f1s.at[d], f1r.at[d], leaf, x, y, (z + d) % NZ)

    def f2_copy(d, dy):
        part = fall.at[y, (z + NZ - d) % NZ]
        return remote(part, part, f2s.at[d, dy], f2r.at[y], leaf, x, (y + dy) % NY, z)

    for d in (4, 3, 5, 2, 6, 1, 7):
        f1_copy(d).start()
        drain.append(f1_copy(d).wait_send)
    fall[y, z] = fown[...]
    for d in (0, 1, 7, 2, 6, 3, 5, 4):
        if d:
            arrived(fall.at[y, (z + NZ - d) % NZ], f1r.at[d])
        for dy in (2, 1, 3):
            f2_copy(d, dy).start()
            drain.append(f2_copy(d, dy).wait_send)

    def f3_copy(y2):
        part = outv.at[pl.ds(pl.multiple_of(y2 * 128, 128), 128), half]
        return remote(part, part, f3s.at[y2], f3r, sibling, x, y, z)

    for d in (0, 1, 3, 2):
        y2 = (y + d) % NY
        if d:
            arrived(fall.at[y2], f2r.at[y2])
        outv[pl.ds(pl.multiple_of(y2 * 128, 128), 128), half] = fall[y2].reshape(128, 128).T
        f3_copy(y2).start()
    drain += [f3_copy(y2).wait_send for y2 in range(NY)]
    arrived(outv.at[:, pl.ds(pl.multiple_of(sibling * 128, 128), 128)], f3r)
    finish()


def write_out(csol_v, top_v, csol_hbm, top_hbm, sem):
    copies = [pltpu.make_async_copy(csol_v.at[s], csol_hbm.at[s], sem.at[s]) for s in range(2)]
    copies += [
        pltpu.make_async_copy(
            top_v.at[256 * s : 256 * s + 256], top_hbm.at[256 * s : 256 * s + 256], sem.at[2 + s]
        )
        for s in range(2)
    ]
    for copy in copies:
        copy.start()
    for copy in copies:
        copy.wait()


def shards(child_rhs, child_diag, child_off, live, targets, top_rhs, top_factor, top_diag):
    any_ = pl.BlockSpec(memory_space=pl.ANY)
    vm = pltpu.VMEM
    dma = pltpu.SemaphoreType.DMA
    solved = pl.pallas_call(
        kernel,
        out_shape=(
            pltpu.VMEM(child_rhs.shape, F32),
            pltpu.VMEM(top_rhs.shape, F32),
        ),
        in_specs=[
            pl.BlockSpec(memory_space=pltpu.SMEM),
            pl.BlockSpec(memory_space=pltpu.VMEM),
        ] + [any_] * 6,
        out_specs=(pl.BlockSpec(memory_space=pltpu.VMEM),) * 2,
        scratch_shapes=[
            vm((2, 256, 256), F32), vm((2, 256, 256), F32), vm((2, 256, 256), F32),
            vm((2, 256, 256), F32),
            vm((512, 256), F32), vm((64, 512), F32), vm((512, 512), F32),
            vm((2, 2, 8, 256), F32), vm((2, 256, 128), F32), vm((1024, 128), F32), vm((256, 1024), BF16),
            vm((4, 128, 256), F32), vm((3, 128, 256), F32),
            vm((4, 4, 64, 128), F32), vm((3, 4, 64, 128), F32), vm((4, 64, 128), F32), vm((3, 64, 128), F32),
            vm((8, 16, 256), F32), vm((7, 16, 256), F32), vm((4, 16, 128), F32), vm((8, 16, 128), F32),
            vm((16, 256), F32), vm((2, 4, 16, 256), F32), vm((16, 128), F32), vm((2, 2, 16, 128), F32),
            vm((2, 16, 256), F32),
            vm((256, 256), F32), vm((2, 256, 128), BF16),
            vm((4, 64, 128), F32), vm((3, 4, 64, 128), F32), vm((3, 2, 256, 128), BF16),
            vm((2, 16, 128), F32), vm((3, 2, 2, 2, 16, 128), F32),
            vm((16, 128), F32), vm((16, 128), F32), vm((4, 8, 16, 128), F32),
            dma((6, 2)), dma, dma, dma((2,)), dma((2,)), dma((4,)), dma, dma((8,)), dma((4,)),
            dma((4,)), dma, dma((4, 4)), dma, dma((4,)), dma, dma((8,)), dma,
            dma((4,)), dma, dma((4,)), dma, dma((4,)), dma,
            dma((4, 4)), dma((3,)), dma, dma, dma((8,)), dma((8,)), dma((8, 4)), dma((4,)), dma((4,)), dma,
        ],
        compiler_params=pltpu.CompilerParams(collective_id=0, has_side_effects=True),
    )(live, targets, child_rhs, child_diag, child_off, top_rhs, top_factor.T, top_diag)
    return pl.pallas_call(
        write_out,
        out_shape=tuple(jax.ShapeDtypeStruct(a.shape, F32) for a in (child_rhs, top_rhs)),
        in_specs=[pl.BlockSpec(memory_space=pltpu.VMEM)] * 2,
        out_specs=(any_, any_),
        scratch_shapes=[dma((4,))],
    )(*(pltpu.with_memory_space_constraint(a, pltpu.VMEM) for a in solved))


def solution(mesh):
    parts = ("leaf", "row", "col")
    in_specs = (
        P(parts, None, None),
        P(parts, None, None),
        P(parts, None, None),
        P(parts),
        P(parts, None),
        P("row", None),
        P("row", "col"),
        P("row", None),
    )
    out_specs = (P(parts, None, None), P("row", None))
    return jax.shard_map(shards, mesh=mesh, in_specs=in_specs, out_specs=out_specs, check_vma=False)
```

```python
import jax
import jax.numpy as jnp
from jax import lax
from jax.experimental import pallas as pl
from jax.experimental.pallas import tpu as pltpu
from jax.sharding import PartitionSpec as P

MESH = pl.DeviceIdType.MESH
F32 = jnp.float32
BF16 = jnp.bfloat16
NX, NY, NZ = 4, 4, 8


def split(value):
    high = value.astype(BF16)
    return high, (value - high.astype(F32)).astype(BF16)


def dot(a, b):
    return jnp.dot(a, b, preferred_element_type=F32)


def dot3(a, b):
    ah, al = split(a)
    bh, bl = split(b)
    return dot(ah, bh) + (dot(ah, bl) + dot(al, bh))


def dot3p(a, bh, bl):
    n = a.shape[0]
    ah, al = split(a)
    both = dot(jnp.concatenate([ah, al], axis=0), bh)
    return both[:n] + (dot(ah, bl) + both[n:])


def dott(a, b):
    return lax.dot_general(a, b, (((1,), (1,)), ((), ())), preferred_element_type=F32)


def dot3t(a, b):
    ah, al = split(a)
    bh, bl = split(b)
    return dott(ah, bh) + (dott(ah, bl) + dott(al, bh))


def tril(value, row0, col0):
    rows = lax.broadcasted_iota(jnp.int32, value.shape, 0) + row0
    cols = lax.broadcasted_iota(jnp.int32, value.shape, 1) + col0
    return jnp.where(rows >= cols, value, 0.0), rows == cols


def kernel(
    live_ref, targ_ref, rhs_hbm, diag_hbm, off_hbm, trhs_hbm, fac_hbm, td_hbm,
    csol_v, outv,
    rhs_v, diag_v, off_v, tile_v, trhs_v, fac_v, td_v,
    tg, trecv, tcol, tt, cbuf, axrecv, ybuf, byrecv, ysum, bxrecv, azsrc, azrecv, bzsrc, bzrecv,
    aysrc, ayrecv, cysrc, cyrecv, upd,
    rhst, tinv, gsrc, grecv, gparts, fsrc, xrecv, frecv, fown, fall,
    near, load_sem, tgs, tgr, cs, cr, gas, gar, gs, gr, axs, axr, bys, byr, bxs, bxr, azs, azr,
    bzs, bzr, ays, ayr, cys, cyr, xs, xr, fps, fpr, f1s, f1r, f2s, f2r, f3s, f3r,
):
    leaf, x, col = lax.axis_index("leaf"), lax.axis_index("row"), lax.axis_index("col")
    y, z = col % NY, col // NY
    sibling = 1 - leaf

    def local(src, dst, sem):
        return pltpu.make_async_copy(src, dst, sem)

    def remote(src, dst, send, recv, l2, x2, y2, z2):
        return pltpu.make_async_remote_copy(
            src_ref=src, dst_ref=dst, send_sem=send, recv_sem=recv,
            device_id=(l2, x2, z2 * NY + y2), device_id_type=MESH,
        )

    def arrived(ref, sem):
        pltpu.make_async_copy(ref, ref, sem).wait()

    drain = []

    def finish():
        for wait in drain:
            wait()

    loads = [
        local(ref.at[s], buf.at[s], load_sem.at[i, s])
        for s in range(2)
        for i, (ref, buf) in enumerate(((diag_hbm, diag_v), (rhs_hbm, rhs_v), (off_hbm, off_v)))
    ] + [
        local(td_hbm, td_v, load_sem.at[3, 0]),
        local(fac_hbm, fac_v, load_sem.at[4, 0]),
        local(trhs_hbm, trhs_v, load_sem.at[5, 0]),
    ]
    for copy in loads:
        copy.start()

    barrier = pltpu.get_barrier_semaphore()

    def greet(l2, x2, y2, z2):
        pl.semaphore_signal(barrier, inc=1, device_id=(l2, x2, z2 * NY + y2), device_id_type=MESH)

    greet(sibling, x, y, z)
    for d in range(1, NX):
        greet(leaf, (x + d) % NX, y, z)
    for d in range(1, NY):
        greet(leaf, x, (y + d) % NY, z)
    for d in (1, NZ - 1):
        greet(leaf, x, y, (z + d) % NZ)

    lane = lax.broadcasted_iota(jnp.int32, (1, 256), 1)
    for s in range(2):
        row = jnp.where(lane < live_ref[s], targ_ref[s : s + 1, :], -1).astype(F32)
        tg[0, s, :, :] = jnp.broadcast_to(row, (8, 256))

    for s in range(2):
        loads[3 * s].wait()
        loads[3 * s + 1].wait()
        low, _ = tril(diag_v[s], 0, 0)
        sol = rhs_v[s] + dot3(low, rhs_v[s])
        csol_v[s] = sol
        loads[3 * s + 2].wait()
        tile_v[s] = dot3(off_v[s], sol)

    pl.semaphore_wait(barrier, 1 + NX - 1 + NY - 1 + 2)

    def spread(step):
        for d in (step, NZ - step):
            pl.semaphore_signal(
                near.at[step - 1], inc=1, device_id=(leaf, x, (z + d) % NZ * NY + y), device_id_type=MESH
            )

    spread(1)
    tg_copy = remote(tg.at[0], tg.at[1], tgs, tgr, sibling, x, y, z)
    tg_copy.start()
    drain.append(tg_copy.wait_send)
    core_copies = []
    for s in range(2):
        copy = remote(
            tile_v.at[s, :, pl.ds(pl.multiple_of(sibling * 128, 128), 128)], trecv.at[s],
            cs.at[s], cr.at[s], sibling, x, y, z,
        )
        copy.start()
        core_copies.append(copy)
        drain.append(copy.wait_send)

    half = pl.ds(pl.multiple_of(leaf * 128, 128), 128)
    for s in range(2):
        tcol[256 * s : 256 * s + 256, :] = jnp.broadcast_to(tg[0, s, 0:1, :], (128, 256)).T
        high, rest = split(tile_v[s, :, half].T)
        tt[0:128, 256 * s : 256 * s + 256] = high
        tt[128:256, 256 * s : 256 * s + 256] = rest
    tg_copy.wait_recv()
    for s in range(2):
        tcol[512 + 256 * s : 768 + 256 * s, :] = jnp.broadcast_to(tg[1, s, 0:1, :], (128, 256)).T
        core_copies[s].wait_recv()
        high, rest = split(trecv[s].T)
        tt[0:128, 512 + 256 * s : 768 + 256 * s] = high
        tt[128:256, 512 + 256 * s : 768 + 256 * s] = rest
    lane = lax.broadcasted_iota(jnp.int32, (1024, 128), 1)

    def contrib(start):
        rel = tcol[...] - start.astype(F32)
        lanes = lane.astype(F32)
        hot = jnp.concatenate(
            [jnp.where(rel == lanes, 1.0, 0.0), jnp.where(rel == lanes + 128.0, 1.0, 0.0)], axis=1
        ).astype(BF16)
        both = dot(tt[...], hot)
        return both[0:128] + both[128:256]

    def ax_copy(d):
        return remote(cbuf.at[d], axrecv.at[d - 1], axs.at[d], axr, leaf, (x + d) % NX, y, z)

    def by_copy(d, b):
        y2 = (y + d) % NY
        return remote(ybuf.at[y2, b], byrecv.at[d - 1, b], bys.at[d, b], byr, leaf, x, y2, z)

    def lower(d):
        cbuf[d] = contrib((x + d) % NX * 512)

    def upper(b, _):
        value = contrib(b * 512 + 256)
        for part in range(NY):
            ybuf[part, b] = value[
                part % 2 * 64 : part % 2 * 64 + 64, part // 2 * 128 : part // 2 * 128 + 128
            ]
        for d in (2, 1, 3):
            by_copy(d, b).start()
        return 0

    def lower_upper(i, _):
        d = (i * 2 + 1) % NX + i // 2
        lower(d)
        ax_copy(d).start()
        upper(i, 0)
        return 0

    lax.fori_loop(0, 3, lower_upper, 0)
    upper(jnp.int32(3), 0)
    pl.semaphore_wait(near.at[0], 2)
    spread(2)
    drain += [ax_copy(d).wait_send for d in range(1, NX)]
    drain += [by_copy(d, b).wait_send for d in range(1, NY) for b in range(NX)]

    giver = (leaf == z % 2) & (z // 2 < x)
    for load in loads[6:]:
        load.wait()

    def ga_copy(d):
        y2 = (y + d) % NY
        return remote(gsrc.at[y2], grecv.at[z // 2, y], gas.at[d], gar, leaf, x, y2, z)

    @pl.when(giver)
    def _():
        low, _ = tril(td_v[...], 0, 0)
        fac = fac_v[...]
        gt = fac + dot3t(fac, low)
        for y2 in range(NY):
            gsrc[y2] = gt[:, 128 * y2 : 128 * y2 + 128]
        for d in range(1, NY):
            ga_copy(d).start()
        local(gsrc.at[y], grecv.at[z // 2, y], gar).start()

    def gb_copy(d):
        return remote(
            grecv.at[z // 2], grecv.at[z // 2], gs.at[d], gr.at[z // 2], leaf, x, y, (z + d) % NZ
        )

    def g_forward():
        @pl.when(giver)
        def _():
            arrived(grecv.at[z // 2], gar)
            for d in range(1, NZ):
                gb_copy(d).start()

    def g_drain():
        @pl.when(giver)
        def _():
            for d in range(1, NY):
                ga_copy(d).wait_send()
            for d in range(1, NZ):
                gb_copy(d).wait_send()

    drain.append(g_drain)

    row0, col0 = pl.multiple_of(y * 128, 128), pl.multiple_of(leaf * 256, 256)
    low, eye = tril(td_v[pl.ds(row0, 128), pl.ds(col0, 256)], row0, col0)
    tinv[0], tinv[1] = split((low + jnp.where(eye, 1.0, 0.0)).T)
    rhst[...] = trhs_v[pl.ds(col0, 256), :].T

    lower(0)
    pl.semaphore_wait(near.at[1], 2)

    arrived(byrecv, byr)

    def bx_copy(d):
        block = (x + d) % NX
        return remote(ysum.at[block], bxrecv.at[d - 1], bxs.at[d], bxr, leaf, block, y, z)

    def add_y(d):
        b = (x + d) % NX
        ysum[b] = ybuf[y, b] + byrecv[0, b] + byrecv[1, b] + byrecv[2, b]

    for d in (2, 1, 3):
        add_y(d)
        bx_copy(d).start()
        drain.append(bx_copy(d).wait_send)
    add_y(0)

    def az_copy(e):
        z2 = (z + e) % NZ
        return remote(azsrc.at[z2], azrecv.at[e - 1], azs.at[e], azr, leaf, x, y, z2)

    arrived(axrecv, axr)
    azsrc[...] = (cbuf[0] + axrecv[0] + axrecv[1] + axrecv[2]).reshape(NZ, 16, 256)
    for e in (4, 3, 5, 2, 6, 1, 7):
        az_copy(e).start()
        drain.append(az_copy(e).wait_send)

    keeper = z // 4 == y % 2

    def bz_copy(i):
        z2 = y % 2 * 4 + i
        return z2 != z, remote(bzsrc.at[i], bzrecv.at[z], bzs.at[i], bzr, leaf, x, y, z2)

    arrived(bxrecv, bxr)
    bzsrc[...] = (ysum[x] + bxrecv[0] + bxrecv[1] + bxrecv[2]).reshape(4, 16, 128)
    for i in range(4):
        away, copy = bz_copy(i)
        pl.when(away)(copy.start)

    def bz_drain():
        for i in range(4):
            away, copy = bz_copy(i)
            pl.when(away)(copy.wait_send)

    drain.append(bz_drain)
    pl.when(keeper)(local(bzsrc.at[z % 4], bzrecv.at[z], bzr).start)
    g_forward()

    def ay_copy(dy):
        return remote(aysrc, ayrecv.at[leaf, dy], ays.at[dy], ayr, 0, x, (y + dy) % NY, z)

    arrived(azrecv, azr)
    total = azsrc[z]
    for e in range(NZ - 1):
        total = total + azrecv[e]
    aysrc[...] = total
    for dy in (2, 1, 3):
        ay_copy(dy).start()
        drain.append(ay_copy(dy).wait_send)
    pl.when(leaf == 0)(local(aysrc, ayrecv.at[leaf, 0], ayr).start)
    pl.when(leaf == 1)(ay_copy(0).start)
    drain.append(lambda: pl.when(leaf == 1)(ay_copy(0).wait_send))

    def cy_copy(dy):
        return remote(cysrc, cyrecv.at[leaf, y // 2], cys.at[dy], cyr, 1, x, (y + dy) % NY, z)

    @pl.when(keeper)
    def _():
        arrived(bzrecv, bzr)
        total = bzrecv[0]
        for e in range(1, NZ):
            total = total + bzrecv[e]
        cysrc[...] = total
        for dy in (2, 1, 3):
            cy_copy(dy).start()
        pl.when(leaf == 1)(local(cysrc, cyrecv.at[leaf, y // 2], cyr).start)
        pl.when(leaf == 0)(cy_copy(0).start)

    def cy_drain():
        @pl.when(keeper)
        def _():
            for dy in range(1, NY):
                cy_copy(dy).wait_send()
            pl.when(leaf == 0)(cy_copy(0).wait_send)

    drain.append(cy_drain)

    @pl.when(leaf == 0)
    def _():
        arrived(ayrecv, ayr)
        for h in range(2):
            upd[h] = ayrecv[h, 0] + ayrecv[h, 1] + ayrecv[h, 2] + ayrecv[h, 3]

    @pl.when(leaf == 1)
    def _():
        arrived(cyrecv, cyr)
        for h in range(2):
            upd[h] = jnp.concatenate([cyrecv[h, 0], cyrecv[h, 1]], axis=1)

    reds = []
    for h in range(2):
        reds.append(rhst[pl.ds(pl.multiple_of(h * 128 + z * 16, 16), 16), :] - upd[h])
    acc = dot3p(jnp.concatenate(reds, axis=0), tinv[0], tinv[1])
    fsrc[...] = acc.reshape(2, 16, 128)

    def x_copy(k, x2, y2):
        return remote(
            fsrc, xrecv.at[k, leaf, y % 2], xs.at[x2, y2], xr.at[k], y // 2, x2, y2, z
        )

    for k in range(NX - 1):

        @pl.when(x == k)
        def _(k=k):
            for x2 in range(k + 1, NX):
                for y2 in range(NY):
                    x_copy(k, x2, y2).start()

        @pl.when(x > k)
        def _(k=k):
            @pl.when(z != 2 * k + leaf)
            def _():
                arrived(grecv.at[k], gr.at[k])

            high, rest = split(grecv[k].reshape(256, 128))
            gparts[k, 0] = high
            gparts[k, 1] = rest
            arrived(xrecv.at[k], xr.at[k])
            parts = (xrecv[k, 0] + xrecv[k, 1]).reshape(2, 32, 128)
            solved = jnp.concatenate([parts[0], parts[1]], axis=1)
            step = dot3p(solved, gparts[k, 0], gparts[k, 1])
            fsrc[...] = fsrc[...] - step.reshape(2, 16, 128)

        def x_drain(k=k):
            @pl.when(x == k)
            def _():
                for x2 in range(k + 1, NX):
                    for y2 in range(NY):
                        x_copy(k, x2, y2).wait_send()

        drain.append(x_drain)

    pair = remote(fsrc.at[sibling], frecv, fps, fpr, sibling, x, y, z)
    pair.start()
    drain.append(pair.wait_send)
    pair.wait_recv()
    fown[...] = fsrc[leaf] + frecv[...]

    def f1_copy(d):
        return remote(fown, fall.at[y, z], f1s.at[d], f1r.at[d], leaf, x, y, (z + d) % NZ)

    def f2_copy(d, dy):
        part = fall.at[y, (z + NZ - d) % NZ]
        return remote(part, part, f2s.at[d, dy], f2r.at[y], leaf, x, (y + dy) % NY, z)

    for d in (4, 3, 5, 2, 6, 1, 7):
        f1_copy(d).start()
        drain.append(f1_copy(d).wait_send)
    fall[y, z] = fown[...]
    for d in (0, 1, 7, 2, 6, 3, 5, 4):
        if d:
            arrived(fall.at[y, (z + NZ - d) % NZ], f1r.at[d])
        for dy in (2, 1, 3):
            f2_copy(d, dy).start()
            drain.append(f2_copy(d, dy).wait_send)

    def f3_copy(y2):
        part = outv.at[pl.ds(pl.multiple_of(y2 * 128, 128), 128), half]
        return remote(part, part, f3s.at[y2], f3r, sibling, x, y, z)

    for d in (0, 1, 3, 2):
        y2 = (y + d) % NY
        if d:
            arrived(fall.at[y2], f2r.at[y2])
        outv[pl.ds(pl.multiple_of(y2 * 128, 128), 128), half] = fall[y2].reshape(128, 128).T
        f3_copy(y2).start()
    drain += [f3_copy(y2).wait_send for y2 in range(NY)]
    arrived(outv.at[:, pl.ds(pl.multiple_of(sibling * 128, 128), 128)], f3r)
    finish()


def write_out(csol_v, top_v, csol_hbm, top_hbm, sem):
    copies = [pltpu.make_async_copy(csol_v.at[s], csol_hbm.at[s], sem.at[s]) for s in range(2)]
    copies += [
        pltpu.make_async_copy(
            top_v.at[256 * s : 256 * s + 256], top_hbm.at[256 * s : 256 * s + 256], sem.at[2 + s]
        )
        for s in range(2)
    ]
    for copy in copies:
        copy.start()
    for copy in copies:
        copy.wait()


def shards(child_rhs, child_diag, child_off, live, targets, top_rhs, top_factor, top_diag):
    any_ = pl.BlockSpec(memory_space=pl.ANY)
    vm = pltpu.VMEM
    dma = pltpu.SemaphoreType.DMA
    solved = pl.pallas_call(
        kernel,
        out_shape=(
            pltpu.VMEM(child_rhs.shape, F32),
            pltpu.VMEM(top_rhs.shape, F32),
        ),
        in_specs=[
            pl.BlockSpec(memory_space=pltpu.SMEM),
            pl.BlockSpec(memory_space=pltpu.VMEM),
        ] + [any_] * 6,
        out_specs=(pl.BlockSpec(memory_space=pltpu.VMEM),) * 2,
        scratch_shapes=[
            vm((2, 256, 256), F32), vm((2, 256, 256), F32), vm((2, 256, 256), F32),
            vm((2, 256, 256), F32),
            vm((512, 256), F32), vm((64, 512), F32), vm((512, 512), F32),
            vm((2, 2, 8, 256), F32), vm((2, 256, 128), F32), vm((1024, 128), F32), vm((256, 1024), BF16),
            vm((4, 128, 256), F32), vm((3, 128, 256), F32),
            vm((4, 4, 64, 128), F32), vm((3, 4, 64, 128), F32), vm((4, 64, 128), F32), vm((3, 64, 128), F32),
            vm((8, 16, 256), F32), vm((7, 16, 256), F32), vm((4, 16, 128), F32), vm((8, 16, 128), F32),
            vm((16, 256), F32), vm((2, 4, 16, 256), F32), vm((16, 128), F32), vm((2, 2, 16, 128), F32),
            vm((2, 16, 256), F32),
            vm((256, 256), F32), vm((2, 256, 128), BF16),
            vm((4, 64, 128), F32), vm((3, 4, 64, 128), F32), vm((3, 2, 256, 128), BF16),
            vm((2, 16, 128), F32), vm((3, 2, 2, 2, 16, 128), F32),
            vm((16, 128), F32), vm((16, 128), F32), vm((4, 8, 16, 128), F32),
            pltpu.SemaphoreType.REGULAR((2,)),
            dma((6, 2)), dma, dma, dma((2,)), dma((2,)), dma((4,)), dma, dma((8,)), dma((4,)),
            dma((4,)), dma, dma((4, 4)), dma, dma((4,)), dma, dma((8,)), dma,
            dma((4,)), dma, dma((4,)), dma, dma((4,)), dma,
            dma((4, 4)), dma((3,)), dma, dma, dma((8,)), dma((8,)), dma((8, 4)), dma((4,)), dma((4,)), dma,
        ],
        compiler_params=pltpu.CompilerParams(collective_id=0, has_side_effects=True),
    )(live, targets, child_rhs, child_diag, child_off, top_rhs, top_factor.T, top_diag)
    return pl.pallas_call(
        write_out,
        out_shape=tuple(jax.ShapeDtypeStruct(a.shape, F32) for a in (child_rhs, top_rhs)),
        in_specs=[pl.BlockSpec(memory_space=pltpu.VMEM)] * 2,
        out_specs=(any_, any_),
        scratch_shapes=[dma((4,))],
    )(*(pltpu.with_memory_space_constraint(a, pltpu.VMEM) for a in solved))


def solution(mesh):
    parts = ("leaf", "row", "col")
    in_specs = (
        P(parts, None, None),
        P(parts, None, None),
        P(parts, None, None),
        P(parts),
        P(parts, None),
        P("row", None),
        P("row", "col"),
        P("row", None),
    )
    out_specs = (P(parts, None, None), P("row", None))
    return jax.shard_map(shards, mesh=mesh, in_specs=in_specs, out_specs=out_specs, check_vma=False)
```

```python
import jax
import jax.numpy as jnp
from jax import lax
from jax.experimental import pallas as pl
from jax.experimental.pallas import tpu as pltpu
from jax.sharding import PartitionSpec as P

MESH = pl.DeviceIdType.MESH
F32 = jnp.float32
BF16 = jnp.bfloat16
NX, NY, NZ = 4, 4, 8


def split(value):
    high = value.astype(BF16)
    return high, (value - high.astype(F32)).astype(BF16)


def dot(a, b):
    return jnp.dot(a, b, preferred_element_type=F32)


def dot3(a, b):
    ah, al = split(a)
    bh, bl = split(b)
    return dot(ah, bh) + (dot(ah, bl) + dot(al, bh))


def dot3p(a, bh, bl):
    n = a.shape[0]
    ah, al = split(a)
    both = dot(jnp.concatenate([ah, al], axis=0), bh)
    return both[:n] + (dot(ah, bl) + both[n:])


def dott(a, b):
    return lax.dot_general(a, b, (((1,), (1,)), ((), ())), preferred_element_type=F32)


def dot3t(a, b):
    ah, al = split(a)
    bh, bl = split(b)
    return dott(ah, bh) + (dott(ah, bl) + dott(al, bh))


def tril(value, row0, col0):
    rows = lax.broadcasted_iota(jnp.int32, value.shape, 0) + row0
    cols = lax.broadcasted_iota(jnp.int32, value.shape, 1) + col0
    return jnp.where(rows >= cols, value, 0.0), rows == cols


def kernel(
    live_ref, targ_ref, rhs_hbm, diag_hbm, off_hbm, trhs_hbm, fac_hbm, td_hbm,
    csol_v, outv,
    rhs_v, diag_v, off_v, tile_v, trhs_v, fac_v, td_v,
    tg, trecv, tcol, tt, cbuf, axrecv, ybuf, byrecv, ysum, bxrecv, azsrc, azrecv, bzsrc, bzrecv,
    aysrc, ayrecv, cysrc, cyrecv, upd,
    rhst, tinv, gsrc, grecv, gparts, fsrc, xrecv, frecv, fown, fall,
    near, load_sem, tgs, tgr, cs, cr, gas, gar, gs, gr, axs, axr, bys, byr, bxs, bxr, azs, azr,
    bzs, bzr, ays, ayr, cys, cyr, xs, xr, fps, fpr, f1s, f1r, f2s, f2r, f3s, f3r,
):
    leaf, x, col = lax.axis_index("leaf"), lax.axis_index("row"), lax.axis_index("col")
    y, z = col % NY, col // NY
    sibling = 1 - leaf

    def local(src, dst, sem):
        return pltpu.make_async_copy(src, dst, sem)

    def remote(src, dst, send, recv, l2, x2, y2, z2):
        return pltpu.make_async_remote_copy(
            src_ref=src, dst_ref=dst, send_sem=send, recv_sem=recv,
            device_id=(l2, x2, z2 * NY + y2), device_id_type=MESH,
        )

    def arrived(ref, sem):
        pltpu.make_async_copy(ref, ref, sem).wait()

    drain = []

    def finish():
        for wait in drain:
            wait()

    loads = [
        local(ref.at[s], buf.at[s], load_sem.at[i, s])
        for s in range(2)
        for i, (ref, buf) in enumerate(((diag_hbm, diag_v), (rhs_hbm, rhs_v), (off_hbm, off_v)))
    ] + [
        local(td_hbm, td_v, load_sem.at[3, 0]),
        local(fac_hbm, fac_v, load_sem.at[4, 0]),
        local(trhs_hbm, trhs_v, load_sem.at[5, 0]),
    ]
    for copy in loads:
        copy.start()

    barrier = pltpu.get_barrier_semaphore()

    def greet(l2, x2, y2, z2):
        pl.semaphore_signal(barrier, inc=1, device_id=(l2, x2, z2 * NY + y2), device_id_type=MESH)

    greet(sibling, x, y, z)
    for d in range(1, NX):
        greet(leaf, (x + d) % NX, y, z)
    for d in range(1, NY):
        greet(leaf, x, (y + d) % NY, z)
    for d in (1, NZ - 1):
        greet(leaf, x, y, (z + d) % NZ)

    lane = lax.broadcasted_iota(jnp.int32, (1, 256), 1)
    for s in range(2):
        row = jnp.where(lane < live_ref[s], targ_ref[s : s + 1, :], -1).astype(F32)
        tg[0, s, :, :] = jnp.broadcast_to(row, (8, 256))

    for s in range(2):
        loads[3 * s].wait()
        loads[3 * s + 1].wait()
        low, _ = tril(diag_v[s], 0, 0)
        sol = rhs_v[s] + dot3(low, rhs_v[s])
        csol_v[s] = sol
        loads[3 * s + 2].wait()
        tile_v[s] = dot3(off_v[s], sol)

    pl.semaphore_wait(barrier, 1 + NX - 1 + NY - 1 + 2)

    def spread(step):
        for d in (step, NZ - step):
            pl.semaphore_signal(
                near.at[step - 1], inc=1, device_id=(leaf, x, (z + d) % NZ * NY + y), device_id_type=MESH
            )

    spread(1)
    tg_copy = remote(tg.at[0], tg.at[1], tgs, tgr, sibling, x, y, z)
    tg_copy.start()
    drain.append(tg_copy.wait_send)
    core_copies = []
    for s in range(2):
        copy = remote(
            tile_v.at[s, :, pl.ds(pl.multiple_of(sibling * 128, 128), 128)], trecv.at[s],
            cs.at[s], cr.at[s], sibling, x, y, z,
        )
        copy.start()
        core_copies.append(copy)
        drain.append(copy.wait_send)

    half = pl.ds(pl.multiple_of(leaf * 128, 128), 128)
    for s in range(2):
        tcol[256 * s : 256 * s + 256, :] = jnp.broadcast_to(tg[0, s, 0:1, :], (128, 256)).T
        high, rest = split(tile_v[s, :, half].T)
        tt[0:128, 256 * s : 256 * s + 256] = high
        tt[128:256, 256 * s : 256 * s + 256] = rest
    tg_copy.wait_recv()
    for s in range(2):
        tcol[512 + 256 * s : 768 + 256 * s, :] = jnp.broadcast_to(tg[1, s, 0:1, :], (128, 256)).T
        core_copies[s].wait_recv()
        high, rest = split(trecv[s].T)
        tt[0:128, 512 + 256 * s : 768 + 256 * s] = high
        tt[128:256, 512 + 256 * s : 768 + 256 * s] = rest
    lane = lax.broadcasted_iota(jnp.int32, (1024, 128), 1)

    def contrib(start):
        rel = tcol[...] - start.astype(F32)
        lanes = lane.astype(F32)
        hot = jnp.concatenate(
            [jnp.where(rel == lanes, 1.0, 0.0), jnp.where(rel == lanes + 128.0, 1.0, 0.0)], axis=1
        ).astype(BF16)
        both = dot(tt[...], hot)
        return both[0:128] + both[128:256]

    def ax_copy(d):
        return remote(cbuf.at[d], axrecv.at[d - 1], axs.at[d], axr, leaf, (x + d) % NX, y, z)

    def by_copy(d, b):
        y2 = (y + d) % NY
        return remote(ybuf.at[y2, b], byrecv.at[d - 1, b], bys.at[d, b], byr, leaf, x, y2, z)

    def lower(d):
        cbuf[d] = contrib((x + d) % NX * 512)

    def upper(b, _):
        value = contrib(b * 512 + 256)
        for part in range(NY):
            ybuf[part, b] = value[
                part % 2 * 64 : part % 2 * 64 + 64, part // 2 * 128 : part // 2 * 128 + 128
            ]
        for d in (2, 1, 3):
            by_copy(d, b).start()
        return 0

    def lower_upper(i, _):
        d = (i * 2 + 1) % NX + i // 2
        lower(d)
        ax_copy(d).start()
        upper(i, 0)
        return 0

    lax.fori_loop(0, 3, lower_upper, 0)
    upper(jnp.int32(3), 0)
    pl.semaphore_wait(near.at[0], 2)
    spread(2)
    drain += [ax_copy(d).wait_send for d in range(1, NX)]
    drain += [by_copy(d, b).wait_send for d in range(1, NY) for b in range(NX)]

    giver = (leaf == z % 2) & (z // 2 < x)
    for load in loads[6:]:
        load.wait()

    def ga_copy(d):
        y2 = (y + d) % NY
        return remote(gsrc.at[y2], grecv.at[z // 2, y], gas.at[d], gar, leaf, x, y2, z)

    @pl.when(giver)
    def _():
        low, _ = tril(td_v[...], 0, 0)
        fac = fac_v[...]
        gt = fac + dot3t(fac, low)
        for y2 in range(NY):
            gsrc[y2] = gt[:, 128 * y2 : 128 * y2 + 128]
        for d in range(1, NY):
            ga_copy(d).start()
        local(gsrc.at[y], grecv.at[z // 2, y], gar).start()

    def gb_copy(d):
        return remote(
            grecv.at[z // 2], grecv.at[z // 2], gs.at[d], gr.at[z // 2], leaf, x, y, (z + d) % NZ
        )

    def g_forward():
        @pl.when(giver)
        def _():
            arrived(grecv.at[z // 2], gar)
            for d in range(1, NZ):
                gb_copy(d).start()

    def g_drain():
        @pl.when(giver)
        def _():
            for d in range(1, NY):
                ga_copy(d).wait_send()
            for d in range(1, NZ):
                gb_copy(d).wait_send()

    drain.append(g_drain)

    row0, col0 = pl.multiple_of(y * 128, 128), pl.multiple_of(leaf * 256, 256)
    low, eye = tril(td_v[pl.ds(row0, 128), pl.ds(col0, 256)], row0, col0)
    tinv[0], tinv[1] = split((low + jnp.where(eye, 1.0, 0.0)).T)
    rhst[...] = trhs_v[pl.ds(col0, 256), :].T

    lower(0)
    pl.semaphore_wait(near.at[1], 2)

    arrived(byrecv, byr)

    def bx_copy(d):
        block = (x + d) % NX
        return remote(ysum.at[block], bxrecv.at[d - 1], bxs.at[d], bxr, leaf, block, y, z)

    def add_y(d):
        b = (x + d) % NX
        ysum[b] = ybuf[y, b] + byrecv[0, b] + byrecv[1, b] + byrecv[2, b]

    for d in (2, 1, 3):
        add_y(d)
        bx_copy(d).start()
        drain.append(bx_copy(d).wait_send)
    add_y(0)

    def az_copy(e):
        z2 = (z + e) % NZ
        return remote(azsrc.at[z2], azrecv.at[e - 1], azs.at[e], azr, leaf, x, y, z2)

    arrived(axrecv, axr)
    azsrc[...] = (cbuf[0] + axrecv[0] + axrecv[1] + axrecv[2]).reshape(NZ, 16, 256)
    for e in (4, 3, 5, 2, 6, 1, 7):
        az_copy(e).start()
        drain.append(az_copy(e).wait_send)

    keeper = z // 4 == y % 2

    def bz_copy(i):
        z2 = y % 2 * 4 + i
        return z2 != z, remote(bzsrc.at[i], bzrecv.at[z], bzs.at[i], bzr, leaf, x, y, z2)

    arrived(bxrecv, bxr)
    bzsrc[...] = (ysum[x] + bxrecv[0] + bxrecv[1] + bxrecv[2]).reshape(4, 16, 128)
    for i in range(4):
        away, copy = bz_copy(i)
        pl.when(away)(copy.start)

    def bz_drain():
        for i in range(4):
            away, copy = bz_copy(i)
            pl.when(away)(copy.wait_send)

    drain.append(bz_drain)
    pl.when(keeper)(local(bzsrc.at[z % 4], bzrecv.at[z], bzr).start)
    g_forward()

    def ay_copy(dy):
        return remote(aysrc, ayrecv.at[leaf, dy], ays.at[dy], ayr, 0, x, (y + dy) % NY, z)

    arrived(azrecv, azr)
    total = azsrc[z]
    for e in range(NZ - 1):
        total = total + azrecv[e]
    aysrc[...] = total
    for dy in (2, 1, 3):
        ay_copy(dy).start()
        drain.append(ay_copy(dy).wait_send)
    pl.when(leaf == 0)(local(aysrc, ayrecv.at[leaf, 0], ayr).start)
    pl.when(leaf == 1)(ay_copy(0).start)
    drain.append(lambda: pl.when(leaf == 1)(ay_copy(0).wait_send))

    def cy_copy(dy):
        return remote(cysrc, cyrecv.at[leaf, y // 2], cys.at[dy], cyr, 1, x, (y + dy) % NY, z)

    @pl.when(keeper)
    def _():
        arrived(bzrecv, bzr)
        total = bzrecv[0]
        for e in range(1, NZ):
            total = total + bzrecv[e]
        cysrc[...] = total
        for dy in (2, 1, 3):
            cy_copy(dy).start()
        pl.when(leaf == 1)(local(cysrc, cyrecv.at[leaf, y // 2], cyr).start)
        pl.when(leaf == 0)(cy_copy(0).start)

    def cy_drain():
        @pl.when(keeper)
        def _():
            for dy in range(1, NY):
                cy_copy(dy).wait_send()
            pl.when(leaf == 0)(cy_copy(0).wait_send)

    drain.append(cy_drain)

    @pl.when(leaf == 0)
    def _():
        arrived(ayrecv, ayr)
        for h in range(2):
            upd[h] = ayrecv[h, 0] + ayrecv[h, 1] + ayrecv[h, 2] + ayrecv[h, 3]

    @pl.when(leaf == 1)
    def _():
        arrived(cyrecv, cyr)
        for h in range(2):
            upd[h] = jnp.concatenate([cyrecv[h, 0], cyrecv[h, 1]], axis=1)

    reds = []
    for h in range(2):
        reds.append(rhst[pl.ds(pl.multiple_of(h * 128 + z * 16, 16), 16), :] - upd[h])
    acc = dot3p(jnp.concatenate(reds, axis=0), tinv[0], tinv[1])
    fsrc[...] = acc.reshape(2, 16, 128)

    def x_copy(k, x2, y2):
        return remote(
            fsrc, xrecv.at[k, leaf, y % 2], xs.at[x2, y2], xr.at[k], y // 2, x2, y2, z
        )

    for k in range(NX - 1):

        @pl.when(x == k)
        def _(k=k):
            for x2 in range(k + 1, NX):
                for y2 in range(NY):
                    x_copy(k, x2, y2).start()

        @pl.when(x > k)
        def _(k=k):
            @pl.when(z != 2 * k + leaf)
            def _():
                arrived(grecv.at[k], gr.at[k])

            high, rest = split(grecv[k].reshape(256, 128))
            gparts[k, 0] = high
            gparts[k, 1] = rest
            arrived(xrecv.at[k], xr.at[k])
            parts = (xrecv[k, 0] + xrecv[k, 1]).reshape(2, 32, 128)
            solved = jnp.concatenate([parts[0], parts[1]], axis=1)
            step = dot3p(solved, gparts[k, 0], gparts[k, 1])
            fsrc[...] = fsrc[...] - step.reshape(2, 16, 128)

        def x_drain(k=k):
            @pl.when(x == k)
            def _():
                for x2 in range(k + 1, NX):
                    for y2 in range(NY):
                        x_copy(k, x2, y2).wait_send()

        drain.append(x_drain)

    pair = remote(fsrc.at[sibling], frecv, fps, fpr, sibling, x, y, z)
    pair.start()
    drain.append(pair.wait_send)
    pair.wait_recv()
    fown[...] = fsrc[leaf] + frecv[...]

    late = []

    def f1_copy(d):
        return remote(fown, fall.at[y, z], f1s.at[d], f1r.at[d], leaf, x, y, (z + d) % NZ)

    def f2_copy(d, dy):
        part = fall.at[y, (z + NZ - d) % NZ]
        return remote(part, part, f2s.at[d, dy], f2r.at[y], leaf, x, (y + dy) % NY, z)

    for d in (4, 3, 5, 2, 6, 1, 7):
        f1_copy(d).start()
        late.append(f1_copy(d).wait_send)
    fall[y, z] = fown[...]
    for d in (0, 1, 7, 2, 6, 3, 5, 4):
        if d:
            arrived(fall.at[y, (z + NZ - d) % NZ], f1r.at[d])
        for dy in (2, 1, 3):
            f2_copy(d, dy).start()
            late.append(f2_copy(d, dy).wait_send)
        if d == 0:
            finish()

    def f3_copy(y2):
        part = outv.at[pl.ds(pl.multiple_of(y2 * 128, 128), 128), half]
        return remote(part, part, f3s.at[y2], f3r, sibling, x, y, z)

    for d in (0, 1, 3, 2):
        y2 = (y + d) % NY
        if d:
            arrived(fall.at[y2], f2r.at[y2])
        outv[pl.ds(pl.multiple_of(y2 * 128, 128), 128), half] = fall[y2].reshape(128, 128).T
        f3_copy(y2).start()
    for wait in late:
        wait()
    arrived(outv.at[:, pl.ds(pl.multiple_of(sibling * 128, 128), 128)], f3r)
    for y2 in range(NY):
        f3_copy(y2).wait_send()


def write_out(csol_v, top_v, csol_hbm, top_hbm, sem):
    copies = [pltpu.make_async_copy(csol_v.at[s], csol_hbm.at[s], sem.at[s]) for s in range(2)]
    copies += [
        pltpu.make_async_copy(
            top_v.at[256 * s : 256 * s + 256], top_hbm.at[256 * s : 256 * s + 256], sem.at[2 + s]
        )
        for s in range(2)
    ]
    for copy in copies:
        copy.start()
    for copy in copies:
        copy.wait()


def shards(child_rhs, child_diag, child_off, live, targets, top_rhs, top_factor, top_diag):
    any_ = pl.BlockSpec(memory_space=pl.ANY)
    vm = pltpu.VMEM
    dma = pltpu.SemaphoreType.DMA
    solved = pl.pallas_call(
        kernel,
        out_shape=(
            pltpu.VMEM(child_rhs.shape, F32),
            pltpu.VMEM(top_rhs.shape, F32),
        ),
        in_specs=[
            pl.BlockSpec(memory_space=pltpu.SMEM),
            pl.BlockSpec(memory_space=pltpu.VMEM),
        ] + [any_] * 6,
        out_specs=(pl.BlockSpec(memory_space=pltpu.VMEM),) * 2,
        scratch_shapes=[
            vm((2, 256, 256), F32), vm((2, 256, 256), F32), vm((2, 256, 256), F32),
            vm((2, 256, 256), F32),
            vm((512, 256), F32), vm((64, 512), F32), vm((512, 512), F32),
            vm((2, 2, 8, 256), F32), vm((2, 256, 128), F32), vm((1024, 128), F32), vm((256, 1024), BF16),
            vm((4, 128, 256), F32), vm((3, 128, 256), F32),
            vm((4, 4, 64, 128), F32), vm((3, 4, 64, 128), F32), vm((4, 64, 128), F32), vm((3, 64, 128), F32),
            vm((8, 16, 256), F32), vm((7, 16, 256), F32), vm((4, 16, 128), F32), vm((8, 16, 128), F32),
            vm((16, 256), F32), vm((2, 4, 16, 256), F32), vm((16, 128), F32), vm((2, 2, 16, 128), F32),
            vm((2, 16, 256), F32),
            vm((256, 256), F32), vm((2, 256, 128), BF16),
            vm((4, 64, 128), F32), vm((3, 4, 64, 128), F32), vm((3, 2, 256, 128), BF16),
            vm((2, 16, 128), F32), vm((3, 2, 2, 2, 16, 128), F32),
            vm((16, 128), F32), vm((16, 128), F32), vm((4, 8, 16, 128), F32),
            pltpu.SemaphoreType.REGULAR((2,)),
            dma((6, 2)), dma, dma, dma((2,)), dma((2,)), dma((4,)), dma, dma((8,)), dma((4,)),
            dma((4,)), dma, dma((4, 4)), dma, dma((4,)), dma, dma((8,)), dma,
            dma((4,)), dma, dma((4,)), dma, dma((4,)), dma,
            dma((4, 4)), dma((3,)), dma, dma, dma((8,)), dma((8,)), dma((8, 4)), dma((4,)), dma((4,)), dma,
        ],
        compiler_params=pltpu.CompilerParams(collective_id=0, has_side_effects=True),
    )(live, targets, child_rhs, child_diag, child_off, top_rhs, top_factor.T, top_diag)
    return pl.pallas_call(
        write_out,
        out_shape=tuple(jax.ShapeDtypeStruct(a.shape, F32) for a in (child_rhs, top_rhs)),
        in_specs=[pl.BlockSpec(memory_space=pltpu.VMEM)] * 2,
        out_specs=(any_, any_),
        scratch_shapes=[dma((4,))],
    )(*(pltpu.with_memory_space_constraint(a, pltpu.VMEM) for a in solved))


def solution(mesh):
    parts = ("leaf", "row", "col")
    in_specs = (
        P(parts, None, None),
        P(parts, None, None),
        P(parts, None, None),
        P(parts),
        P(parts, None),
        P("row", None),
        P("row", "col"),
        P("row", None),
    )
    out_specs = (P(parts, None, None), P("row", None))
    return jax.shard_map(shards, mesh=mesh, in_specs=in_specs, out_specs=out_specs, check_vma=False)
```

```python
import jax
import jax.numpy as jnp
from jax import lax
from jax.experimental import pallas as pl
from jax.experimental.pallas import tpu as pltpu
from jax.sharding import PartitionSpec as P

MESH = pl.DeviceIdType.MESH
F32 = jnp.float32
BF16 = jnp.bfloat16
NX, NY, NZ = 4, 4, 8


def split(value):
    high = value.astype(BF16)
    return high, (value - high.astype(F32)).astype(BF16)


def dot(a, b):
    return jnp.dot(a, b, preferred_element_type=F32)


def dot3(a, b):
    ah, al = split(a)
    bh, bl = split(b)
    return dot(ah, bh) + (dot(ah, bl) + dot(al, bh))


def dot3p(a, bh, bl):
    n = a.shape[0]
    ah, al = split(a)
    both = dot(jnp.concatenate([ah, al], axis=0), bh)
    return both[:n] + (dot(ah, bl) + both[n:])


def dott(a, b):
    return lax.dot_general(a, b, (((1,), (1,)), ((), ())), preferred_element_type=F32)


def dot3t(a, b):
    ah, al = split(a)
    bh, bl = split(b)
    return dott(ah, bh) + (dott(ah, bl) + dott(al, bh))


def tril(value, row0, col0):
    rows = lax.broadcasted_iota(jnp.int32, value.shape, 0) + row0
    cols = lax.broadcasted_iota(jnp.int32, value.shape, 1) + col0
    return jnp.where(rows >= cols, value, 0.0), rows == cols


def kernel(
    live_ref, targ_ref, rhs_hbm, diag_hbm, off_hbm, trhs_hbm, fac_hbm, td_hbm,
    csol_v, outv,
    rhs_v, diag_v, off_v, tile_v, trhs_v, fac_v, td_v,
    tg, trecv, tcol, tt, cbuf, axrecv, ybuf, byrecv, ysum, bxrecv, azsrc, azrecv, bzsrc, bzrecv,
    aysrc, ayrecv, cysrc, cyrecv, upd,
    rhst, tinv, gsrc, grecv, gparts, gsib, lastrecv, fsrc, xrecv, frecv, fown, fall,
    near, load_sem, tgs, tgr, cs, cr, gas, gar, gs, gr, axs, axr, bys, byr, bxs, bxr, azs, azr,
    bzs, bzr, ays, ayr, cys, cyr, lasts, lastr, ess, esr, xs, xr, fps, fpr, f1s, f1r, f2s, f2r, f3s, f3r,
):
    leaf, x, col = lax.axis_index("leaf"), lax.axis_index("row"), lax.axis_index("col")
    y, z = col % NY, col // NY
    sibling = 1 - leaf

    def local(src, dst, sem):
        return pltpu.make_async_copy(src, dst, sem)

    def remote(src, dst, send, recv, l2, x2, y2, z2):
        return pltpu.make_async_remote_copy(
            src_ref=src, dst_ref=dst, send_sem=send, recv_sem=recv,
            device_id=(l2, x2, z2 * NY + y2), device_id_type=MESH,
        )

    def arrived(ref, sem):
        pltpu.make_async_copy(ref, ref, sem).wait()

    drain = []

    def finish():
        for wait in drain:
            wait()

    loads = [
        local(ref.at[s], buf.at[s], load_sem.at[i, s])
        for s in range(2)
        for i, (ref, buf) in enumerate(((diag_hbm, diag_v), (rhs_hbm, rhs_v), (off_hbm, off_v)))
    ] + [
        local(td_hbm, td_v, load_sem.at[3, 0]),
        local(fac_hbm, fac_v, load_sem.at[4, 0]),
        local(trhs_hbm, trhs_v, load_sem.at[5, 0]),
    ]
    for copy in loads:
        copy.start()

    barrier = pltpu.get_barrier_semaphore()

    def greet(l2, x2, y2, z2):
        pl.semaphore_signal(barrier, inc=1, device_id=(l2, x2, z2 * NY + y2), device_id_type=MESH)

    greet(sibling, x, y, z)
    for d in range(1, NX):
        greet(leaf, (x + d) % NX, y, z)
    for d in range(1, NY):
        greet(leaf, x, (y + d) % NY, z)
    for d in (1, NZ - 1):
        greet(leaf, x, y, (z + d) % NZ)

    lane = lax.broadcasted_iota(jnp.int32, (1, 256), 1)
    for s in range(2):
        row = jnp.where(lane < live_ref[s], targ_ref[s : s + 1, :], -1).astype(F32)
        tg[0, s, :, :] = jnp.broadcast_to(row, (8, 256))

    for s in range(2):
        loads[3 * s].wait()
        loads[3 * s + 1].wait()
        low, _ = tril(diag_v[s], 0, 0)
        sol = rhs_v[s] + dot3(low, rhs_v[s])
        csol_v[s] = sol
        loads[3 * s + 2].wait()
        tile_v[s] = dot3(off_v[s], sol)

    pl.semaphore_wait(barrier, 1 + NX - 1 + NY - 1 + 2)

    def spread(step):
        for d in (step, NZ - step):
            pl.semaphore_signal(
                near.at[step - 1], inc=1, device_id=(leaf, x, (z + d) % NZ * NY + y), device_id_type=MESH
            )

    spread(1)
    tg_copy = remote(tg.at[0], tg.at[1], tgs, tgr, sibling, x, y, z)
    tg_copy.start()
    drain.append(tg_copy.wait_send)
    core_copies = []
    for s in range(2):
        copy = remote(
            tile_v.at[s, :, pl.ds(pl.multiple_of(sibling * 128, 128), 128)], trecv.at[s],
            cs.at[s], cr.at[s], sibling, x, y, z,
        )
        copy.start()
        core_copies.append(copy)
        drain.append(copy.wait_send)

    half = pl.ds(pl.multiple_of(leaf * 128, 128), 128)
    for s in range(2):
        tcol[256 * s : 256 * s + 256, :] = jnp.broadcast_to(tg[0, s, 0:1, :], (128, 256)).T
        high, rest = split(tile_v[s, :, half].T)
        tt[0:128, 256 * s : 256 * s + 256] = high
        tt[128:256, 256 * s : 256 * s + 256] = rest
    tg_copy.wait_recv()
    for s in range(2):
        tcol[512 + 256 * s : 768 + 256 * s, :] = jnp.broadcast_to(tg[1, s, 0:1, :], (128, 256)).T
        core_copies[s].wait_recv()
        high, rest = split(trecv[s].T)
        tt[0:128, 512 + 256 * s : 768 + 256 * s] = high
        tt[128:256, 512 + 256 * s : 768 + 256 * s] = rest
    lane = lax.broadcasted_iota(jnp.int32, (1024, 128), 1)

    def contrib(start):
        rel = tcol[...] - start.astype(F32)
        lanes = lane.astype(F32)
        hot = jnp.concatenate(
            [jnp.where(rel == lanes, 1.0, 0.0), jnp.where(rel == lanes + 128.0, 1.0, 0.0)], axis=1
        ).astype(BF16)
        both = dot(tt[...], hot)
        return both[0:128] + both[128:256]

    def ax_copy(d):
        return remote(cbuf.at[d], axrecv.at[d - 1], axs.at[d], axr, leaf, (x + d) % NX, y, z)

    def by_copy(d, b):
        y2 = (y + d) % NY
        return remote(ybuf.at[y2, b], byrecv.at[d - 1, b], bys.at[d, b], byr, leaf, x, y2, z)

    def lower(d):
        cbuf[d] = contrib((x + d) % NX * 512)

    def upper(b, _):
        value = contrib(b * 512 + 256)
        for part in range(NY):
            ybuf[part, b] = value[
                part % 2 * 64 : part % 2 * 64 + 64, part // 2 * 128 : part // 2 * 128 + 128
            ]
        for d in (2, 1, 3):
            by_copy(d, b).start()
        return 0

    def lower_upper(i, _):
        d = (i * 2 + 1) % NX + i // 2
        lower(d)
        ax_copy(d).start()
        upper(i, 0)
        return 0

    lax.fori_loop(0, 3, lower_upper, 0)
    upper(jnp.int32(3), 0)
    pl.semaphore_wait(near.at[0], 2)
    spread(2)
    drain += [ax_copy(d).wait_send for d in range(1, NX)]
    drain += [by_copy(d, b).wait_send for d in range(1, NY) for b in range(NX)]

    giver = (leaf == z % 2) & (z // 2 < x)
    for load in loads[6:]:
        load.wait()

    def ga_copy(d):
        y2 = (y + d) % NY
        return remote(gsrc.at[y2], grecv.at[z // 2, y], gas.at[d], gar, leaf, x, y2, z)

    @pl.when(giver)
    def _():
        low, _ = tril(td_v[...], 0, 0)
        fac = fac_v[...]
        gt = fac + dot3t(fac, low)
        for y2 in range(NY):
            gsrc[y2] = gt[:, 128 * y2 : 128 * y2 + 128]
        for d in range(1, NY):
            ga_copy(d).start()
        local(gsrc.at[y], grecv.at[z // 2, y], gar).start()

    def gb_copy(d):
        return remote(
            grecv.at[z // 2], grecv.at[z // 2], gs.at[d], gr.at[z // 2], leaf, x, y, (z + d) % NZ
        )

    def g_forward():
        @pl.when(giver)
        def _():
            arrived(grecv.at[z // 2], gar)
            for d in range(1, NZ):
                gb_copy(d).start()

    def g_drain():
        @pl.when(giver)
        def _():
            for d in range(1, NY):
                ga_copy(d).wait_send()
            for d in range(1, NZ):
                gb_copy(d).wait_send()

    drain.append(g_drain)

    row0, col0 = pl.multiple_of(y * 128, 128), pl.multiple_of(leaf * 256, 256)
    low, eye = tril(td_v[pl.ds(row0, 128), pl.ds(col0, 256)], row0, col0)
    tinv[0], tinv[1] = split((low + jnp.where(eye, 1.0, 0.0)).T)
    rhst[...] = trhs_v[pl.ds(col0, 256), :].T

    lower(0)
    pl.semaphore_wait(near.at[1], 2)

    arrived(byrecv, byr)

    def bx_copy(d):
        block = (x + d) % NX
        return remote(ysum.at[block], bxrecv.at[d - 1], bxs.at[d], bxr, leaf, block, y, z)

    def add_y(d):
        b = (x + d) % NX
        ysum[b] = ybuf[y, b] + byrecv[0, b] + byrecv[1, b] + byrecv[2, b]

    for d in (2, 1, 3):
        add_y(d)
        bx_copy(d).start()
        drain.append(bx_copy(d).wait_send)
    add_y(0)

    def az_copy(e):
        z2 = (z + e) % NZ
        return remote(azsrc.at[z2], azrecv.at[e - 1], azs.at[e], azr, leaf, x, y, z2)

    arrived(axrecv, axr)
    azsrc[...] = (cbuf[0] + axrecv[0] + axrecv[1] + axrecv[2]).reshape(NZ, 16, 256)
    for e in (4, 3, 5, 2, 6, 1, 7):
        az_copy(e).start()
        drain.append(az_copy(e).wait_send)

    keeper = z // 4 == y % 2

    def bz_copy(i):
        z2 = y % 2 * 4 + i
        return z2 != z, remote(bzsrc.at[i], bzrecv.at[z], bzs.at[i], bzr, leaf, x, y, z2)

    arrived(bxrecv, bxr)
    bzsrc[...] = (ysum[x] + bxrecv[0] + bxrecv[1] + bxrecv[2]).reshape(4, 16, 128)
    for i in range(4):
        away, copy = bz_copy(i)
        pl.when(away)(copy.start)

    def bz_drain():
        for i in range(4):
            away, copy = bz_copy(i)
            pl.when(away)(copy.wait_send)

    drain.append(bz_drain)
    pl.when(keeper)(local(bzsrc.at[z % 4], bzrecv.at[z], bzr).start)
    g_forward()

    def ay_copy(dy):
        return remote(aysrc, ayrecv.at[leaf, dy], ays.at[dy], ayr, 0, x, (y + dy) % NY, z)

    arrived(azrecv, azr)
    total = azsrc[z]
    for e in range(NZ - 1):
        total = total + azrecv[e]
    aysrc[...] = total
    for dy in (2, 1, 3):
        ay_copy(dy).start()
        drain.append(ay_copy(dy).wait_send)
    pl.when(leaf == 0)(local(aysrc, ayrecv.at[leaf, 0], ayr).start)
    pl.when(leaf == 1)(ay_copy(0).start)
    drain.append(lambda: pl.when(leaf == 1)(ay_copy(0).wait_send))

    def cy_copy(dy):
        return remote(cysrc, cyrecv.at[leaf, y // 2], cys.at[dy], cyr, 1, x, (y + dy) % NY, z)

    @pl.when(keeper)
    def _():
        arrived(bzrecv, bzr)
        total = bzrecv[0]
        for e in range(1, NZ):
            total = total + bzrecv[e]
        cysrc[...] = total
        for dy in (2, 1, 3):
            cy_copy(dy).start()
        pl.when(leaf == 1)(local(cysrc, cyrecv.at[leaf, y // 2], cyr).start)
        pl.when(leaf == 0)(cy_copy(0).start)

    def cy_drain():
        @pl.when(keeper)
        def _():
            for dy in range(1, NY):
                cy_copy(dy).wait_send()
            pl.when(leaf == 0)(cy_copy(0).wait_send)

    drain.append(cy_drain)

    @pl.when(leaf == 0)
    def _():
        arrived(ayrecv, ayr)
        for h in range(2):
            upd[h] = ayrecv[h, 0] + ayrecv[h, 1] + ayrecv[h, 2] + ayrecv[h, 3]

    @pl.when(leaf == 1)
    def _():
        arrived(cyrecv, cyr)
        for h in range(2):
            upd[h] = jnp.concatenate([cyrecv[h, 0], cyrecv[h, 1]], axis=1)

    reds = []
    for h in range(2):
        reds.append(rhst[pl.ds(pl.multiple_of(h * 128 + z * 16, 16), 16), :] - upd[h])
    acc = dot3p(jnp.concatenate(reds, axis=0), tinv[0], tinv[1])
    fsrc[...] = acc.reshape(2, 16, 128)

    def x_copy(k, x2, y2):
        return remote(
            fsrc, xrecv.at[k, leaf, y % 2], xs.at[x2, y2], xr.at[k], y // 2, x2, y2, z
        )

    for k in range(NX - 2):

        @pl.when(x == k)
        def _(k=k):
            for x2 in range(k + 1, NX):
                for y2 in range(NY):
                    x_copy(k, x2, y2).start()

        @pl.when(x > k)
        def _(k=k):
            @pl.when(z != 2 * k + leaf)
            def _():
                arrived(grecv.at[k], gr.at[k])

            high, rest = split(grecv[k].reshape(256, 128))
            gparts[k, 0] = high
            gparts[k, 1] = rest
            arrived(xrecv.at[k], xr.at[k])
            parts = (xrecv[k, 0] + xrecv[k, 1]).reshape(2, 32, 128)
            solved = jnp.concatenate([parts[0], parts[1]], axis=1)
            step = dot3p(solved, gparts[k, 0], gparts[k, 1])
            fsrc[...] = fsrc[...] - step.reshape(2, 16, 128)

        def x_drain(k=k):
            @pl.when(x == k)
            def _():
                for x2 in range(k + 1, NX):
                    for y2 in range(NY):
                        x_copy(k, x2, y2).wait_send()

        drain.append(x_drain)

    def last_copy(h, y2):
        return remote(fsrc.at[h], lastrecv.at[leaf, y], lasts.at[h, y2], lastr, h, NX - 1, y2, z)

    other_g = remote(grecv.at[NX - 2], gsib, ess, esr, sibling, x, y, z)
    pair = remote(fsrc.at[sibling], frecv, fps, fpr, sibling, x, y, z)

    @pl.when(x == NX - 2)
    def _():
        for y2 in range(NY):
            for h in range(2):
                last_copy(h, y2).start()

    pair.start()
    drain.append(pair.wait_send)

    @pl.when(x == NX - 1)
    def _():
        @pl.when(z != 2 * (NX - 2) + leaf)
        def _():
            arrived(grecv.at[NX - 2], gr.at[NX - 2])

        other_g.start()

    pair.wait_recv()
    fown[...] = fsrc[leaf] + frecv[...]

    @pl.when(x == NX - 1)
    def _():
        own = split(grecv[NX - 2].reshape(256, 128))
        other_g.wait_recv()
        other = split(gsib[...].reshape(256, 128))
        arrived(lastrecv, lastr)

        def solved(core):
            first = lastrecv[0, 2 * core] + lastrecv[1, 2 * core]
            second = lastrecv[0, 2 * core + 1] + lastrecv[1, 2 * core + 1]
            return jnp.concatenate([first, second], axis=1)

        fown[...] = fown[...] - (dot3p(solved(leaf), *own) + dot3p(solved(sibling), *other))

    def last_drain():
        @pl.when(x == NX - 2)
        def _():
            for y2 in range(NY):
                for h in range(2):
                    last_copy(h, y2).wait_send()

        pl.when(x == NX - 1)(other_g.wait_send)

    drain.append(last_drain)

    late = []

    def f1_copy(d):
        return remote(fown, fall.at[y, z], f1s.at[d], f1r.at[d], leaf, x, y, (z + d) % NZ)

    def f2_copy(d, dy):
        part = fall.at[y, (z + NZ - d) % NZ]
        return remote(part, part, f2s.at[d, dy], f2r.at[y], leaf, x, (y + dy) % NY, z)

    for d in (4, 3, 5, 2, 6, 1, 7):
        f1_copy(d).start()
        late.append(f1_copy(d).wait_send)
    fall[y, z] = fown[...]
    for d in (0, 1, 7, 2, 6, 3, 5, 4):
        if d:
            arrived(fall.at[y, (z + NZ - d) % NZ], f1r.at[d])
        for dy in (2, 1, 3):
            f2_copy(d, dy).start()
            late.append(f2_copy(d, dy).wait_send)
        if d == 0:
            finish()

    def f3_copy(y2):
        part = outv.at[pl.ds(pl.multiple_of(y2 * 128, 128), 128), half]
        return remote(part, part, f3s.at[y2], f3r, sibling, x, y, z)

    for d in (0, 1, 3, 2):
        y2 = (y + d) % NY
        if d:
            arrived(fall.at[y2], f2r.at[y2])
        outv[pl.ds(pl.multiple_of(y2 * 128, 128), 128), half] = fall[y2].reshape(128, 128).T
        f3_copy(y2).start()
    for wait in late:
        wait()
    arrived(outv.at[:, pl.ds(pl.multiple_of(sibling * 128, 128), 128)], f3r)
    for y2 in range(NY):
        f3_copy(y2).wait_send()


def write_out(csol_v, top_v, csol_hbm, top_hbm, sem):
    copies = [pltpu.make_async_copy(csol_v.at[s], csol_hbm.at[s], sem.at[s]) for s in range(2)]
    copies += [
        pltpu.make_async_copy(
            top_v.at[256 * s : 256 * s + 256], top_hbm.at[256 * s : 256 * s + 256], sem.at[2 + s]
        )
        for s in range(2)
    ]
    for copy in copies:
        copy.start()
    for copy in copies:
        copy.wait()


def shards(child_rhs, child_diag, child_off, live, targets, top_rhs, top_factor, top_diag):
    any_ = pl.BlockSpec(memory_space=pl.ANY)
    vm = pltpu.VMEM
    dma = pltpu.SemaphoreType.DMA
    solved = pl.pallas_call(
        kernel,
        out_shape=(
            pltpu.VMEM(child_rhs.shape, F32),
            pltpu.VMEM(top_rhs.shape, F32),
        ),
        in_specs=[
            pl.BlockSpec(memory_space=pltpu.SMEM),
            pl.BlockSpec(memory_space=pltpu.VMEM),
        ] + [any_] * 6,
        out_specs=(pl.BlockSpec(memory_space=pltpu.VMEM),) * 2,
        scratch_shapes=[
            vm((2, 256, 256), F32), vm((2, 256, 256), F32), vm((2, 256, 256), F32),
            vm((2, 256, 256), F32),
            vm((512, 256), F32), vm((64, 512), F32), vm((512, 512), F32),
            vm((2, 2, 8, 256), F32), vm((2, 256, 128), F32), vm((1024, 128), F32), vm((256, 1024), BF16),
            vm((4, 128, 256), F32), vm((3, 128, 256), F32),
            vm((4, 4, 64, 128), F32), vm((3, 4, 64, 128), F32), vm((4, 64, 128), F32), vm((3, 64, 128), F32),
            vm((8, 16, 256), F32), vm((7, 16, 256), F32), vm((4, 16, 128), F32), vm((8, 16, 128), F32),
            vm((16, 256), F32), vm((2, 4, 16, 256), F32), vm((16, 128), F32), vm((2, 2, 16, 128), F32),
            vm((2, 16, 256), F32),
            vm((256, 256), F32), vm((2, 256, 128), BF16),
            vm((4, 64, 128), F32), vm((3, 4, 64, 128), F32), vm((3, 2, 256, 128), BF16),
            vm((4, 64, 128), F32), vm((2, 4, 16, 128), F32),
            vm((2, 16, 128), F32), vm((3, 2, 2, 2, 16, 128), F32),
            vm((16, 128), F32), vm((16, 128), F32), vm((4, 8, 16, 128), F32),
            pltpu.SemaphoreType.REGULAR((2,)),
            dma((6, 2)), dma, dma, dma((2,)), dma((2,)), dma((4,)), dma, dma((8,)), dma((4,)),
            dma((4,)), dma, dma((4, 4)), dma, dma((4,)), dma, dma((8,)), dma,
            dma((4,)), dma, dma((4,)), dma, dma((4,)), dma,
            dma((2, 4)), dma, dma, dma,
            dma((4, 4)), dma((3,)), dma, dma, dma((8,)), dma((8,)), dma((8, 4)), dma((4,)), dma((4,)), dma,
        ],
        compiler_params=pltpu.CompilerParams(collective_id=0, has_side_effects=True),
    )(live, targets, child_rhs, child_diag, child_off, top_rhs, top_factor.T, top_diag)
    return pl.pallas_call(
        write_out,
        out_shape=tuple(jax.ShapeDtypeStruct(a.shape, F32) for a in (child_rhs, top_rhs)),
        in_specs=[pl.BlockSpec(memory_space=pltpu.VMEM)] * 2,
        out_specs=(any_, any_),
        scratch_shapes=[dma((4,))],
    )(*(pltpu.with_memory_space_constraint(a, pltpu.VMEM) for a in solved))


def solution(mesh):
    parts = ("leaf", "row", "col")
    in_specs = (
        P(parts, None, None),
        P(parts, None, None),
        P(parts, None, None),
        P(parts),
        P(parts, None),
        P("row", None),
        P("row", "col"),
        P("row", None),
    )
    out_specs = (P(parts, None, None), P("row", None))
    return jax.shard_map(shards, mesh=mesh, in_specs=in_specs, out_specs=out_specs, check_vma=False)
```

```python
import jax
import jax.numpy as jnp
from jax import lax
from jax.experimental import pallas as pl
from jax.experimental.pallas import tpu as pltpu
from jax.sharding import PartitionSpec as P

MESH = pl.DeviceIdType.MESH
F32 = jnp.float32
BF16 = jnp.bfloat16
NX, NY, NZ = 4, 4, 8


def split(value):
    high = value.astype(BF16)
    return high, (value - high.astype(F32)).astype(BF16)


def dot(a, b):
    return jnp.dot(a, b, preferred_element_type=F32)


def dot3(a, b):
    ah, al = split(a)
    bh, bl = split(b)
    return dot(ah, bh) + (dot(ah, bl) + dot(al, bh))


def dot3p(a, bh, bl):
    n = a.shape[0]
    ah, al = split(a)
    both = dot(jnp.concatenate([ah, al], axis=0), bh)
    return both[:n] + (dot(ah, bl) + both[n:])


def dott(a, b):
    return lax.dot_general(a, b, (((1,), (1,)), ((), ())), preferred_element_type=F32)


def dot3t(a, b):
    ah, al = split(a)
    bh, bl = split(b)
    return dott(ah, bh) + (dott(ah, bl) + dott(al, bh))


def tril(value, row0, col0):
    rows = lax.broadcasted_iota(jnp.int32, value.shape, 0) + row0
    cols = lax.broadcasted_iota(jnp.int32, value.shape, 1) + col0
    return jnp.where(rows >= cols, value, 0.0), rows == cols


def kernel(
    live_ref, targ_ref, rhs_hbm, diag_hbm, off_hbm, trhs_hbm, fac_hbm, td_hbm,
    csol_v, outv,
    rhs_v, diag_v, off_v, tile_v, trhs_v, fac_v, td_v,
    tg, trecv, tcol, tt, cbuf, axrecv, ybuf, byrecv, ysum, bxrecv, azsrc, azrecv, bzsrc, bzrecv,
    aysrc, ayrecv, cysrc, cyrecv, upd,
    rhst, tinv, gsrc, grecv, gparts, gsib, lastrecv, fsrc, xrecv, frecv, fown, fall,
    near, load_sem, tgs, tgr, cs, cr, gas, gar, gs, gr, axs, axr, bys, byr, bxs, bxr, azs, azr,
    bzs, bzr, ays, ayr, cys, cyr, lasts, lastr, ess, esr, xs, xr, fps, fpr, f1s, f1r, f2s, f2r, f3s, f3r,
):
    leaf, x, col = lax.axis_index("leaf"), lax.axis_index("row"), lax.axis_index("col")
    y, z = col % NY, col // NY
    sibling = 1 - leaf

    def local(src, dst, sem):
        return pltpu.make_async_copy(src, dst, sem)

    def remote(src, dst, send, recv, l2, x2, y2, z2):
        return pltpu.make_async_remote_copy(
            src_ref=src, dst_ref=dst, send_sem=send, recv_sem=recv,
            device_id=(l2, x2, z2 * NY + y2), device_id_type=MESH,
        )

    def arrived(ref, sem):
        pltpu.make_async_copy(ref, ref, sem).wait()

    drain = []

    def finish():
        for wait in drain:
            wait()

    loads = [
        local(ref.at[s], buf.at[s], load_sem.at[i, s])
        for s in range(2)
        for i, (ref, buf) in enumerate(((diag_hbm, diag_v), (rhs_hbm, rhs_v), (off_hbm, off_v)))
    ] + [
        local(td_hbm, td_v, load_sem.at[3, 0]),
        local(fac_hbm, fac_v, load_sem.at[4, 0]),
        local(trhs_hbm, trhs_v, load_sem.at[5, 0]),
    ]
    for copy in loads:
        copy.start()

    barrier = pltpu.get_barrier_semaphore()

    def greet(l2, x2, y2, z2):
        pl.semaphore_signal(barrier, inc=1, device_id=(l2, x2, z2 * NY + y2), device_id_type=MESH)

    greet(sibling, x, y, z)
    for d in range(1, NX):
        greet(leaf, (x + d) % NX, y, z)
    for d in range(1, NY):
        greet(leaf, x, (y + d) % NY, z)
    for d in (1, NZ - 1):
        greet(leaf, x, y, (z + d) % NZ)

    lane = lax.broadcasted_iota(jnp.int32, (1, 256), 1)
    for s in range(2):
        row = jnp.where(lane < live_ref[s], targ_ref[s : s + 1, :], -1).astype(F32)
        tg[0, s, :, :] = jnp.broadcast_to(row, (8, 256))

    for s in range(2):
        loads[3 * s].wait()
        loads[3 * s + 1].wait()
        low, _ = tril(diag_v[s], 0, 0)
        sol = rhs_v[s] + dot3(low, rhs_v[s])
        csol_v[s] = sol
        loads[3 * s + 2].wait()
        tile_v[s] = dot3(off_v[s], sol)

    pl.semaphore_wait(barrier, 1 + NX - 1 + NY - 1 + 2)

    def spread(step):
        for d in (step, NZ - step):
            pl.semaphore_signal(
                near.at[step - 1], inc=1, device_id=(leaf, x, (z + d) % NZ * NY + y), device_id_type=MESH
            )

    spread(1)
    tg_copy = remote(tg.at[0], tg.at[1], tgs, tgr, sibling, x, y, z)
    tg_copy.start()
    drain.append(tg_copy.wait_send)
    core_copies = []
    for s in range(2):
        copy = remote(
            tile_v.at[s, :, pl.ds(pl.multiple_of(sibling * 128, 128), 128)], trecv.at[s],
            cs.at[s], cr.at[s], sibling, x, y, z,
        )
        copy.start()
        core_copies.append(copy)
        drain.append(copy.wait_send)

    half = pl.ds(pl.multiple_of(leaf * 128, 128), 128)
    for s in range(2):
        tcol[256 * s : 256 * s + 256, :] = jnp.broadcast_to(tg[0, s, 0:1, :], (128, 256)).T
        high, rest = split(tile_v[s, :, half].T)
        tt[0:128, 256 * s : 256 * s + 256] = high
        tt[128:256, 256 * s : 256 * s + 256] = rest
    tg_copy.wait_recv()
    for s in range(2):
        tcol[512 + 256 * s : 768 + 256 * s, :] = jnp.broadcast_to(tg[1, s, 0:1, :], (128, 256)).T
        core_copies[s].wait_recv()
        high, rest = split(trecv[s].T)
        tt[0:128, 512 + 256 * s : 768 + 256 * s] = high
        tt[128:256, 512 + 256 * s : 768 + 256 * s] = rest
    lane = lax.broadcasted_iota(jnp.int32, (1024, 128), 1)

    def contrib(start):
        rel = tcol[...] - start.astype(F32)
        lanes = lane.astype(F32)
        hot = jnp.concatenate(
            [jnp.where(rel == lanes, 1.0, 0.0), jnp.where(rel == lanes + 128.0, 1.0, 0.0)], axis=1
        ).astype(BF16)
        both = dot(tt[...], hot)
        return both[0:128] + both[128:256]

    def ax_copy(d):
        return remote(cbuf.at[d], axrecv.at[d - 1], axs.at[d], axr, leaf, (x + d) % NX, y, z)

    def by_copy(d, b):
        y2 = (y + d) % NY
        return remote(ybuf.at[y2, b], byrecv.at[d - 1, b], bys.at[d, b], byr, leaf, x, y2, z)

    def lower(d):
        cbuf[d] = contrib((x + d) % NX * 512)

    def upper(b, _):
        value = contrib(b * 512 + 256)
        for part in range(NY):
            ybuf[part, b] = value[
                part % 2 * 64 : part % 2 * 64 + 64, part // 2 * 128 : part // 2 * 128 + 128
            ]
        for d in (2, 1, 3):
            by_copy(d, b).start()
        return 0

    def lower_upper(i, _):
        d = (i * 2 + 1) % NX + i // 2
        lower(d)
        ax_copy(d).start()
        upper(i, 0)
        return 0

    lax.fori_loop(0, 3, lower_upper, 0)
    upper(jnp.int32(3), 0)
    pl.semaphore_wait(near.at[0], 2)
    spread(2)
    drain += [ax_copy(d).wait_send for d in range(1, NX)]
    drain += [by_copy(d, b).wait_send for d in range(1, NY) for b in range(NX)]

    giver = (leaf == z % 2) & (z // 2 < x)
    for load in loads[6:]:
        load.wait()

    def ga_copy(d):
        y2 = (y + d) % NY
        return remote(gsrc.at[y2], grecv.at[z // 2, y], gas.at[d], gar, leaf, x, y2, z)

    @pl.when(giver)
    def _():
        low, _ = tril(td_v[...], 0, 0)
        fac = fac_v[...]
        gt = fac + dot3t(fac, low)
        for y2 in range(NY):
            gsrc[y2] = gt[:, 128 * y2 : 128 * y2 + 128]
        for d in range(1, NY):
            ga_copy(d).start()
        local(gsrc.at[y], grecv.at[z // 2, y], gar).start()

    def gb_copy(d):
        return remote(
            grecv.at[z // 2], grecv.at[z // 2], gs.at[d], gr.at[z // 2], leaf, x, y, (z + d) % NZ
        )

    def g_forward():
        @pl.when(giver)
        def _():
            arrived(grecv.at[z // 2], gar)
            for d in range(1, NZ):
                gb_copy(d).start()

    def g_drain():
        @pl.when(giver)
        def _():
            for d in range(1, NY):
                ga_copy(d).wait_send()
            for d in range(1, NZ):
                gb_copy(d).wait_send()

    drain.append(g_drain)

    row0, col0 = pl.multiple_of(y * 128, 128), pl.multiple_of(leaf * 256, 256)
    low, eye = tril(td_v[pl.ds(row0, 128), pl.ds(col0, 256)], row0, col0)
    tinv[0], tinv[1] = split((low + jnp.where(eye, 1.0, 0.0)).T)
    rhst[...] = trhs_v[pl.ds(col0, 256), :].T

    lower(0)
    pl.semaphore_wait(near.at[1], 2)

    arrived(byrecv, byr)

    def bx_copy(d):
        block = (x + d) % NX
        return remote(ysum.at[block], bxrecv.at[d - 1], bxs.at[d], bxr, leaf, block, y, z)

    def add_y(d):
        b = (x + d) % NX
        ysum[b] = ybuf[y, b] + byrecv[0, b] + byrecv[1, b] + byrecv[2, b]

    for d in (2, 1, 3):
        add_y(d)
        bx_copy(d).start()
        drain.append(bx_copy(d).wait_send)
    add_y(0)

    def az_copy(e):
        z2 = (z + e) % NZ
        return remote(azsrc.at[z2], azrecv.at[e - 1], azs.at[e], azr, leaf, x, y, z2)

    arrived(axrecv, axr)
    azsrc[...] = (cbuf[0] + axrecv[0] + axrecv[1] + axrecv[2]).reshape(NZ, 16, 256)
    for e in (4, 3, 5, 2, 6, 1, 7):
        az_copy(e).start()
        drain.append(az_copy(e).wait_send)

    keeper = z // 4 == y % 2

    def bz_copy(i):
        z2 = y % 2 * 4 + i
        return z2 != z, remote(bzsrc.at[i], bzrecv.at[z], bzs.at[i], bzr, leaf, x, y, z2)

    arrived(bxrecv, bxr)
    bzsrc[...] = (ysum[x] + bxrecv[0] + bxrecv[1] + bxrecv[2]).reshape(4, 16, 128)
    for i in range(4):
        away, copy = bz_copy(i)
        pl.when(away)(copy.start)

    def bz_drain():
        for i in range(4):
            away, copy = bz_copy(i)
            pl.when(away)(copy.wait_send)

    drain.append(bz_drain)
    pl.when(keeper)(local(bzsrc.at[z % 4], bzrecv.at[z], bzr).start)
    g_forward()

    def ay_copy(dy):
        return remote(aysrc, ayrecv.at[leaf, dy], ays.at[dy], ayr, 0, x, (y + dy) % NY, z)

    arrived(azrecv, azr)
    total = azsrc[z]
    for e in range(NZ - 1):
        total = total + azrecv[e]
    aysrc[...] = total
    for dy in (2, 1, 3):
        ay_copy(dy).start()
        drain.append(ay_copy(dy).wait_send)
    pl.when(leaf == 0)(local(aysrc, ayrecv.at[leaf, 0], ayr).start)
    pl.when(leaf == 1)(ay_copy(0).start)
    drain.append(lambda: pl.when(leaf == 1)(ay_copy(0).wait_send))

    def cy_copy(dy):
        return remote(cysrc, cyrecv.at[leaf, y // 2], cys.at[dy], cyr, 1, x, (y + dy) % NY, z)

    @pl.when(keeper)
    def _():
        arrived(bzrecv, bzr)
        total = bzrecv[0]
        for e in range(1, NZ):
            total = total + bzrecv[e]
        cysrc[...] = total
        for dy in (2, 1, 3):
            cy_copy(dy).start()
        pl.when(leaf == 1)(local(cysrc, cyrecv.at[leaf, y // 2], cyr).start)
        pl.when(leaf == 0)(cy_copy(0).start)

    def cy_drain():
        @pl.when(keeper)
        def _():
            for dy in range(1, NY):
                cy_copy(dy).wait_send()
            pl.when(leaf == 0)(cy_copy(0).wait_send)

    drain.append(cy_drain)

    @pl.when(leaf == 0)
    def _():
        arrived(ayrecv, ayr)
        for h in range(2):
            upd[h] = ayrecv[h, 0] + ayrecv[h, 1] + ayrecv[h, 2] + ayrecv[h, 3]

    @pl.when(leaf == 1)
    def _():
        arrived(cyrecv, cyr)
        for h in range(2):
            upd[h] = jnp.concatenate([cyrecv[h, 0], cyrecv[h, 1]], axis=1)

    reds = []
    for h in range(2):
        reds.append(rhst[pl.ds(pl.multiple_of(h * 128 + z * 16, 16), 16), :] - upd[h])
    acc = dot3p(jnp.concatenate(reds, axis=0), tinv[0], tinv[1])
    fsrc[...] = acc.reshape(2, 16, 128)

    def x_copy(k, x2, dy):
        return remote(
            fsrc, xrecv.at[k, leaf, y % 2], xs.at[x2, dy], xr.at[k], y // 2, x2, (y + dy) % NY, z
        )

    for k in range(NX - 2):

        @pl.when(x == k)
        def _(k=k):
            for x2 in range(k + 1, NX):
                for dy in (2, 1, 3, 0):
                    x_copy(k, x2, dy).start()

        @pl.when(x > k)
        def _(k=k):
            @pl.when(z != 2 * k + leaf)
            def _():
                arrived(grecv.at[k], gr.at[k])

            high, rest = split(grecv[k].reshape(256, 128))
            gparts[k, 0] = high
            gparts[k, 1] = rest
            arrived(xrecv.at[k], xr.at[k])
            parts = (xrecv[k, 0] + xrecv[k, 1]).reshape(2, 32, 128)
            solved = jnp.concatenate([parts[0], parts[1]], axis=1)
            step = dot3p(solved, gparts[k, 0], gparts[k, 1])
            fsrc[...] = fsrc[...] - step.reshape(2, 16, 128)

        def x_drain(k=k):
            @pl.when(x == k)
            def _():
                for x2 in range(k + 1, NX):
                    for y2 in range(NY):
                        x_copy(k, x2, y2).wait_send()

        drain.append(x_drain)

    def last_copy(h, dy):
        return remote(
            fsrc.at[h], lastrecv.at[leaf, y], lasts.at[h, dy], lastr, h, NX - 1, (y + dy) % NY, z
        )

    other_g = remote(grecv.at[NX - 2], gsib, ess, esr, sibling, x, y, z)
    pair = remote(fsrc.at[sibling], frecv, fps, fpr, sibling, x, y, z)

    @pl.when(x == NX - 2)
    def _():
        for dy in (2, 1, 3, 0):
            for h in range(2):
                last_copy(h, dy).start()

    pair.start()
    drain.append(pair.wait_send)

    @pl.when(x == NX - 1)
    def _():
        @pl.when(z != 2 * (NX - 2) + leaf)
        def _():
            arrived(grecv.at[NX - 2], gr.at[NX - 2])

        other_g.start()

    pair.wait_recv()
    fown[...] = fsrc[leaf] + frecv[...]

    @pl.when(x == NX - 1)
    def _():
        own = split(grecv[NX - 2].reshape(256, 128))
        other_g.wait_recv()
        other = split(gsib[...].reshape(256, 128))
        arrived(lastrecv, lastr)

        def solved(core):
            first = lastrecv[0, 2 * core] + lastrecv[1, 2 * core]
            second = lastrecv[0, 2 * core + 1] + lastrecv[1, 2 * core + 1]
            return jnp.concatenate([first, second], axis=1)

        fown[...] = fown[...] - (dot3p(solved(leaf), *own) + dot3p(solved(sibling), *other))

    def last_drain():
        @pl.when(x == NX - 2)
        def _():
            for y2 in range(NY):
                for h in range(2):
                    last_copy(h, y2).wait_send()

        pl.when(x == NX - 1)(other_g.wait_send)

    drain.append(last_drain)

    late = []

    def f1_copy(d):
        return remote(fown, fall.at[y, z], f1s.at[d], f1r.at[d], leaf, x, y, (z + d) % NZ)

    def f2_copy(d, dy):
        part = fall.at[y, (z + NZ - d) % NZ]
        return remote(part, part, f2s.at[d, dy], f2r.at[y], leaf, x, (y + dy) % NY, z)

    for d in (4, 3, 5, 2, 6, 1, 7):
        f1_copy(d).start()
        late.append(f1_copy(d).wait_send)
    fall[y, z] = fown[...]
    for d in (0, 1, 7, 2, 6, 3, 5, 4):
        if d:
            arrived(fall.at[y, (z + NZ - d) % NZ], f1r.at[d])
        for dy in (2, 1, 3):
            f2_copy(d, dy).start()
            late.append(f2_copy(d, dy).wait_send)
        if d == 0:
            finish()

    def f3_copy(y2):
        part = outv.at[pl.ds(pl.multiple_of(y2 * 128, 128), 128), half]
        return remote(part, part, f3s.at[y2], f3r, sibling, x, y, z)

    for d in (0, 1, 3, 2):
        y2 = (y + d) % NY
        if d:
            arrived(fall.at[y2], f2r.at[y2])
        outv[pl.ds(pl.multiple_of(y2 * 128, 128), 128), half] = fall[y2].reshape(128, 128).T
        f3_copy(y2).start()
    for wait in late:
        wait()
    arrived(outv.at[:, pl.ds(pl.multiple_of(sibling * 128, 128), 128)], f3r)
    for y2 in range(NY):
        f3_copy(y2).wait_send()


def write_out(csol_v, top_v, csol_hbm, top_hbm, sem):
    copies = [pltpu.make_async_copy(csol_v.at[s], csol_hbm.at[s], sem.at[s]) for s in range(2)]
    copies += [
        pltpu.make_async_copy(
            top_v.at[256 * s : 256 * s + 256], top_hbm.at[256 * s : 256 * s + 256], sem.at[2 + s]
        )
        for s in range(2)
    ]
    for copy in copies:
        copy.start()
    for copy in copies:
        copy.wait()


def shards(child_rhs, child_diag, child_off, live, targets, top_rhs, top_factor, top_diag):
    any_ = pl.BlockSpec(memory_space=pl.ANY)
    vm = pltpu.VMEM
    dma = pltpu.SemaphoreType.DMA
    solved = pl.pallas_call(
        kernel,
        out_shape=(
            pltpu.VMEM(child_rhs.shape, F32),
            pltpu.VMEM(top_rhs.shape, F32),
        ),
        in_specs=[
            pl.BlockSpec(memory_space=pltpu.SMEM),
            pl.BlockSpec(memory_space=pltpu.VMEM),
        ] + [any_] * 6,
        out_specs=(pl.BlockSpec(memory_space=pltpu.VMEM),) * 2,
        scratch_shapes=[
            vm((2, 256, 256), F32), vm((2, 256, 256), F32), vm((2, 256, 256), F32),
            vm((2, 256, 256), F32),
            vm((512, 256), F32), vm((64, 512), F32), vm((512, 512), F32),
            vm((2, 2, 8, 256), F32), vm((2, 256, 128), F32), vm((1024, 128), F32), vm((256, 1024), BF16),
            vm((4, 128, 256), F32), vm((3, 128, 256), F32),
            vm((4, 4, 64, 128), F32), vm((3, 4, 64, 128), F32), vm((4, 64, 128), F32), vm((3, 64, 128), F32),
            vm((8, 16, 256), F32), vm((7, 16, 256), F32), vm((4, 16, 128), F32), vm((8, 16, 128), F32),
            vm((16, 256), F32), vm((2, 4, 16, 256), F32), vm((16, 128), F32), vm((2, 2, 16, 128), F32),
            vm((2, 16, 256), F32),
            vm((256, 256), F32), vm((2, 256, 128), BF16),
            vm((4, 64, 128), F32), vm((3, 4, 64, 128), F32), vm((3, 2, 256, 128), BF16),
            vm((4, 64, 128), F32), vm((2, 4, 16, 128), F32),
            vm((2, 16, 128), F32), vm((3, 2, 2, 2, 16, 128), F32),
            vm((16, 128), F32), vm((16, 128), F32), vm((4, 8, 16, 128), F32),
            pltpu.SemaphoreType.REGULAR((2,)),
            dma((6, 2)), dma, dma, dma((2,)), dma((2,)), dma((4,)), dma, dma((8,)), dma((4,)),
            dma((4,)), dma, dma((4, 4)), dma, dma((4,)), dma, dma((8,)), dma,
            dma((4,)), dma, dma((4,)), dma, dma((4,)), dma,
            dma((2, 4)), dma, dma, dma,
            dma((4, 4)), dma((3,)), dma, dma, dma((8,)), dma((8,)), dma((8, 4)), dma((4,)), dma((4,)), dma,
        ],
        compiler_params=pltpu.CompilerParams(collective_id=0, has_side_effects=True),
    )(live, targets, child_rhs, child_diag, child_off, top_rhs, top_factor.T, top_diag)
    return pl.pallas_call(
        write_out,
        out_shape=tuple(jax.ShapeDtypeStruct(a.shape, F32) for a in (child_rhs, top_rhs)),
        in_specs=[pl.BlockSpec(memory_space=pltpu.VMEM)] * 2,
        out_specs=(any_, any_),
        scratch_shapes=[dma((4,))],
    )(*(pltpu.with_memory_space_constraint(a, pltpu.VMEM) for a in solved))


def solution(mesh):
    parts = ("leaf", "row", "col")
    in_specs = (
        P(parts, None, None),
        P(parts, None, None),
        P(parts, None, None),
        P(parts),
        P(parts, None),
        P("row", None),
        P("row", "col"),
        P("row", None),
    )
    out_specs = (P(parts, None, None), P("row", None))
    return jax.shard_map(shards, mesh=mesh, in_specs=in_specs, out_specs=out_specs, check_vma=False)
```

```python
import jax
import jax.numpy as jnp
from jax import lax
from jax.experimental import pallas as pl
from jax.experimental.pallas import tpu as pltpu
from jax.sharding import PartitionSpec as P

MESH = pl.DeviceIdType.MESH
F32 = jnp.float32
BF16 = jnp.bfloat16
NX, NY, NZ = 4, 4, 8


def split(value):
    high = value.astype(BF16)
    return high, (value - high.astype(F32)).astype(BF16)


def dot(a, b):
    return jnp.dot(a, b, preferred_element_type=F32)


def dot3(a, b):
    ah, al = split(a)
    bh, bl = split(b)
    return dot(ah, bh) + (dot(ah, bl) + dot(al, bh))


def dot3p(a, bh, bl):
    n = a.shape[0]
    ah, al = split(a)
    both = dot(jnp.concatenate([ah, al], axis=0), bh)
    return both[:n] + (dot(ah, bl) + both[n:])


def dott(a, b):
    return lax.dot_general(a, b, (((1,), (1,)), ((), ())), preferred_element_type=F32)


def dot3t(a, b):
    ah, al = split(a)
    bh, bl = split(b)
    return dott(ah, bh) + (dott(ah, bl) + dott(al, bh))


def tril(value, row0, col0):
    rows = lax.broadcasted_iota(jnp.int32, value.shape, 0) + row0
    cols = lax.broadcasted_iota(jnp.int32, value.shape, 1) + col0
    return jnp.where(rows >= cols, value, 0.0), rows == cols


def kernel(
    live_ref, targ_ref, rhs_hbm, diag_hbm, off_hbm, trhs_hbm, fac_hbm, td_hbm,
    csol_v, outv,
    rhs_v, diag_v, off_v, tile_v, trhs_v, fac_v, td_v,
    tg, trecv, tcol, tt, cbuf, axrecv, ybuf, byrecv, ysum, bxrecv, azsrc, azrecv, bzsrc, bzrecv,
    aysrc, ayrecv, cysrc, cyrecv, upd,
    rhst, tinv, gsrc, grecv, gparts, gsib, lastrecv, fsrc, xrecv, frecv, fown, fall,
    near, load_sem, tgs, tgr, cs, cr, gas, gar, gs, gr, axs, axr, bys, byr, bxs, bxr, azs, azr,
    bzs, bzr, ays, ayr, cys, cyr, lasts, lastr, ess, esr, xs, xr, fps, fpr, f1s, f1r, f2s, f2r, f3s, f3r,
):
    leaf, x, col = lax.axis_index("leaf"), lax.axis_index("row"), lax.axis_index("col")
    y, z = col % NY, col // NY
    sibling = 1 - leaf

    def local(src, dst, sem):
        return pltpu.make_async_copy(src, dst, sem)

    def remote(src, dst, send, recv, l2, x2, y2, z2):
        return pltpu.make_async_remote_copy(
            src_ref=src, dst_ref=dst, send_sem=send, recv_sem=recv,
            device_id=(l2, x2, z2 * NY + y2), device_id_type=MESH,
        )

    def arrived(ref, sem):
        pltpu.make_async_copy(ref, ref, sem).wait()

    drain = []

    def finish():
        for wait in drain:
            wait()

    loads = [
        local(ref.at[s], buf.at[s], load_sem.at[i, s])
        for s in range(2)
        for i, (ref, buf) in enumerate(((diag_hbm, diag_v), (rhs_hbm, rhs_v), (off_hbm, off_v)))
    ] + [
        local(td_hbm, td_v, load_sem.at[3, 0]),
        local(fac_hbm, fac_v, load_sem.at[4, 0]),
        local(trhs_hbm, trhs_v, load_sem.at[5, 0]),
    ]
    for copy in loads:
        copy.start()

    barrier = pltpu.get_barrier_semaphore()

    def greet(l2, x2, y2, z2):
        pl.semaphore_signal(barrier, inc=1, device_id=(l2, x2, z2 * NY + y2), device_id_type=MESH)

    greet(sibling, x, y, z)
    for d in range(1, NX):
        greet(leaf, (x + d) % NX, y, z)
    for d in range(1, NY):
        greet(leaf, x, (y + d) % NY, z)
    for d in (1, NZ - 1):
        greet(leaf, x, y, (z + d) % NZ)

    lane = lax.broadcasted_iota(jnp.int32, (1, 256), 1)
    for s in range(2):
        row = jnp.where(lane < live_ref[s], targ_ref[s : s + 1, :], -1).astype(F32)
        tg[0, s, :, :] = jnp.broadcast_to(row, (8, 256))

    for s in range(2):
        loads[3 * s].wait()
        loads[3 * s + 1].wait()
        low, _ = tril(diag_v[s], 0, 0)
        sol = rhs_v[s] + dot3(low, rhs_v[s])
        csol_v[s] = sol
        loads[3 * s + 2].wait()
        tile_v[s] = dot3(off_v[s], sol)

    pl.semaphore_wait(barrier, 1 + NX - 1 + NY - 1 + 2)

    def spread(step):
        for d in (step, NZ - step):
            pl.semaphore_signal(
                near.at[step - 1], inc=1, device_id=(leaf, x, (z + d) % NZ * NY + y), device_id_type=MESH
            )

    spread(1)
    tg_copy = remote(tg.at[0], tg.at[1], tgs, tgr, sibling, x, y, z)
    tg_copy.start()
    drain.append(tg_copy.wait_send)
    core_copies = []
    for s in range(2):
        copy = remote(
            tile_v.at[s, :, pl.ds(pl.multiple_of(sibling * 128, 128), 128)], trecv.at[s],
            cs.at[s], cr.at[s], sibling, x, y, z,
        )
        copy.start()
        core_copies.append(copy)
        drain.append(copy.wait_send)

    half = pl.ds(pl.multiple_of(leaf * 128, 128), 128)
    for s in range(2):
        tcol[256 * s : 256 * s + 256, :] = jnp.broadcast_to(tg[0, s, 0:1, :], (128, 256)).T
        high, rest = split(tile_v[s, :, half].T)
        tt[0:128, 256 * s : 256 * s + 256] = high
        tt[128:256, 256 * s : 256 * s + 256] = rest
    tg_copy.wait_recv()
    for s in range(2):
        tcol[512 + 256 * s : 768 + 256 * s, :] = jnp.broadcast_to(tg[1, s, 0:1, :], (128, 256)).T
        core_copies[s].wait_recv()
        high, rest = split(trecv[s].T)
        tt[0:128, 512 + 256 * s : 768 + 256 * s] = high
        tt[128:256, 512 + 256 * s : 768 + 256 * s] = rest
    lane = lax.broadcasted_iota(jnp.int32, (1024, 128), 1)

    def contrib(start):
        rel = tcol[...] - start.astype(F32)
        lanes = lane.astype(F32)
        hot = jnp.concatenate(
            [jnp.where(rel == lanes, 1.0, 0.0), jnp.where(rel == lanes + 128.0, 1.0, 0.0)], axis=1
        ).astype(BF16)
        both = dot(tt[...], hot)
        return both[0:128] + both[128:256]

    def ax_copy(d):
        return remote(cbuf.at[d], axrecv.at[d - 1], axs.at[d], axr, leaf, (x + d) % NX, y, z)

    def by_copy(d, b):
        y2 = (y + d) % NY
        return remote(ybuf.at[y2, b], byrecv.at[d - 1, b], bys.at[d, b], byr, leaf, x, y2, z)

    def lower(d):
        cbuf[d] = contrib((x + d) % NX * 512)

    def upper(b, _):
        value = contrib(b * 512 + 256)
        for part in range(NY):
            ybuf[part, b] = value[
                part % 2 * 64 : part % 2 * 64 + 64, part // 2 * 128 : part // 2 * 128 + 128
            ]
        for d in (2, 1, 3):
            by_copy(d, b).start()
        return 0

    def lower_upper(i, _):
        d = (i * 2 + 1) % NX + i // 2
        lower(d)
        ax_copy(d).start()
        upper(i, 0)
        return 0

    lax.fori_loop(0, 3, lower_upper, 0)
    upper(jnp.int32(3), 0)
    pl.semaphore_wait(near.at[0], 2)
    spread(2)
    drain += [ax_copy(d).wait_send for d in range(1, NX)]
    drain += [by_copy(d, b).wait_send for d in range(1, NY) for b in range(NX)]

    giver = (leaf == z % 2) & (z // 2 < x)
    for load in loads[6:]:
        load.wait()

    def ga_copy(d):
        y2 = (y + d) % NY
        return remote(gsrc.at[y2], grecv.at[z // 2, y], gas.at[d], gar, leaf, x, y2, z)

    @pl.when(giver)
    def _():
        low, _ = tril(td_v[...], 0, 0)
        fac = fac_v[...]
        gt = fac + dot3t(fac, low)
        for y2 in range(NY):
            gsrc[y2] = gt[:, 128 * y2 : 128 * y2 + 128]
        for d in range(1, NY):
            ga_copy(d).start()
        local(gsrc.at[y], grecv.at[z // 2, y], gar).start()

    def gb_copy(d):
        return remote(
            grecv.at[z // 2], grecv.at[z // 2], gs.at[d], gr.at[z // 2], leaf, x, y, (z + d) % NZ
        )

    def g_forward():
        @pl.when(giver)
        def _():
            arrived(grecv.at[z // 2], gar)
            for d in range(1, NZ):
                gb_copy(d).start()

    def g_drain():
        @pl.when(giver)
        def _():
            for d in range(1, NY):
                ga_copy(d).wait_send()
            for d in range(1, NZ):
                gb_copy(d).wait_send()

    drain.append(g_drain)

    row0, col0 = pl.multiple_of(y * 128, 128), pl.multiple_of(leaf * 256, 256)
    low, eye = tril(td_v[pl.ds(row0, 128), pl.ds(col0, 256)], row0, col0)
    tinv[0], tinv[1] = split((low + jnp.where(eye, 1.0, 0.0)).T)
    rhst[...] = trhs_v[pl.ds(col0, 256), :].T

    lower(0)
    pl.semaphore_wait(near.at[1], 2)

    arrived(byrecv, byr)

    def bx_copy(d):
        block = (x + d) % NX
        return remote(ysum.at[block], bxrecv.at[d - 1], bxs.at[d], bxr, leaf, block, y, z)

    def add_y(d):
        b = (x + d) % NX
        ysum[b] = ybuf[y, b] + byrecv[0, b] + byrecv[1, b] + byrecv[2, b]

    for d in (2, 1, 3):
        add_y(d)
        bx_copy(d).start()
        drain.append(bx_copy(d).wait_send)
    add_y(0)

    def az_copy(e):
        z2 = (z + e) % NZ
        return remote(azsrc.at[z2], azrecv.at[e - 1], azs.at[e], azr, leaf, x, y, z2)

    arrived(axrecv, axr)
    azsrc[...] = (cbuf[0] + axrecv[0] + axrecv[1] + axrecv[2]).reshape(NZ, 16, 256)
    for e in (4, 3, 5, 2, 6, 1, 7):
        az_copy(e).start()
        drain.append(az_copy(e).wait_send)

    keeper = z // 4 == y % 2

    def bz_copy(turn):
        i = (z + turn) % 4
        z2 = y % 2 * 4 + i
        return z2 != z, remote(bzsrc.at[i], bzrecv.at[z], bzs.at[i], bzr, leaf, x, y, z2)

    arrived(bxrecv, bxr)
    bzsrc[...] = (ysum[x] + bxrecv[0] + bxrecv[1] + bxrecv[2]).reshape(4, 16, 128)
    for i in (0, 1, 3, 2):
        away, copy = bz_copy(i)
        pl.when(away)(copy.start)

    def bz_drain():
        for i in range(4):
            away, copy = bz_copy(i)
            pl.when(away)(copy.wait_send)

    drain.append(bz_drain)
    pl.when(keeper)(local(bzsrc.at[z % 4], bzrecv.at[z], bzr).start)
    g_forward()

    def ay_copy(dy):
        return remote(aysrc, ayrecv.at[leaf, dy], ays.at[dy], ayr, 0, x, (y + dy) % NY, z)

    arrived(azrecv, azr)
    total = azsrc[z]
    for e in range(NZ - 1):
        total = total + azrecv[e]
    aysrc[...] = total
    for dy in (2, 1, 3):
        ay_copy(dy).start()
        drain.append(ay_copy(dy).wait_send)
    pl.when(leaf == 0)(local(aysrc, ayrecv.at[leaf, 0], ayr).start)
    pl.when(leaf == 1)(ay_copy(0).start)
    drain.append(lambda: pl.when(leaf == 1)(ay_copy(0).wait_send))

    def cy_copy(dy):
        return remote(cysrc, cyrecv.at[leaf, y // 2], cys.at[dy], cyr, 1, x, (y + dy) % NY, z)

    @pl.when(keeper)
    def _():
        arrived(bzrecv, bzr)
        total = bzrecv[0]
        for e in range(1, NZ):
            total = total + bzrecv[e]
        cysrc[...] = total
        for dy in (2, 1, 3):
            cy_copy(dy).start()
        pl.when(leaf == 1)(local(cysrc, cyrecv.at[leaf, y // 2], cyr).start)
        pl.when(leaf == 0)(cy_copy(0).start)

    def cy_drain():
        @pl.when(keeper)
        def _():
            for dy in range(1, NY):
                cy_copy(dy).wait_send()
            pl.when(leaf == 0)(cy_copy(0).wait_send)

    drain.append(cy_drain)

    @pl.when(leaf == 0)
    def _():
        arrived(ayrecv, ayr)
        for h in range(2):
            upd[h] = ayrecv[h, 0] + ayrecv[h, 1] + ayrecv[h, 2] + ayrecv[h, 3]

    @pl.when(leaf == 1)
    def _():
        arrived(cyrecv, cyr)
        for h in range(2):
            upd[h] = jnp.concatenate([cyrecv[h, 0], cyrecv[h, 1]], axis=1)

    reds = []
    for h in range(2):
        reds.append(rhst[pl.ds(pl.multiple_of(h * 128 + z * 16, 16), 16), :] - upd[h])
    acc = dot3p(jnp.concatenate(reds, axis=0), tinv[0], tinv[1])
    fsrc[...] = acc.reshape(2, 16, 128)

    def x_copy(k, x2, dy):
        return remote(
            fsrc, xrecv.at[k, leaf, y % 2], xs.at[x2, dy], xr.at[k], y // 2, x2, (y + dy) % NY, z
        )

    for k in range(NX - 2):

        @pl.when(x == k)
        def _(k=k):
            for x2 in range(k + 1, NX):
                for dy in (2, 1, 3, 0):
                    x_copy(k, x2, dy).start()

        @pl.when(x > k)
        def _(k=k):
            @pl.when(z != 2 * k + leaf)
            def _():
                arrived(grecv.at[k], gr.at[k])

            high, rest = split(grecv[k].reshape(256, 128))
            gparts[k, 0] = high
            gparts[k, 1] = rest
            arrived(xrecv.at[k], xr.at[k])
            parts = (xrecv[k, 0] + xrecv[k, 1]).reshape(2, 32, 128)
            solved = jnp.concatenate([parts[0], parts[1]], axis=1)
            step = dot3p(solved, gparts[k, 0], gparts[k, 1])
            fsrc[...] = fsrc[...] - step.reshape(2, 16, 128)

        def x_drain(k=k):
            @pl.when(x == k)
            def _():
                for x2 in range(k + 1, NX):
                    for y2 in range(NY):
                        x_copy(k, x2, y2).wait_send()

        drain.append(x_drain)

    def last_copy(h, dy):
        return remote(
            fsrc.at[h], lastrecv.at[leaf, y], lasts.at[h, dy], lastr, h, NX - 1, (y + dy) % NY, z
        )

    other_g = remote(grecv.at[NX - 2], gsib, ess, esr, sibling, x, y, z)
    pair = remote(fsrc.at[sibling], frecv, fps, fpr, sibling, x, y, z)

    @pl.when(x == NX - 2)
    def _():
        for dy in (2, 1, 3, 0):
            for h in range(2):
                last_copy(h, dy).start()

    pair.start()
    drain.append(pair.wait_send)

    @pl.when(x == NX - 1)
    def _():
        @pl.when(z != 2 * (NX - 2) + leaf)
        def _():
            arrived(grecv.at[NX - 2], gr.at[NX - 2])

        other_g.start()

    pair.wait_recv()
    fown[...] = fsrc[leaf] + frecv[...]

    @pl.when(x == NX - 1)
    def _():
        own = split(grecv[NX - 2].reshape(256, 128))
        other_g.wait_recv()
        other = split(gsib[...].reshape(256, 128))
        arrived(lastrecv, lastr)

        def solved(core):
            first = lastrecv[0, 2 * core] + lastrecv[1, 2 * core]
            second = lastrecv[0, 2 * core + 1] + lastrecv[1, 2 * core + 1]
            return jnp.concatenate([first, second], axis=1)

        fown[...] = fown[...] - (dot3p(solved(leaf), *own) + dot3p(solved(sibling), *other))

    def last_drain():
        @pl.when(x == NX - 2)
        def _():
            for y2 in range(NY):
                for h in range(2):
                    last_copy(h, y2).wait_send()

        pl.when(x == NX - 1)(other_g.wait_send)

    drain.append(last_drain)

    late = []

    def f1_copy(d):
        return remote(fown, fall.at[y, z], f1s.at[d], f1r.at[d], leaf, x, y, (z + d) % NZ)

    def f2_copy(d, dy):
        part = fall.at[y, (z + NZ - d) % NZ]
        return remote(part, part, f2s.at[d, dy], f2r.at[y], leaf, x, (y + dy) % NY, z)

    for d in (4, 3, 5, 2, 6, 1, 7):
        f1_copy(d).start()
        late.append(f1_copy(d).wait_send)
    fall[y, z] = fown[...]
    for d in (0, 1, 7, 2, 6, 3, 5, 4):
        if d:
            arrived(fall.at[y, (z + NZ - d) % NZ], f1r.at[d])
        for dy in (2, 1, 3):
            f2_copy(d, dy).start()
            late.append(f2_copy(d, dy).wait_send)
        if d == 0:
            finish()

    def f3_copy(y2):
        part = outv.at[pl.ds(pl.multiple_of(y2 * 128, 128), 128), half]
        return remote(part, part, f3s.at[y2], f3r, sibling, x, y, z)

    for d in (0, 1, 3, 2):
        y2 = (y + d) % NY
        if d:
            arrived(fall.at[y2], f2r.at[y2])
        outv[pl.ds(pl.multiple_of(y2 * 128, 128), 128), half] = fall[y2].reshape(128, 128).T
        f3_copy(y2).start()
    for wait in late:
        wait()
    arrived(outv.at[:, pl.ds(pl.multiple_of(sibling * 128, 128), 128)], f3r)
    for y2 in range(NY):
        f3_copy(y2).wait_send()


def write_out(csol_v, top_v, csol_hbm, top_hbm, sem):
    copies = [pltpu.make_async_copy(csol_v.at[s], csol_hbm.at[s], sem.at[s]) for s in range(2)]
    copies += [
        pltpu.make_async_copy(
            top_v.at[256 * s : 256 * s + 256], top_hbm.at[256 * s : 256 * s + 256], sem.at[2 + s]
        )
        for s in range(2)
    ]
    for copy in copies:
        copy.start()
    for copy in copies:
        copy.wait()


def shards(child_rhs, child_diag, child_off, live, targets, top_rhs, top_factor, top_diag):
    any_ = pl.BlockSpec(memory_space=pl.ANY)
    vm = pltpu.VMEM
    dma = pltpu.SemaphoreType.DMA
    solved = pl.pallas_call(
        kernel,
        out_shape=(
            pltpu.VMEM(child_rhs.shape, F32),
            pltpu.VMEM(top_rhs.shape, F32),
        ),
        in_specs=[
            pl.BlockSpec(memory_space=pltpu.SMEM),
            pl.BlockSpec(memory_space=pltpu.VMEM),
        ] + [any_] * 6,
        out_specs=(pl.BlockSpec(memory_space=pltpu.VMEM),) * 2,
        scratch_shapes=[
            vm((2, 256, 256), F32), vm((2, 256, 256), F32), vm((2, 256, 256), F32),
            vm((2, 256, 256), F32),
            vm((512, 256), F32), vm((64, 512), F32), vm((512, 512), F32),
            vm((2, 2, 8, 256), F32), vm((2, 256, 128), F32), vm((1024, 128), F32), vm((256, 1024), BF16),
            vm((4, 128, 256), F32), vm((3, 128, 256), F32),
            vm((4, 4, 64, 128), F32), vm((3, 4, 64, 128), F32), vm((4, 64, 128), F32), vm((3, 64, 128), F32),
            vm((8, 16, 256), F32), vm((7, 16, 256), F32), vm((4, 16, 128), F32), vm((8, 16, 128), F32),
            vm((16, 256), F32), vm((2, 4, 16, 256), F32), vm((16, 128), F32), vm((2, 2, 16, 128), F32),
            vm((2, 16, 256), F32),
            vm((256, 256), F32), vm((2, 256, 128), BF16),
            vm((4, 64, 128), F32), vm((3, 4, 64, 128), F32), vm((3, 2, 256, 128), BF16),
            vm((4, 64, 128), F32), vm((2, 4, 16, 128), F32),
            vm((2, 16, 128), F32), vm((3, 2, 2, 2, 16, 128), F32),
            vm((16, 128), F32), vm((16, 128), F32), vm((4, 8, 16, 128), F32),
            pltpu.SemaphoreType.REGULAR((2,)),
            dma((6, 2)), dma, dma, dma((2,)), dma((2,)), dma((4,)), dma, dma((8,)), dma((4,)),
            dma((4,)), dma, dma((4, 4)), dma, dma((4,)), dma, dma((8,)), dma,
            dma((4,)), dma, dma((4,)), dma, dma((4,)), dma,
            dma((2, 4)), dma, dma, dma,
            dma((4, 4)), dma((3,)), dma, dma, dma((8,)), dma((8,)), dma((8, 4)), dma((4,)), dma((4,)), dma,
        ],
        compiler_params=pltpu.CompilerParams(collective_id=0, has_side_effects=True),
    )(live, targets, child_rhs, child_diag, child_off, top_rhs, top_factor.T, top_diag)
    return pl.pallas_call(
        write_out,
        out_shape=tuple(jax.ShapeDtypeStruct(a.shape, F32) for a in (child_rhs, top_rhs)),
        in_specs=[pl.BlockSpec(memory_space=pltpu.VMEM)] * 2,
        out_specs=(any_, any_),
        scratch_shapes=[dma((4,))],
    )(*(pltpu.with_memory_space_constraint(a, pltpu.VMEM) for a in solved))


def solution(mesh):
    parts = ("leaf", "row", "col")
    in_specs = (
        P(parts, None, None),
        P(parts, None, None),
        P(parts, None, None),
        P(parts),
        P(parts, None),
        P("row", None),
        P("row", "col"),
        P("row", None),
    )
    out_specs = (P(parts, None, None), P("row", None))
    return jax.shard_map(shards, mesh=mesh, in_specs=in_specs, out_specs=out_specs, check_vma=False)
```
